32 devices in a mesh: dp: 8 (over z, x), tensor: 4 (over y, core).
Axes of the slice: x: 2, y: 2, z: 4, core: 2. Of those that a mesh axis runs over, the one named last changes fastest.
Arguments:
- patches: float32 [4, 16, 256, 768], P(None, 'dp', 'tensor'), may hold values from -6 to 6
- mask_queries: float32 [4, 16, 256, 768], P(None, 'dp', 'tensor'), may hold values from -6 to 6
- visible: int32 [4, 16, 256], P(None, 'dp'), may hold values 0 or 1
- lengths: int32 [4, 16], P(None, 'dp'), may hold values from 32 to 256, as said below
- d_latent: float32 [4, 16, 256, 768], P(None, 'dp', 'tensor'), may hold values from -6 to 6
- d_regress: float32 [4, 16, 256, 768], P(None, 'dp', 'tensor'), may hold values from -6 to 6
- encoder_gain: float32 [2, 768], replicated, may hold values from 0.5 to 1.5
- encoder_shift: float32 [2, 768], replicated, may hold values from -1 to 1
- encoder_scale: float32 [2, 768], replicated, may hold values from 0.5 to 1.5
- encoder_inproj: bfloat16 [3, 768, 768], P(None, None, 'tensor'), may hold values from -0.21875 to 0.21875
- encoder_inbias: float32 [2, 768], P(None, 'tensor'), may hold values from -1 to 1
- encoder_outproj: bfloat16 [768, 768], P('tensor'), may hold values from -0.875 to 0.875
- encoder_outbias: float32 [2, 768], replicated, may hold values from -1 to 1
- encoder_expand: bfloat16 [768, 3072], P(None, 'tensor'), may hold values from -0.21875 to 0.21875
- encoder_expbias: float32 [3072], P('tensor'), may hold values from -1 to 1
- encoder_shrink: bfloat16 [3072, 768], P('tensor'), may hold values from -0.21875 to 0.21875
- regress_gain: float32 [3, 768], replicated, may hold values from 0.5 to 1.5
- regress_shift: float32 [3, 768], replicated, may hold values from -1 to 1
- regress_scale: float32 [2, 768], replicated, may hold values from 0.5 to 1.5
- regress_inproj: bfloat16 [3, 768, 768], P(None, None, 'tensor'), may hold values from -0.21875 to 0.21875
- regress_inbias: float32 [2, 768], P(None, 'tensor'), may hold values from -1 to 1
- regress_outproj: bfloat16 [768, 768], P('tensor'), may hold values from -0.875 to 0.875
- regress_outbias: float32 [2, 768], replicated, may hold values from -1 to 1
- regress_expand: bfloat16 [768, 3072], P(None, 'tensor'), may hold values from -0.21875 to 0.21875
- regress_expbias: float32 [3072], P('tensor'), may hold values from -1 to 1
- regressor_down_weight: bfloat16 [3072, 768], P('tensor'), may hold values from -0.21875 to 0.21875
Outputs:
- latent: float32 [4, 16, 256, 768], P(None, 'dp', 'tensor')
- regressed: float32 [4, 16, 256, 768], P(None, 'dp', 'tensor')
- grad_patches: float32 [4, 16, 256, 768], P(None, 'dp', 'tensor')
- grad_queries: float32 [4, 16, 256, 768], P(None, 'dp', 'tensor')
- encoder_gain_grad: float32 [2, 768], replicated
- encoder_shift_grad: float32 [2, 768], replicated
- encoder_scale_grad: float32 [2, 768], replicated
- encoder_inproj_grad: float32 [3, 768, 768], P(None, None, 'tensor')
- encoder_inbias_grad: float32 [2, 768], P(None, 'tensor')
- encoder_outproj_grad: float32 [768, 768], P('tensor')
- encoder_outbias_grad: float32 [2, 768], replicated
- encoder_expand_grad: float32 [768, 3072], P(None, 'tensor')
- encoder_expbias_grad: float32 [3072], P('tensor')
- encoder_shrink_grad: float32 [3072, 768], P('tensor')
- regress_gain_grad: float32 [3, 768], replicated
- regress_shift_grad: float32 [3, 768], replicated
- regress_scale_grad: float32 [2, 768], replicated
- regress_inproj_grad: float32 [3, 768, 768], P(None, None, 'tensor')
- regress_inbias_grad: float32 [2, 768], P(None, 'tensor')
- regress_outproj_grad: float32 [768, 768], P('tensor')
- regress_outbias_grad: float32 [2, 768], replicated
- regress_expand_grad: float32 [768, 3072], P(None, 'tensor')
- regress_expbias_grad: float32 [3072], P('tensor')
- regress_shrink_grad: float32 [3072, 768], P('tensor')
The draws below stay inside these ranges and needn't reach their ends.
Inputs may be any that keep to these rules, and one draw needn't show every extreme that they name: `lengths`: patches at positions below an image's length are valid, the rest padding. Each index of dp holds, over all micro-batches together, at least one image, drawn from the seed, with all 256 patches valid.
All inputs are finite; a program needn't handle non-finite values. No bound on the sum of `visible` on one device may be relied on, other than what follows from the above.
Results may differ from the reference program's by a relative error of at most 0.023.
Values may be sent and summed in bfloat16 or wider, within the bound.
No kernel may reach another device: no remote copies, remote signals or barrier semaphores. Data moves between devices by JAX's collectives and lax.ppermute only.
A program may use at most 256 MiB of HBM per device.

```python
import jax
import jax.numpy as jnp
from jax import lax

D = 768
HDIM = 64
FF = 3072
PATCH = 256
MICRO = 4
IMG_MB = 2
IMAGES_MB = 16


def draw_lengths(key, part):
    key_one = jax.random.fold_in(key, 11)
    key_two = jax.random.fold_in(key, 12)
    key_pick = jax.random.fold_in(key, 13)
    shape_now = (MICRO, IMAGES_MB)
    spread_one = jax.random.randint(key_one, shape_now, 0, PATCH)
    spread_two = jax.random.randint(key_two, shape_now, 0, PATCH)
    tailed = jnp.maximum(PATCH // 8, spread_one * spread_two // PATCH + 1)
    group_count = IMAGES_MB // IMG_MB
    chosen = jax.random.randint(key_pick, (group_count,), 0, MICRO * IMG_MB)
    column = jnp.arange(IMAGES_MB, dtype=jnp.int32)
    group_of = column // IMG_MB
    within = column % IMG_MB
    micro_index = jnp.arange(MICRO, dtype=jnp.int32)
    slot = micro_index[:, None] * IMG_MB + within[None, :]
    chosen_each = chosen[group_of]
    return jnp.where(slot == chosen_each[None, :], PATCH, tailed).astype(jnp.int32)


def plant(values, stream_key, smallest, largest):
    longest = values.shape.index(max(values.shape))
    spots = []
    for shift in (0, 1):
        where = [jax.random.randint(jax.random.fold_in(stream_key, axis), (), 0, length) for axis, length in enumerate(values.shape)]
        where[longest] = (where[longest] + shift) % values.shape[longest]
        spots.append(tuple(where))
    return values.at[spots[0]].set(smallest).at[spots[1]].set(largest)


def steps_of(key, shape, shards, low, high):
    loudness = 1.0
    for axis_at, parts in shards:
        steps = jax.random.uniform(jax.random.fold_in(jax.random.fold_in(key, 6), axis_at), (parts,), jnp.float32, low / len(shards), high / len(shards))
        loudness = loudness * jnp.repeat(jnp.exp(steps), shape[axis_at] // parts).reshape((-1,) + (1,) * (len(shape) - 1 - axis_at))
    return loudness


def scatter_about(rng, extent, width, most, split=(), kind=jnp.bfloat16):
    array = width * jax.random.normal(rng, extent, jnp.float32)
    if split:
        array = array * steps_of(rng, extent, split, -0.22, 0.18)
    return jnp.clip(array, -most, most).astype(kind)


def setup_inputs(seed: int = 0) -> dict:
    key_list = jax.random.split(jax.random.key(seed), 27)
    return {
        "patches": scatter_about(key_list[0], (MICRO, IMAGES_MB, PATCH, D), 1.0, 6.0, ((1, 8), (2, 4)), jnp.float32),
        "mask_queries": scatter_about(key_list[1], (MICRO, IMAGES_MB, PATCH, D), 1.0, 6.0, ((1, 8), (2, 4)), jnp.float32),
        "visible": plant((jax.random.randint(key_list[2], (MICRO, IMAGES_MB, PATCH), 0, 2) < 1).astype(jnp.int32), jax.random.fold_in(key_list[2], 1), 0, 1),
        "lengths": draw_lengths(jax.random.fold_in(key_list[26], 71), 0),
        "d_latent": scatter_about(key_list[4], (MICRO, IMAGES_MB, PATCH, D), 1.0, 6.0, ((1, 8), (2, 4)), jnp.float32),
        "d_regress": scatter_about(key_list[5], (MICRO, IMAGES_MB, PATCH, D), 1.0, 6.0, ((1, 8), (2, 4)), jnp.float32),
        "encoder_gain": jnp.clip(1.0 + 0.1 * jax.random.normal(key_list[6], (2, D), jnp.float32), 0.5, 1.5),
        "encoder_shift": scatter_about(key_list[7], (2, D), 0.2, 1.0, (), jnp.float32),
        "encoder_scale": jnp.clip(jax.random.uniform(key_list[8], (2, D), jnp.float32, 0.5, 1.5), 0.5, 1.5),
        "encoder_inproj": scatter_about(key_list[9], (3, D, D), D ** -0.5, 0.21875, ((2, 4),)),
        "encoder_inbias": scatter_about(key_list[10], (2, D), 0.2, 1.0, ((1, 4),), jnp.float32),
        "encoder_outproj": scatter_about(key_list[11], (D, D), (D // 16) ** -0.5, 0.875, ((0, 4),)),
        "encoder_outbias": scatter_about(key_list[12], (2, D), 0.2, 1.0, (), jnp.float32),
        "encoder_expand": scatter_about(key_list[13], (D, FF), D ** -0.5, 0.21875, ((1, 4),)),
        "encoder_expbias": scatter_about(key_list[14], (FF,), 0.2, 1.0, ((0, 4),), jnp.float32),
        "encoder_shrink": scatter_about(key_list[15], (FF, D), (FF // 4) ** -0.5, 0.21875, ((0, 4),)),
        "regress_gain": jnp.clip(1.0 + 0.1 * jax.random.normal(key_list[16], (3, D), jnp.float32), 0.5, 1.5),
        "regress_shift": scatter_about(key_list[17], (3, D), 0.2, 1.0, (), jnp.float32),
        "regress_scale": jnp.clip(jax.random.uniform(key_list[18], (2, D), jnp.float32, 0.5, 1.5), 0.5, 1.5),
        "regress_inproj": scatter_about(key_list[19], (3, D, D), D ** -0.5, 0.21875, ((2, 4),)),
        "regress_inbias": scatter_about(key_list[20], (2, D), 0.2, 1.0, ((1, 4),), jnp.float32),
        "regress_outproj": scatter_about(key_list[21], (D, D), (D // 16) ** -0.5, 0.875, ((0, 4),)),
        "regress_outbias": scatter_about(key_list[22], (2, D), 0.2, 1.0, (), jnp.float32),
        "regress_expand": scatter_about(key_list[23], (D, FF), D ** -0.5, 0.21875, ((1, 4),)),
        "regress_expbias": scatter_about(key_list[24], (FF,), 0.2, 1.0, ((0, 4),), jnp.float32),
        "regressor_down_weight": scatter_about(key_list[25], (FF, D), (FF // 4) ** -0.5, 0.21875, ((0, 4),)),
    }


@jax.custom_vjp
def low(v):
    return lax.optimization_barrier(v.astype(jnp.bfloat16)).astype(jnp.float32)

@jax.custom_vjp
def low_back(v):
    return v

def low_keep(v):
    return (low(v), None)

def low_pass(kept, grad):
    return (grad,)

def back_keep(v):
    return (v, None)

def back_low(kept, grad):
    return (low(grad),)
low.defvjp(low_keep, low_pass)
low_back.defvjp(back_keep, back_low)
highest = lax.Precision.HIGHEST
epsilon = 1e-06

def rounded_both(values):
    return low(low_back(values))

def layer_norm(values, gain_row, shift_row):
    average = lax.optimization_barrier(jnp.mean(values, axis=-1, keepdims=True))
    centred = values - average
    variance = lax.optimization_barrier(jnp.mean(centred * centred, axis=-1, keepdims=True))
    return centred * lax.rsqrt(variance + epsilon) * gain_row + shift_row

def project(values, weight):
    return jnp.einsum('ipd,dc->ipc', values, weight, precision=highest)

def attend(queries, keys, values, key_mask):
    images, patches, col_width = queries.shape
    head_count = col_width // HDIM
    query_heads = queries.reshape(images, patches, head_count, HDIM)
    key_heads = keys.reshape(images, patches, head_count, HDIM)
    value_heads = values.reshape(images, patches, head_count, HDIM)
    scores = low_back(jnp.einsum('iqhe,ikhe->ihqk', query_heads, key_heads, precision=highest) * HDIM ** (-0.5))
    scores = jnp.where(key_mask[:, None, None, :], scores, -1e+30)
    row_top = lax.optimization_barrier(jnp.max(scores, axis=-1, keepdims=True))
    expo = jnp.exp(scores - row_top)
    soft_weights = expo / lax.optimization_barrier(jnp.sum(expo, axis=-1, keepdims=True))
    mixed = jnp.einsum('ihqk,ikhe->iqhe', low(soft_weights), value_heads, precision=highest)
    return mixed.reshape(images, patches, col_width)

def attention_branch(query_in, context_in, inproj, inbias, outproj, outbias_row, key_mask):
    queries = rounded_both(project(query_in, inproj[0]) + inbias[0])
    keys = rounded_both(project(context_in, inproj[1]))
    values = rounded_both(project(context_in, inproj[2]) + inbias[1])
    mixed = rounded_both(attend(queries, keys, values, key_mask))
    return low_back(project(mixed, outproj) + outbias_row)

def feed_forward(stream, gain_row, shift_row, scale_row, outbias_row, expand, expbias, shrink):
    normed = low(layer_norm(stream, gain_row, shift_row))
    hidden = low_back(project(normed, expand) + expbias)
    active = low(jax.nn.gelu(hidden, approximate=False))
    branch = low_back(project(active, shrink) + outbias_row)
    return stream + scale_row * branch

def encoder(patches, key_mask, gain, shift, scale_rows, inproj, inbias, outproj, outbias, expand, expbias, shrink):
    normed = low(layer_norm(patches, gain[0], shift[0]))
    middle = patches + scale_rows[0] * attention_branch(normed, normed, inproj, inbias, outproj, outbias[0], key_mask)
    return feed_forward(middle, gain[1], shift[1], scale_rows[1], outbias[1], expand, expbias, shrink)

def regressor(latent, queries, seen_mask, key_mask, gain, shift, scale_rows, inproj, inbias, outproj, outbias, expand, expbias, shrink):
    query_in = low(layer_norm(queries, gain[0], shift[0]))
    context = jnp.where(seen_mask[:, :, None], latent, queries)
    context_in = low(layer_norm(context, gain[1], shift[1]))
    middle = queries + scale_rows[0] * attention_branch(query_in, context_in, inproj, inbias, outproj, outbias[0], key_mask)
    return feed_forward(middle, gain[2], shift[2], scale_rows[1], outbias[1], expand, expbias, shrink)

def reference(patches, mask_queries, visible, lengths, d_latent, d_regress, encoder_gain, encoder_shift, encoder_scale, encoder_inproj, encoder_inbias, encoder_outproj, encoder_outbias, encoder_expand, encoder_expbias, encoder_shrink, regress_gain, regress_shift, regress_scale, regress_inproj, regress_inbias, regress_outproj, regress_outbias, regress_expand, regress_expbias, regressor_down_weight):
    params = tuple((item.astype(jnp.float32) for item in (encoder_gain, encoder_shift, encoder_scale, encoder_inproj, encoder_inbias, encoder_outproj, encoder_outbias, encoder_expand, encoder_expbias, encoder_shrink, regress_gain, regress_shift, regress_scale, regress_inproj, regress_inbias, regress_outproj, regress_outbias, regress_expand, regress_expbias, regressor_down_weight)))
    position = jnp.arange(PATCH, dtype=jnp.int32)

    def single_microbatch(carry, item):
        rows_in, query_rows, visible_now, lengths_now, latent_cot, regress_cot = item
        valid_mask = position[None, :] < lengths_now[:, None]
        seen_mask = (visible_now == 1) | (position[None, :] == 0)

        def forward(rows_arg, query_arg, weights):
            latent = encoder(rows_arg, valid_mask & seen_mask, *weights[:10])
            regressed = regressor(latent, query_arg, seen_mask, valid_mask, *weights[10:])
            return (latent, regressed)
        results, backward = jax.vjp(forward, rows_in, query_rows, params)
        grad_rows, grad_query, grad_weights = backward((latent_cot, regress_cot))
        carry = jax.tree.map(lambda earlier, further: earlier + further, carry, grad_weights)
        return (carry, (results[0], results[1], grad_rows, grad_query))
    zeros = jax.tree.map(jnp.zeros_like, params)
    totals, stacked = lax.scan(single_microbatch, zeros, (patches, mask_queries, visible, lengths, d_latent, d_regress))
    return (stacked[0], stacked[1], stacked[2], stacked[3], totals[0], totals[1], totals[2], totals[3], totals[4], totals[5], totals[6], totals[7], totals[8], totals[9], totals[10], totals[11], totals[12], totals[13], totals[14], totals[15], totals[16], totals[17], totals[18], totals[19])
```

```python
import jax
import jax.numpy as jnp
from jax import lax
from jax.sharding import PartitionSpec as P

HDIM = 64
epsilon = 1e-06
bfloat = jnp.bfloat16
single = jnp.float32


def dot(a, b, ca, cb):
    return lax.dot_general(a, b, (((ca,), (cb,)), ((), ())), preferred_element_type=single)


def norm_parts(values):
    average = jnp.mean(values, axis=-1, keepdims=True)
    centred = values - average
    variance = jnp.mean(centred * centred, axis=-1, keepdims=True)
    factor = lax.rsqrt(variance + epsilon)
    return centred * factor, factor


def norm_grads(gradient, unit, factor, gain_row):
    scaled = gradient * gain_row
    flowing = factor * (
        scaled
        - jnp.mean(scaled, axis=-1, keepdims=True)
        - unit * jnp.mean(scaled * unit, axis=-1, keepdims=True)
    )
    return flowing, jnp.sum(gradient * unit, axis=0), jnp.sum(gradient, axis=0)


def rows_sum(values):
    return jnp.sum(values.astype(single), axis=0)


def gelu_parts(hidden):
    half = 0.5 * (1.0 + lax.erf(hidden * (0.5**0.5)))
    slope = half + hidden * jnp.exp(-0.5 * hidden * hidden) * ((0.5 / jnp.pi) ** 0.5)
    return hidden * half, slope


def split_heads(values, images):
    rows, width = values.shape
    return values.reshape(images, rows // images, width // HDIM, HDIM)


def attend(q, k, v, key_mask):
    images = key_mask.shape[0]
    qh, kh, vh = (split_heads(x, images) for x in (q, k, v))
    scores = jnp.einsum("iqhe,ikhe->ihqk", qh, kh, preferred_element_type=single) * HDIM**-0.5
    scores = jnp.where(key_mask[:, None, None, :], scores, -1e30)
    top = jnp.max(scores, axis=-1, keepdims=True)
    expo = jnp.exp(scores - top)
    total = jnp.sum(expo, axis=-1, keepdims=True)
    probs = expo / total
    mixed = jnp.einsum("ihqk,ikhe->iqhe", probs.astype(bfloat), vh, preferred_element_type=single)
    return mixed.reshape(q.shape).astype(bfloat), top + jnp.log(total)


def attend_grads(q, k, v, lse, gmixed, key_mask):
    images = key_mask.shape[0]
    qh, kh, vh, gh = (split_heads(x, images) for x in (q, k, v, gmixed))
    scale = HDIM**-0.5
    scores = jnp.einsum("iqhe,ikhe->ihqk", qh, kh, preferred_element_type=single) * scale
    scores = jnp.where(key_mask[:, None, None, :], scores, -1e30)
    probs = jnp.exp(scores - lse)
    gprobs = jnp.einsum("iqhe,ikhe->ihqk", gh, vh, preferred_element_type=single)
    gscores = (
        probs * (gprobs - jnp.sum(probs * gprobs, axis=-1, keepdims=True))
    ).astype(bfloat)
    gq = jnp.einsum("ihqk,ikhe->iqhe", gscores, kh, preferred_element_type=single) * scale
    gk = jnp.einsum("ihqk,iqhe->ikhe", gscores, qh, preferred_element_type=single) * scale
    gv = jnp.einsum("ihqk,iqhe->ikhe", probs.astype(bfloat), gh, preferred_element_type=single)
    return tuple(x.reshape(q.shape).astype(bfloat) for x in (gq, gk, gv))


def swap(values, axis, count, bit):
    return lax.ppermute(values, axis, [(i, i ^ bit) for i in range(count)])


def dp_stages(count):
    stages, stride = [], 1
    while stride < count:
        radix = 2 if stride == 1 else min(4, count // stride)
        stages.append((radix, stride))
        stride *= radix
    return stages


def part_at(values, index, parts):
    size = values.shape[0] // parts
    return lax.dynamic_slice_in_dim(values, index * size, size, 0)


def scatter_dp(values, count):
    place = lax.axis_index("dp")
    for radix, stride in dp_stages(count):
        mine = (place // stride) % radix
        total = part_at(values, mine, radix).astype(single)
        for hop in range(1, radix):
            piece = part_at(values, mine ^ hop, radix)
            total = total + swap(piece, "dp", count, hop * stride).astype(single)
        values = total.astype(bfloat)
    return values


def gather_dp(values, count):
    place = lax.axis_index("dp")
    for radix, stride in reversed(dp_stages(count)):
        mine = (place // stride) % radix
        size = values.shape[0]
        whole = jnp.zeros((size * radix,) + values.shape[1:], values.dtype)
        whole = lax.dynamic_update_slice_in_dim(whole, values, mine * size, 0)
        for hop in range(1, radix):
            piece = swap(values, "dp", count, hop * stride)
            whole = lax.dynamic_update_slice_in_dim(whole, piece, (mine ^ hop) * size, 0)
        values = whole
    return values


def gather_slots(shard):
    across = swap(shard, "tensor", 4, 2)
    return [shard, swap(shard, "tensor", 4, 1), across, swap(across, "tensor", 4, 1)]


def scatter_slots(slots, count):
    near = swap(slots[1], "tensor", 4, 1)
    far = swap(slots[3], "tensor", 4, 1)
    far = (slots[2].astype(single) + far.astype(single)).astype(bfloat)
    across = swap(far, "tensor", 4, 2)
    total = (slots[0].astype(single) + near.astype(single) + across.astype(single)).astype(bfloat)
    return gather_dp(scatter_dp(total, count), count)


def feed_forward(stream, gain_row, shift_row, expand, expbias, shrink, outbias_row):
    unit, factor = norm_parts(stream)
    n = (unit * gain_row + shift_row).astype(bfloat)
    hidden, active = [], []
    branch = outbias_row
    for r in range(4):
        h = dot(n, expand[r], 1, 0) + expbias[r]
        a = gelu_parts(h)[0].astype(bfloat)
        hidden.append(h)
        active.append(a)
        branch = branch + dot(a, shrink[r], 1, 0)
    return branch, (unit, factor, n, hidden, active)


def feed_grads(upstream, scale_row, saved, gain_row, expand, shrink):
    unit, factor, n, hidden, active = saved
    gb = (scale_row * upstream).astype(bfloat)
    gn = 0.0
    packs, bias_rows = [], []
    for r in range(4):
        gact = dot(gb, shrink[r], 1, 1)
        gh = (gelu_parts(hidden[r])[1] * gact).astype(bfloat)
        gn = gn + dot(gh, expand[r], 1, 1)
        packs.append(
            jnp.concatenate([dot(n, gh, 0, 0).astype(bfloat), dot(active[r], gb, 0, 0).astype(bfloat)], 0)
        )
        bias_rows.append(rows_sum(gh))
    flowing, gain_grad, shift_grad = norm_grads(gn, unit, factor, gain_row)
    return upstream + flowing, gain_grad, shift_grad, rows_sum(gb), packs, bias_rows


def attention(query_in, context_in, weights, inbias, outbias_row, key_mask):
    wq, wk, wv, wo = weights
    q = (dot(query_in, wq, 1, 0) + inbias[0]).astype(bfloat)
    k = dot(context_in, wk, 1, 0).astype(bfloat)
    v = (dot(context_in, wv, 1, 0) + inbias[1]).astype(bfloat)
    mixed, lse = attend(q, k, v, key_mask)
    return dot(mixed, wo, 1, 0) + outbias_row, (q, k, v, mixed, lse)


def attention_grads(upstream, scale_row, saved, query_in, context_in, weights, key_mask):
    wq, wk, wv, wo = weights
    q, k, v, mixed, lse = saved
    ga = (scale_row * upstream).astype(bfloat)
    gmixed = dot(ga, wo, 1, 1).astype(bfloat)
    gq, gk, gv = attend_grads(q, k, v, lse, gmixed, key_mask)
    g_out = dot(mixed, ga, 0, 0).astype(bfloat)
    g_q = dot(gq, query_in, 0, 0).astype(bfloat)
    g_k = dot(gk, context_in, 0, 0).astype(bfloat)
    g_v = dot(gv, context_in, 0, 0).astype(bfloat)
    width = g_out.shape[0] // 4
    packs = [
        jnp.concatenate([g[r * width : (r + 1) * width] for g in (g_q, g_k, g_v, g_out)], 0)
        for r in range(4)
    ]
    g_query_in = dot(gq, wq, 1, 1)
    g_context_in = dot(gk, wk, 1, 1) + dot(gv, wv, 1, 1)
    gq_sum = rows_sum(gq).reshape(4, width)
    gv_sum = rows_sum(gv).reshape(4, width)
    return g_query_in, g_context_in, packs, rows_sum(ga), jnp.concatenate([gq_sum, gv_sum], 1)


def attention_weights(inproj, outproj):
    inslots, outslots = gather_slots(inproj), gather_slots(outproj)
    projections = [jnp.concatenate([s[j] for s in inslots], 1) for j in range(3)]
    return (*projections, jnp.concatenate(outslots, 0))


def make_local(dp_count):
    def to_images(values):
        moved = lax.all_to_all(values.astype(bfloat), "tensor", split_axis=0, concat_axis=2, tiled=True)
        return moved.reshape(-1, values.shape[-1]).astype(single)

    def local(
        patches, mask_queries, visible, lengths, d_latent, d_regress,
        e_gain, e_shift, e_scale, e_inproj, e_inbias, e_outproj, e_outbias, e_expand, e_expbias, e_shrink,
        r_gain, r_shift, r_scale, r_inproj, r_inbias, r_outproj, r_outbias, r_expand, r_expbias, r_shrink,
    ):
        micro, images, part, width = patches.shape
        me = lax.axis_index("tensor")
        patch_count = visible.shape[2]
        rows = images * patch_count
        heads_width = e_inbias.shape[1]

        def to_patches(values):
            moved = values.astype(bfloat).reshape(1, images, patch_count, width)
            return lax.all_to_all(moved, "tensor", split_axis=2, concat_axis=0, tiled=True).astype(single)

        tokens = to_images(patches)
        queries = to_images(mask_queries)
        g_latent_in = to_images(d_latent)
        g_regress_in = to_images(d_regress)

        position = jnp.arange(patch_count, dtype=jnp.int32)
        my_lengths = lax.dynamic_index_in_dim(lengths, me, 0, keepdims=False)
        my_visible = lax.dynamic_index_in_dim(visible, me, 0, keepdims=False)
        valid = position[None, :] < my_lengths[:, None]
        seen = (my_visible == 1) | (position[None, :] == 0)
        seen_rows = seen.reshape(rows, 1)

        small_bias = jnp.concatenate(
            [e_inbias.reshape(-1), r_inbias.reshape(-1), e_expbias, r_expbias]
        )
        all_bias = lax.all_gather(small_bias, "tensor", axis=0)
        all_bias = jnp.stack(
            [lax.dynamic_index_in_dim(all_bias, me ^ r, 0, keepdims=False) for r in range(4)]
        )
        hw = heads_width
        e_inb = all_bias[:, : 2 * hw].reshape(4, 2, hw).transpose(1, 0, 2).reshape(2, 4 * hw)
        r_inb = all_bias[:, 2 * hw : 4 * hw].reshape(4, 2, hw).transpose(1, 0, 2).reshape(2, 4 * hw)
        hidden_width = e_expbias.shape[0]
        e_exb = all_bias[:, 4 * hw : 4 * hw + hidden_width]
        r_exb = all_bias[:, 4 * hw + hidden_width :]

        e_att = attention_weights(e_inproj, e_outproj)
        e_exp, e_shr = gather_slots(e_expand), gather_slots(e_shrink)
        r_att = attention_weights(r_inproj, r_outproj)
        r_exp, r_shr = gather_slots(r_expand), gather_slots(r_shrink)

        unit0, factor0 = norm_parts(tokens)
        n0 = (unit0 * e_gain[0] + e_shift[0]).astype(bfloat)
        e_branch_a, e_saved = attention(n0, n0, e_att, e_inb, e_outbias[0], valid & seen)
        middle = tokens + e_scale[0] * e_branch_a
        e_branch_f, e_ff = feed_forward(middle, e_gain[1], e_shift[1], e_exp, e_exb, e_shr, e_outbias[1])
        latent = middle + e_scale[1] * e_branch_f

        unit_q, factor_q = norm_parts(queries)
        qn = (unit_q * r_gain[0] + r_shift[0]).astype(bfloat)
        context = jnp.where(seen_rows, latent, queries)
        unit_c, factor_c = norm_parts(context)
        cn = (unit_c * r_gain[1] + r_shift[1]).astype(bfloat)
        r_branch_a, r_saved = attention(qn, cn, r_att, r_inb, r_outbias[0], valid)
        r_mid = queries + r_scale[0] * r_branch_a
        r_branch_f, r_ff = feed_forward(r_mid, r_gain[2], r_shift[2], r_exp, r_exb, r_shr, r_outbias[1])
        regressed = r_mid + r_scale[1] * r_branch_f

        g = g_regress_in
        r_scale1 = jnp.sum(g * r_branch_f, axis=0)
        h, r_gain2, r_shift2, r_ob1, r_ff_packs, r_exb_rows = feed_grads(
            g, r_scale[1], r_ff, r_gain[2], r_exp, r_shr
        )
        r_ff_shard = scatter_slots(r_ff_packs, dp_count)
        r_scale0 = jnp.sum(h * r_branch_a, axis=0)
        g_q, g_c, r_at_packs, r_ob0, r_inb_rows = attention_grads(
            h, r_scale[0], r_saved, qn, cn, r_att, valid
        )
        r_at_shard = scatter_slots(r_at_packs, dp_count)
        flow_q, r_gain0, r_shift0 = norm_grads(g_q, unit_q, factor_q, r_gain[0])
        flow_c, r_gain1, r_shift1 = norm_grads(g_c, unit_c, factor_c, r_gain[1])
        grad_queries = h + flow_q + jnp.where(seen_rows, 0.0, flow_c)

        g = g_latent_in + jnp.where(seen_rows, flow_c, 0.0)
        e_scale1 = jnp.sum(g * e_branch_f, axis=0)
        h, e_gain1, e_shift1, e_ob1, e_ff_packs, e_exb_rows = feed_grads(
            g, e_scale[1], e_ff, e_gain[1], e_exp, e_shr
        )
        e_ff_shard = scatter_slots(e_ff_packs, dp_count)
        e_scale0 = jnp.sum(h * e_branch_a, axis=0)
        g_a, g_b, e_at_packs, e_ob0, e_inb_rows = attention_grads(
            h, e_scale[0], e_saved, n0, n0, e_att, valid & seen
        )
        e_at_shard = scatter_slots(e_at_packs, dp_count)
        flow, e_gain0, e_shift0 = norm_grads(g_a + g_b, unit0, factor0, e_gain[0])
        grad_patches = h + flow

        shared = jnp.stack(
            [
                e_gain0, e_gain1, e_shift0, e_shift1, e_scale0, e_scale1, e_ob0, e_ob1,
                r_gain0, r_gain1, r_gain2, r_shift0, r_shift1, r_shift2, r_scale0, r_scale1, r_ob0, r_ob1,
            ]
        )
        owned = [
            jnp.concatenate([e_inb_rows[r], r_inb_rows[r], e_exb_rows[r], r_exb_rows[r]])
            for r in range(4)
        ]
        owned = jnp.stack(owned)
        owned = jnp.stack([lax.dynamic_index_in_dim(owned, me ^ r, 0, keepdims=False) for r in range(4)])
        shared, owned = lax.psum((shared, owned), ("dp", "tensor"))
        mine = lax.dynamic_index_in_dim(owned, me, 0, keepdims=False)

        def attention_outputs(shard):
            shard = shard.astype(single)
            proj = shard[: 3 * hw].reshape(3, hw, width).transpose(0, 2, 1)
            return proj, shard[3 * hw :]

        def feed_outputs(shard):
            shard = shard.astype(single)
            return shard[:width], shard[width:]

        e_in_g, e_out_g = attention_outputs(e_at_shard)
        r_in_g, r_out_g = attention_outputs(r_at_shard)
        e_exp_g, e_shr_g = feed_outputs(e_ff_shard)
        r_exp_g, r_shr_g = feed_outputs(r_ff_shard)
        e_inb_g = mine[: 2 * hw].reshape(2, hw)
        r_inb_g = mine[2 * hw : 4 * hw].reshape(2, hw)
        e_exb_g = mine[4 * hw : 4 * hw + hidden_width]
        r_exb_g = mine[4 * hw + hidden_width :]
        return (
            to_patches(latent),
            to_patches(regressed),
            to_patches(grad_patches),
            to_patches(grad_queries),
            shared[0:2], shared[2:4], shared[4:6], e_in_g, e_inb_g, e_out_g, shared[6:8],
            e_exp_g, e_exb_g, e_shr_g,
            shared[8:11], shared[11:14], shared[14:16], r_in_g, r_inb_g, r_out_g, shared[16:18],
            r_exp_g, r_exb_g, r_shr_g,
        )

    return local


def solution(mesh):
    rows = P(None, "dp", "tensor", None)
    columns = P(None, "tensor")
    block_in = lambda: (P(), P(), P(), P(None, None, "tensor"), columns, P("tensor", None), P(), columns, P("tensor"), P("tensor", None))
    assert mesh.shape["tensor"] == 4
    return jax.shard_map(
        make_local(mesh.shape["dp"]),
        mesh=mesh,
        in_specs=(rows, rows, P(None, "dp", None), P(None, "dp"), rows, rows, *block_in(), *block_in()),
        out_specs=(rows, rows, rows, rows, *block_in(), *block_in()),
        check_vma=False,
    )
```

```python
import functools
import jax
import jax.numpy as jnp
from jax import lax
from jax.experimental import pallas as pl
from jax.experimental.pallas import tpu as pltpu
from jax.sharding import PartitionSpec as P

HDIM = 64
epsilon = 1e-06
bfloat = jnp.bfloat16
single = jnp.float32
SLOTS = 4
GRANT = 60 * 2**20


def dot(a, b, ca, cb):
    return lax.dot_general(a, b, (((ca,), (cb,)), ((), ())), preferred_element_type=single)


def norm_parts(values):
    average = jnp.mean(values, axis=-1, keepdims=True)
    centred = values - average
    variance = jnp.mean(centred * centred, axis=-1, keepdims=True)
    factor = lax.rsqrt(variance + epsilon)
    return centred * factor, factor


def norm_back(gradient, unit, factor, gain_row):
    scaled = gradient * gain_row
    return factor * (
        scaled
        - jnp.mean(scaled, axis=-1, keepdims=True)
        - unit * jnp.mean(scaled * unit, axis=-1, keepdims=True)
    )


def column_sum(values):
    return jnp.sum(values, axis=0, keepdims=True)


def gelu_parts(hidden):
    size = jnp.abs(hidden)
    bell = jnp.exp(-0.5 * hidden * hidden)
    t = 1.0 / (1.0 + (0.3275911 * 0.5**0.5) * size)
    poly = t * (0.127414796 + t * (-0.142248368 + t * (0.7107068705 + t * (-0.7265760135 + t * 0.5307027145))))
    tail = poly * bell
    below = jnp.where(hidden < 0, tail, 1.0 - tail)
    return hidden * below, below + hidden * bell * 0.3989422804


def start_copies(step, sources, buffer, sems):
    @pl.when(step == 0)
    def _():
        for r, source in enumerate(sources):
            pltpu.make_async_copy(source, buffer.at[r], sems.at[r]).start()


def wait_copy(step, sources, buffer, sems):
    for r, source in enumerate(sources):

        @pl.when(step == r)
        def _(r=r, source=source):
            pltpu.make_async_copy(source, buffer.at[r], sems.at[r]).wait()


def whole(shape):
    zeros = (0,) * len(shape)
    return pl.BlockSpec(shape, lambda j: zeros, pipeline_mode=pl.Buffered(1))


def by_slot(shape):
    zeros = (0,) * (len(shape) - 1)
    return pl.BlockSpec((1,) + shape[1:], lambda j: (j,) + zeros)


ANY = pl.BlockSpec(memory_space=pl.ANY)
SEND, KEEP = (1, 3), (0, 2)
BIAS_ROWS = 16


def store_blocks(low_ref, values):
    blocks, images, part = low_ref.shape[:3]
    for r in range(blocks):
        for i in range(images):
            start = (i * blocks + r) * part
            low_ref[r, i] = values[start : start + part].astype(bfloat)


def run(call_inputs, outs, specs, deps, body, **kwargs):
    skip = len(deps)
    return pl.pallas_call(
        lambda *refs: body(*refs[skip:]),
        in_specs=[ANY] * skip + [s for s, _ in call_inputs],
        out_specs=specs,
        out_shape=[jax.ShapeDtypeStruct(s, d) for s, d in outs],
        compiler_params=pltpu.CompilerParams(vmem_limit_bytes=GRANT),
        cost_estimate=pl.CostEstimate(flops=1, bytes_accessed=1, transcendentals=0),
        **kwargs,
    )(*deps, *[v for _, v in call_inputs])


def feed_sources(refs):
    near, far = refs[:4], refs[4:]
    return [near[0], near[2], *(f.at[0] for f in far)], [near[1], near[3], *(f.at[1] for f in far)]


def feed_forward_kernel(wide, *refs):
    x_ref, rows_ref = refs[:2]
    expand, shrink = feed_sources(refs[2:8])
    biases = refs[8:12]
    outs = refs[12 : 17 + wide]
    out_ref = outs[0] if wide else None
    low_ref, branch_ref, n_ref, act_ref, slope_ref = outs[wide:]
    ebuf, sbuf, bbuf, acc, esem, ssem, bsem = refs[17 + wide :]
    j = pl.program_id(0)
    width = x_ref.shape[1]
    tops = [b.at[pl.ds(width, BIAS_ROWS)] for b in biases]
    start_copies(j, tops, bbuf, bsem)
    start_copies(j, expand, ebuf, esem)
    start_copies(j, shrink, sbuf, ssem)

    @pl.when(j == 0)
    def _():
        unit, _ = norm_parts(x_ref[...])
        n_ref[...] = (unit * rows_ref[0:1] + rows_ref[1:2]).astype(bfloat)
        acc[...] = jnp.zeros_like(acc)

    wait_copy(j, tops, bbuf, bsem)
    wait_copy(j, expand, ebuf, esem)
    bias = bbuf[j].astype(single)
    bias = bias[1:2] + bias[2:3]
    hidden_width = ebuf.shape[2]
    step = 256
    n = n_ref[...]
    for c in range(0, hidden_width, step):
        hidden = dot(n, ebuf[j, :, c : c + step], 1, 0) + bias[:, c : c + step]
        act, slope = gelu_parts(hidden)
        act_ref[0, :, c : c + step] = act.astype(bfloat)
        slope_ref[0, :, c : c + step] = slope.astype(bfloat)
    wait_copy(j, shrink, sbuf, ssem)
    acc[...] += dot(act_ref[0], sbuf[j], 1, 0)

    @pl.when(j == SLOTS - 1)
    def _():
        branch = acc[...] + rows_ref[2:3]
        branch_ref[...] = branch.astype(bfloat)
        out = x_ref[...] + rows_ref[3:4] * branch
        if wide:
            out_ref[...] = out
        store_blocks(low_ref, out)


def feed_forward(x, gain, shift, outbias, scale, weights, biases, blocks, wide, deps=()):
    rows, width = x.shape
    hidden = weights[0].shape[1]
    params = jnp.stack([gain, shift, outbias, scale])
    outs = [((rows, width), single)] if wide else []
    outs += [(blocks, bfloat)] + [((rows, width), bfloat)] * 2 + [((SLOTS, rows, hidden), bfloat)] * 2
    specs = [whole(s) for s, _ in outs[:-2]] + [by_slot(s) for s, _ in outs[-2:]]
    return run(
        [(whole(x.shape), x), (whole(params.shape), params)] + [(ANY, w) for w in (*weights, *biases)],
        outs,
        specs,
        deps,
        body=functools.partial(feed_forward_kernel, wide),
        grid=(SLOTS,),
        name="feed_forward",
        scratch_shapes=[
            pltpu.VMEM((SLOTS, width, hidden), bfloat),
            pltpu.VMEM((SLOTS, hidden, width), bfloat),
            pltpu.VMEM((SLOTS, BIAS_ROWS, width), bfloat),
            pltpu.VMEM((rows, width), single),
            pltpu.SemaphoreType.DMA((SLOTS,)),
            pltpu.SemaphoreType.DMA((SLOTS,)),
            pltpu.SemaphoreType.DMA((SLOTS,)),
        ],
    )


def half_specs(shape, slots):
    zeros = (0,) * (len(shape) - 1)
    first, step = slots[0], slots[1] - slots[0]
    return pl.BlockSpec((1,) + shape[1:], lambda j: (first + step * j,) + zeros)


def feed_grads_kernel(last, *refs):
    g_ref, rows_ref, branch_ref, n_ref, act_ref, slope_ref = refs[:6]
    refs = refs[6:]
    if last:
        x_ref, part_ref = refs[:2]
        refs = refs[2:]
    expand, shrink = (refs[0], refs[2].at[0]), (refs[1], refs[2].at[1])
    if last:
        h_ref, egrad_ref, sgrad_ref, bias_ref, sums_ref = refs[3:8]
        refs = refs[8:]
    else:
        part_out, egrad_ref, sgrad_ref, bias_ref = refs[3:7]
        refs = refs[7:]
    ebuf, sbuf, gb, nt, acc, esem, ssem = refs
    j = pl.program_id(0)
    start_copies(j, shrink, sbuf, ssem)
    start_copies(j, expand, ebuf, esem)

    @pl.when(j == 0)
    def _():
        g = g_ref[...].astype(single)
        low = (rows_ref[1:2] * g).astype(bfloat)
        gb[...] = low
        nt[...] = n_ref[...].T
        if last:
            sums_ref[2:3] = column_sum(g * branch_ref[...].astype(single))
            sums_ref[3:4] = column_sum(low.astype(single))
            acc[...] = part_ref[...]
        else:
            acc[...] = jnp.zeros_like(acc)

    wait_copy(j, shrink, sbuf, ssem)
    wait_copy(j, expand, ebuf, esem)
    width, hidden = ebuf.shape[1], ebuf.shape[2]
    step = 256
    low = gb[...]
    for c in range(0, hidden, step):
        gact = dot(low, sbuf[j, c : c + step, :], 1, 1)
        gh = (slope_ref[0, :, c : c + step].astype(single) * gact).astype(bfloat)
        bias_ref[0, :, c : c + step] = column_sum(gh.astype(single))
        acc[...] += dot(gh, ebuf[j, :, c : c + step], 1, 1)
        egrad_ref[0, :, c : c + step] = dot(nt[...], gh, 1, 0).astype(bfloat)
        sgrad_ref[0, c : c + step, :] = dot(act_ref[0, :, c : c + step], low, 0, 0).astype(bfloat)

    @pl.when(j == 1)
    def _():
        gn = acc[...]
        if last:
            unit, factor = norm_parts(x_ref[...])
            sums_ref[0:1] = column_sum(gn * unit)
            sums_ref[1:2] = column_sum(gn)
            h_ref[...] = g_ref[...].astype(single) + norm_back(gn, unit, factor, rows_ref[0:1])
        else:
            part_out[...] = gn


def feed_grads(slots, part, g, x, gain, scale, branch, n, act, slope, weights, deps=()):
    first = 2 if slots == SEND else 0
    weights = (weights[first], weights[first + 1], weights[5 if slots == SEND else 4])
    last = part is not None
    rows, width = n.shape
    hidden = weights[0].shape[1]
    params = jnp.stack([gain, scale])
    unit = (2, width, hidden)
    outs = [((rows, width), single), (unit, bfloat), ((2, hidden, width), bfloat), ((2, 1, hidden), single)]
    specs = [whole((rows, width)), by_slot(unit), by_slot((2, hidden, width)), by_slot((2, 1, hidden))]
    if last:
        outs.append(((4, width), single))
        specs.append(whole((4, width)))
    ins = [(whole(v.shape), v) for v in (g, params, branch, n)]
    ins += [(half_specs(v.shape, slots), v) for v in (act, slope)]
    if last:
        ins += [(whole(v.shape), v) for v in (x, part)]
    ins += [(ANY, w) for w in weights]
    return run(
        ins,
        outs,
        specs,
        deps,
        body=functools.partial(feed_grads_kernel, last),
        grid=(2,),
        name="feed_grads",
        scratch_shapes=[
            pltpu.VMEM((2, width, hidden), bfloat),
            pltpu.VMEM((2, hidden, width), bfloat),
            pltpu.VMEM((rows, width), bfloat),
            pltpu.VMEM((width, rows), bfloat),
            pltpu.VMEM((rows, width), single),
            pltpu.SemaphoreType.DMA((2,)),
            pltpu.SemaphoreType.DMA((2,)),
        ],
    )


def attention_kernel(cross, *refs):
    x_ref = refs[0]
    refs = refs[1:]
    if cross:
        latent_ref, seen_ref = refs[:2]
        refs = refs[2:]
    rows_ref, mask_ref = refs[:2]
    weights = refs[2:6]
    mid_ref, branch_ref, qn_ref = refs[6:9]
    refs = refs[9:]
    if cross:
        cn_ref = refs[0]
        refs = refs[1:]
    q_ref, k_ref, v_ref, p_ref, mix_ref, wbuf, acc, wsem = refs
    j = pl.program_id(0)
    start_copies(j, weights, wbuf, wsem)

    @pl.when(j == 0)
    def _():
        x = x_ref[...].astype(single)
        unit, _ = norm_parts(x)
        qn_ref[...] = (unit * rows_ref[0:1] + rows_ref[1:2]).astype(bfloat)
        if cross:
            context = jnp.where(seen_ref[...] > 0, latent_ref[...], x)
            unit, _ = norm_parts(context)
            cn_ref[...] = (unit * rows_ref[4:5] + rows_ref[5:6]).astype(bfloat)
        acc[...] = jnp.zeros_like(acc)

    wait_copy(j, weights, wbuf, wsem)
    qn = qn_ref[...]
    cn = cn_ref[...] if cross else qn
    cols = q_ref.shape[2]
    bias = wbuf[j, 4 * cols : 4 * cols + BIAS_ROWS].astype(single)[0:1]
    bias = bias[:, : 2 * cols] + bias[:, 2 * cols :]
    q = (dot(qn, wbuf[j, :cols], 1, 1) + bias[:, :cols]).astype(bfloat)
    k = dot(cn, wbuf[j, cols : 2 * cols], 1, 1).astype(bfloat)
    v = (dot(cn, wbuf[j, 2 * cols : 3 * cols], 1, 1) + bias[:, cols:]).astype(bfloat)
    q_ref[0] = q
    k_ref[0] = k
    v_ref[0] = v
    images = mask_ref.shape[0]
    patches = mask_ref.shape[2]
    heads = cols // HDIM
    scaled = q * jnp.asarray(HDIM**-0.5, bfloat)
    for i in range(images):
        span = slice(i * patches, (i + 1) * patches)
        mixed = []
        for h in range(heads):
            lanes = slice(h * HDIM, (h + 1) * HDIM)
            scores = dot(scaled[span, lanes], k[span, lanes], 1, 1) + mask_ref[i]
            expo = jnp.exp(scores - jnp.max(scores, axis=-1, keepdims=True))
            probs = (expo * (1.0 / jnp.sum(expo, axis=-1, keepdims=True))).astype(bfloat)
            p_ref[0, i * heads + h] = probs
            mixed.append(dot(probs, v[span, lanes], 1, 0))
        mix_ref[0, span, :] = jnp.concatenate(mixed, axis=1).astype(bfloat)
    acc[...] += dot(mix_ref[0], wbuf[j, 3 * cols : 4 * cols], 1, 0)

    @pl.when(j == SLOTS - 1)
    def _():
        branch = acc[...] + rows_ref[2:3]
        branch_ref[...] = branch.astype(bfloat)
        mid_ref[...] = x_ref[...].astype(single) + rows_ref[3:4] * branch


def attention(x, cross, gains, shifts, outbias, scale, mask, weights, deps=()):
    rows, width = x.shape
    cols = (weights[0].shape[0] - BIAS_ROWS) // 4
    images, _, patches = mask.shape
    heads = cols // HDIM
    params = [gains[0], shifts[0], outbias, scale] + ([gains[1], shifts[1]] if cross else [])
    params = jnp.stack(params)
    extra = list(cross) if cross else []
    outs = [((rows, width), single), ((rows, width), bfloat), ((rows, width), bfloat)]
    outs += [((rows, width), bfloat)] if cross else []
    outs += [((SLOTS, rows, cols), bfloat)] * 3
    outs += [((SLOTS, images * heads, patches, patches), bfloat), ((SLOTS, rows, cols), bfloat)]
    return run(
        [(whole(v.shape), v) for v in (x, *extra, params, mask)] + [(ANY, w) for w in weights],
        outs,
        [whole(s) if len(s) == 2 else by_slot(s) for s, _ in outs],
        deps,
        body=functools.partial(attention_kernel, bool(cross)),
        grid=(SLOTS,),
        name="attention",
        scratch_shapes=[
            pltpu.VMEM((SLOTS,) + weights[0].shape, bfloat),
            pltpu.VMEM((rows, width), single),
            pltpu.SemaphoreType.DMA((SLOTS,)),
        ],
    )


def attention_grads_kernel(cross, last, *refs):
    refs = list(refs)
    take = lambda n: [refs.pop(0) for _ in range(n)]
    h_ref, rows_ref, branch_ref, qn_ref = take(4)
    cn_ref = take(1)[0] if cross else qn_ref
    q_ref, k_ref, v_ref, p_ref, mix_ref = take(5)
    if last:
        x_ref, parta_ref = take(2)
        if cross:
            partb_ref, latent_ref, seen_ref, dlat_ref = take(4)
    weights = take(2)
    outa_ref = take(1)[0]
    outb_ref = take(1)[0] if cross else None
    pack_ref, bias_ref = take(2)
    sums_ref = take(1)[0] if last else None
    wbuf, ga, acc_a = take(3)
    acc_b = take(1)[0] if cross else None
    (wsem,) = take(1)
    j = pl.program_id(0)
    start_copies(j, weights, wbuf, wsem)

    @pl.when(j == 0)
    def _():
        h = h_ref[...]
        low = (rows_ref[0:1] * h).astype(bfloat)
        ga[...] = low
        if last:
            sums_ref[0:1] = column_sum(h * branch_ref[...].astype(single))
            sums_ref[1:2] = column_sum(low.astype(single))
            acc_a[...] = parta_ref[...]
            if cross:
                acc_b[...] = partb_ref[...]
        else:
            acc_a[...] = jnp.zeros_like(acc_a)
            if cross:
                acc_b[...] = jnp.zeros_like(acc_b)

    wait_copy(j, weights, wbuf, wsem)
    cols = q_ref.shape[2]
    heads = cols // HDIM
    patches = p_ref.shape[2]
    images = p_ref.shape[1] // heads
    scale = HDIM**-0.5
    low = ga[...]
    gm = dot(low, wbuf[j, 3 * cols : 4 * cols], 1, 1).astype(bfloat)
    parts = []
    for i in range(images):
        span = slice(i * patches, (i + 1) * patches)
        q, k, v = q_ref[0, span], k_ref[0, span], v_ref[0, span]
        gmi = gm[span]
        qt, kt, gmt = q.T, k.T, gmi.T
        gqt, gkt, gvt = [], [], []
        for h in range(heads):
            lanes = slice(h * HDIM, (h + 1) * HDIM)
            low_p = p_ref[0, i * heads + h]
            probs = low_p.astype(single)
            product = probs * dot(gmi[:, lanes], v[:, lanes], 1, 1)
            gs = (product - probs * jnp.sum(product, axis=-1, keepdims=True)).astype(bfloat)
            gqt.append(dot(kt[lanes], gs, 1, 1))
            gkt.append(dot(qt[lanes], gs, 1, 0))
            gvt.append(dot(gmt[lanes], low_p, 1, 0))
        gqt = (jnp.concatenate(gqt, 0) * scale).astype(bfloat)
        gkt = (jnp.concatenate(gkt, 0) * scale).astype(bfloat)
        gvt = jnp.concatenate(gvt, 0).astype(bfloat)
        parts.append((gqt, gkt, gvt))
        a = acc_a[span] + dot(gqt.T, wbuf[j, :cols], 1, 0)
        b = dot(gkt.T, wbuf[j, cols : 2 * cols], 1, 0) + dot(gvt.T, wbuf[j, 2 * cols : 3 * cols], 1, 0)
        if cross:
            acc_a[span] = a
            acc_b[span] += b
        else:
            acc_a[span] = a + b
    gqt, gkt, gvt = (jnp.concatenate([p[n] for p in parts], 1) for n in range(3))
    bias_ref[0, 0] = jnp.sum(gqt.astype(single), axis=1)
    bias_ref[0, 1] = jnp.sum(gvt.astype(single), axis=1)
    qn = qn_ref[...]
    cn = cn_ref[...] if cross else qn
    pack_ref[0, 0:cols] = dot(gqt, qn, 1, 0).astype(bfloat)
    pack_ref[0, cols : 2 * cols] = dot(gkt, cn, 1, 0).astype(bfloat)
    pack_ref[0, 2 * cols : 3 * cols] = dot(gvt, cn, 1, 0).astype(bfloat)
    pack_ref[0, 3 * cols :] = dot(mix_ref[0], low, 0, 0).astype(bfloat)

    @pl.when(j == 1)
    def _():
        gn = acc_a[...]
        if not last:
            outa_ref[...] = gn
            if cross:
                outb_ref[...] = acc_b[...]
            return
        x = x_ref[...].astype(single)
        unit, factor = norm_parts(x)
        sums_ref[2:3] = column_sum(gn * unit)
        sums_ref[3:4] = column_sum(gn)
        gx = h_ref[...] + norm_back(gn, unit, factor, rows_ref[1:2])
        if cross:
            seen = seen_ref[...] > 0
            unit, factor = norm_parts(jnp.where(seen, latent_ref[...], x))
            gn = acc_b[...]
            sums_ref[4:5] = column_sum(gn * unit)
            sums_ref[5:6] = column_sum(gn)
            flow = norm_back(gn, unit, factor, rows_ref[2:3])
            gx = gx + jnp.where(seen, 0.0, flow)
            outb_ref[...] = dlat_ref[...].astype(single) + jnp.where(seen, flow, 0.0)
        store_blocks(outa_ref, gx)


def attention_grads(slots, parts, h, x, cross, gains, scale, branch, qn, cn, q, k, v, p, mix, weights, blocks, deps=()):
    last = parts is not None
    rows, width = x.shape
    cols = q.shape[2]
    params = jnp.stack([scale, gains[0]] + ([gains[1]] if cross else []))
    pack = (2, 4 * cols, width)
    ins = [(whole(v.shape), v) for v in (h, params, branch, qn) + ((cn,) if cross else ())]
    ins += [(half_specs(e.shape, slots), e) for e in (q, k, v, p, mix)]
    if last:
        ins += [(whole(e.shape), e) for e in (x, *parts, *(cross or ()))]
    ins += [(ANY, weights[r]) for r in slots]
    outs = [(blocks, bfloat) if last else ((rows, width), single)]
    outs += [((rows, width), single)] if cross else []
    specs = [whole(s) for s, _ in outs] + [by_slot(pack), by_slot((2, 2, cols))]
    outs += [(pack, bfloat), ((2, 2, cols), single)]
    if last:
        count = 6 if cross else 4
        outs.append(((count, width), single))
        specs.append(whole((count, width)))
    accs = [pltpu.VMEM((rows, width), single)] * (2 if cross else 1)
    return run(
        ins,
        outs,
        specs,
        deps,
        body=functools.partial(attention_grads_kernel, bool(cross), last),
        grid=(2,),
        name="attention_grads",
        scratch_shapes=[
            pltpu.VMEM((2,) + weights[0].shape, bfloat),
            pltpu.VMEM((rows, width), bfloat),
            *accs,
            pltpu.SemaphoreType.DMA((2,)),
        ],
    )


def spread_kernel(names, me_ref, *refs):
    j = pl.program_id(0)
    count = len(refs) - names
    for r in range(count):

        @pl.when(j == r)
        def _(r=r):
            for n in range(names):
                refs[count + n][0] = refs[r][n].astype(single)


def spread(me, pieces):
    names, *block = pieces[0].shape
    zeros = (0,) * len(block)
    spec = pl.BlockSpec((1, *block), lambda j, me_ref: (me_ref[0] ^ j,) + zeros)
    return pl.pallas_call(
        functools.partial(spread_kernel, names),
        grid_spec=pltpu.PrefetchScalarGridSpec(
            num_scalar_prefetch=1,
            grid=(len(pieces),),
            in_specs=[pl.BlockSpec(p.shape, lambda j, me_ref: (0,) + zeros) for p in pieces],
            out_specs=[spec] * names,
        ),
        out_shape=[jax.ShapeDtypeStruct((len(pieces), *block), single)] * names,
        name="spread",
    )(me.reshape(1), *pieces)


def pack_kernel(in_ref, out_ref, inbias_ref, expbias_ref, pack_ref):
    cols = in_ref.shape[2]
    width = in_ref.shape[1]
    for n in range(3):
        pack_ref[n * cols : (n + 1) * cols] = in_ref[n].T
    pack_ref[3 * cols : 4 * cols] = out_ref[...]

    def halves(values):
        high = values.astype(bfloat).astype(single)
        return high, values - high

    lines = [*halves(inbias_ref[...]), *halves(expbias_ref[...])]
    lines = [jnp.concatenate(lines[:2], 1)] + lines[2:] + [jnp.zeros((BIAS_ROWS - 3, width), single)]
    pack_ref[4 * cols :] = jnp.concatenate(lines, 0).astype(bfloat)


def attention_pack(inproj, outproj, inbias, expbias):
    cols, width = outproj.shape
    return pl.pallas_call(
        pack_kernel,
        out_shape=jax.ShapeDtypeStruct((4 * cols + BIAS_ROWS, width), bfloat),
        name="pack",
    )(inproj, outproj, inbias.reshape(1, -1), expbias.reshape(1, -1))


def swap(values, axis, count, bit):
    return lax.ppermute(values, axis, [(i, i ^ bit) for i in range(count)])


def near_core(values):
    return swap(values, "tensor", SLOTS, 1)


def over_chip(values):
    return swap(values, "tensor", SLOTS, 2)


def part_at(values, index, parts, axis=0):
    size = values.shape[axis] // parts
    return lax.dynamic_slice_in_dim(values, index * size, size, axis)


def add_low(*terms):
    total = terms[0].astype(single)
    for term in terms[1:]:
        total = total + term.astype(single)
    return total.astype(bfloat)


def placed(mine, own, other):
    first = mine == 0
    return jnp.concatenate([jnp.where(first, own, other), jnp.where(first, other, own)], 0)


def tie(*values):
    return lax.optimization_barrier(values)


def gather_stages(count):
    stages, stride = [], 1
    while stride < count:
        radix = 2 if stride == 1 else min(4, count // stride)
        stages.append((radix, stride))
        stride *= radix
    return stages


def gather_piece(count):
    place, piece = lax.axis_index("dp"), 0
    for radix, stride in gather_stages(count):
        piece = piece * radix + (place // stride) % radix
    return piece


def gather_send(values, count, stage):
    radix, stride = gather_stages(count)[stage]
    return [values] + [swap(values, "dp", count, hop * stride) for hop in range(1, radix)]


def gather_join(pieces, count, stage, axis):
    radix, stride = gather_stages(count)[stage]
    mine = (lax.axis_index("dp") // stride) % radix
    size = pieces[0].shape[axis]
    shape = list(pieces[0].shape)
    shape[axis] = size * radix
    whole_array = jnp.zeros(shape, pieces[0].dtype)
    for hop, piece in enumerate(pieces):
        whole_array = lax.dynamic_update_slice_in_dim(whole_array, piece, (mine ^ hop) * size, axis)
    return whole_array


class Unit:
    def __init__(self, count, send, across_first):
        self.count, self.across_first = count, across_first
        self.pending = near_core(send)
        self.bits = []
        stride = 1
        while stride < count:
            self.bits.append(stride)
            stride *= 2
        self.stage = 0
        self.steps = 3 + 2 * (len(self.bits) - 1)

    def bit(self, n):
        return (lax.axis_index("dp") // self.bits[n]) % 2

    def hop(self, values, n):
        return swap(values, "dp", self.count, self.bits[n])

    def follow(self, previous):
        name = ("near", "first", "value")[min(previous.stage - 1, 2)]
        self.pending, kept = tie(self.pending, getattr(previous, name))
        setattr(previous, name, kept)

    def step(self):
        pending = self.pending
        stage, last = self.stage, len(self.bits) - 1
        self.stage += 1
        x = self.bit(0)
        if stage == 0:
            self.near = near = pending
            keep = self.keep
            if self.across_first:
                sent = add_low(keep[1], near[1])
                self.pending = over_chip(sent)
            else:
                sent = add_low(part_at(keep, 1 - x, 2, 1), part_at(near, 1 - x, 2, 1))
                self.pending = self.hop(sent, 0)
        elif stage == 1:
            keep, near = self.keep, self.near
            self.first = pending
            if self.across_first:
                sent = add_low(*(part_at(v, 1 - x, 2) for v in (keep[0], near[0], pending)))
                self.pending = self.hop(sent, 0)
            else:
                sent = add_low(part_at(keep[1], x, 2), part_at(near[1], x, 2), pending[1])
                self.pending = over_chip(sent)
        elif stage == 2:
            keep, near = self.keep, self.near
            first = part_at(self.first, x, 2) if self.across_first else self.first[0]
            self.value = add_low(part_at(keep[0], x, 2), part_at(near[0], x, 2), first, pending)
            sent = self.scatter(1)
        elif stage < 2 + last:
            n = stage - 2
            self.value = add_low(part_at(self.value, self.bit(n), 2), pending)
            sent = self.scatter(n + 1)
        elif stage == 2 + last:
            sent = self.value = add_low(part_at(self.value, self.bit(last), 2), pending)
            self.pending = self.hop(sent, last)
        else:
            n = last - (stage - 3 - last)
            sent = self.value = placed(self.bit(n), self.value, pending)
            self.pending = self.hop(sent, n - 1)
        return sent

    def scatter(self, n):
        sent = part_at(self.value, 1 - self.bit(n), 2)
        self.pending = self.hop(sent, n)
        return sent

    def result(self):
        return placed(self.bit(0), self.value, self.pending)


def steps_after(done, units):
    sent = []
    for n, u in enumerate(units):
        if n:
            u.follow(units[n - 1])
        else:
            u.pending, done = tie(u.pending, done)
        sent.append(u.step())
    return done, sent


TAIL = (
    "ea ef_e rf_s ef_s rf_e ra rf_s ef_e rf_e ra ea rf_s ef_e rf_e ra ef_s rf_s ea ef_e ra ef_s ea ef_e "
    "ef_s ea ef_e ef_s ea ef_s ea"
)


def make_local(count):
    def local(
        patches, mask_queries, visible, lengths, d_latent, d_regress,
        e_gain, e_shift, e_scale, e_inproj, e_inbias, e_outproj, e_outbias, e_expand, e_expbias, e_shrink,
        r_gain, r_shift, r_scale, r_inproj, r_inbias, r_outproj, r_outbias, r_expand, r_expbias, r_shrink,
    ):
        micro, images, part, width = patches.shape
        patch_count = visible.shape[2]
        rows = images * patch_count
        cols = e_inbias.shape[1]
        hidden = e_expbias.shape[0]
        blocks = (SLOTS, images, part, width)
        me = lax.axis_index("tensor")

        def pieces_of(*arrays):
            taken = []
            for r in range(SLOTS):
                one = [lax.dynamic_index_in_dim(a, me ^ r, 0, keepdims=False).astype(bfloat) for a in arrays]
                taken.append(jnp.stack(one) if len(one) > 1 else one[0])
            return taken

        def exchange(pieces):
            return [swap(p, "tensor", SLOTS, r) if r else p for r, p in enumerate(pieces)]

        def join(pieces):
            return jnp.stack(pieces, 1).reshape(rows, width)

        tokens_sent = exchange(pieces_of(patches))
        piece = gather_piece(count)
        stages = len(gather_stages(count))

        def feed_piece(expand, shrink):
            return jnp.stack([part_at(expand, piece, count), part_at(shrink, piece, count)])

        def gather_to_last(received):
            sent = gather_send(received, count, stages - 1)
            for stage in range(stages - 1, 0, -1):
                joined = gather_join(sent, count, stage, 1)
                sent = gather_send(joined, count, stage - 1)
            return joined, sent

        e_slice = over_chip(feed_piece(e_expand, e_shrink))
        e_pack = attention_pack(e_inproj, e_outproj, e_inbias, e_expbias)
        e_pack2 = over_chip(e_pack)
        r_piece, e_slice = tie(feed_piece(r_expand, r_shrink), e_slice)
        r_slice = over_chip(r_piece)
        e_gathered, e_half = gather_to_last(e_slice)
        e_pack1 = near_core(e_pack)

        tensor_order = jnp.stack([me ^ r for r in range(SLOTS)])
        position = (tensor_order[:, None] * part + jnp.arange(part)[None, :]).reshape(-1)
        my_lengths = lax.dynamic_index_in_dim(lengths, me, 0, keepdims=False)
        my_visible = lax.dynamic_index_in_dim(visible, me, 0, keepdims=False)
        my_visible = jnp.concatenate([part_at(my_visible, me ^ r, SLOTS, 1) for r in range(SLOTS)], 1)
        valid = position[None, :] < my_lengths[:, None]
        seen = (my_visible == 1) | (position[None, :] == 0)
        seen_rows = seen.reshape(rows, 1).astype(single)
        e_mask = jnp.where(valid & seen, 0.0, -1e30).astype(single)[:, None, :]
        r_mask = jnp.where(valid, 0.0, -1e30).astype(single)[:, None, :]

        tokens = join(tokens_sent)
        r_pack = attention_pack(r_inproj, r_outproj, r_inbias, r_expbias)
        q_pieces = pieces_of(mask_queries)
        g_pieces = pieces_of(d_regress, d_latent)
        e_pack2, r_pack_t, e_exp_t, e_shr_t = tie(e_pack2, r_pack, e_expand, e_shrink)
        e_pack3 = near_core(e_pack2)
        r_pack2 = over_chip(r_pack_t)
        e_exp1, e_shr1 = near_core(e_exp_t), near_core(e_shr_t)
        e_packs = [e_pack, e_pack1, e_pack2, e_pack3]
        e_mid, e_ba, n0, q0, k0, v0, p0, mix0 = attention(
            tokens, None, e_gain, e_shift, e_outbias[0], e_scale[0], e_mask, e_packs,
            [e_gathered, r_pack, *q_pieces, *g_pieces],
        )

        e_mid, r_slice, *e_half = tie(e_mid, r_slice, *e_half)
        r_gathered, r_half = gather_to_last(r_slice)
        e_feed2 = gather_join(e_half, count, 0, 1)
        e_feed3 = near_core(e_feed2)
        queries_sent = exchange(q_pieces)
        e_feeds = [e_expand, e_shrink, e_exp1, e_shr1, e_feed2, e_feed3]
        latent, latent_low, e_bf, n1, e_act, e_slope = feed_forward(
            e_mid, e_gain[1], e_shift[1], e_outbias[1], e_scale[1], e_feeds, e_packs, blocks, True, [r_slice],
        )

        latent, r_pack1_t, r_exp_t, r_shr_t = tie(latent, r_pack, r_expand, r_shrink)
        r_pack1, r_pack3 = near_core(r_pack1_t), near_core(r_pack2)
        r_exp1, r_shr1 = near_core(r_exp_t), near_core(r_shr_t)
        queries = join(queries_sent)
        r_packs = [r_pack, r_pack1, r_pack2, r_pack3]
        r_mid, r_ba, qn, cn, q1, k1, v1, p1, mix1 = attention(
            queries, (latent, seen_rows), r_gain, r_shift, r_outbias[0], r_scale[0], r_mask, r_packs, [r_gathered]
        )

        r_mid, *r_half = tie(r_mid, *r_half)
        r_feed2 = gather_join(r_half, count, 0, 1)
        r_feed3 = near_core(r_feed2)
        g_sent = exchange(g_pieces)
        r_feeds = [r_expand, r_shrink, r_exp1, r_shr1, r_feed2, r_feed3]
        regressed_low, r_bf, n2, r_act, r_slope = feed_forward(
            r_mid, r_gain[2], r_shift[2], r_outbias[1], r_scale[1], r_feeds, r_packs, blocks, False
        )

        g_regress = join([g[0] for g in g_sent])
        g_latent = join([g[1] for g in g_sent])
        outs_sent = exchange([jnp.stack([latent_low[r], regressed_low[r]]) for r in range(SLOTS)])

        def feed_back(orders, g, x, gain, scale, branch, n, act, slope, feed, deps):
            part_sum, send_e, send_s, bias_send = feed_grads(
                SEND, None, g, x, gain, scale, branch, n, act, slope, feed, deps
            )
            unit_e = Unit(count, send_e, orders[0])
            unit_s = Unit(count, send_s, orders[1])
            h, unit_e.keep, unit_s.keep, bias_keep, sums = feed_grads(
                KEEP, part_sum, g, x, gain, scale, branch, n, act, slope, feed
            )
            return h, unit_e, unit_s, (bias_send, bias_keep), sums

        h, rf_e, rf_s, rf_bias, sums_rf = feed_back(
            (True, False), g_regress, r_mid, r_gain[2], r_scale[1], r_bf, n2, r_act, r_slope, r_feeds, []
        )
        h, sent = steps_after(h, [rf_e, rf_s])
        args = (h, queries, (latent, seen_rows, g_latent), r_gain, r_scale[0], r_ba, qn, cn, q1, k1, v1, p1, mix1, r_packs, blocks)
        part_a, part_b, send, bias_send = attention_grads(SEND, None, *args, sent)
        ra = Unit(count, send, True)
        gq_low, g, ra.keep, bias_keep, sums_ra = attention_grads(KEEP, (part_a, part_b), *args, outs_sent[1:])
        ra_bias = (bias_send, bias_keep)

        g, sent = steps_after(g, [ra, rf_e, rf_s])
        outs2_sent = exchange([gq_low[r] for r in range(SLOTS)])
        h, ef_e, ef_s, ef_bias, sums_ef = feed_back(
            (False, True), g, e_mid, e_gain[1], e_scale[1], e_bf, n1, e_act, e_slope, e_feeds, sent
        )
        h, sent = steps_after(h, [rf_e, ef_e, ra, ef_s])
        args = (h, tokens, None, e_gain, e_scale[0], e_ba, n0, None, q0, k0, v0, p0, mix0, e_packs, blocks)
        part_a, send, bias_send = attention_grads(SEND, None, *args, sent)
        ea = Unit(count, send, False)
        part_a, sent = steps_after(part_a, [rf_s, rf_e])
        gp_low, ea.keep, bias_keep, sums_ea = attention_grads(KEEP, (part_a,), *args, [*sent, *outs2_sent[1:]])
        ea_bias = (bias_send, bias_keep)

        def slots_in_order(pair):
            sent, kept = (p.reshape(2, -1) for p in pair)
            return jnp.stack([kept[0], sent[0], kept[1], sent[1]])

        shared = jnp.concatenate([sums_ef, sums_ea, sums_rf, sums_ra], 0)
        owned = jnp.concatenate([slots_in_order(p) for p in (ea_bias, ra_bias, ef_bias, rf_bias)], 1)
        owned = owned.reshape(SLOTS, -1, width)
        count_s, count_o = shared.shape[0], owned.shape[1]
        small = near_core(jnp.concatenate([shared, owned[1], owned[3]], 0))
        own = owned[0] + small[count_s : count_s + count_o]
        other = owned[2] + small[count_s + count_o :]
        shared = shared + small[:count_s]
        totals = jnp.concatenate([shared, own], 0) + over_chip(jnp.concatenate([shared, other], 0))
        for n in range(count.bit_length() - 1):
            totals = totals + swap(totals, "dp", count, 2**n)

        units = dict(ea=ea, rf_e=rf_e, rf_s=rf_s, ra=ra, ef_e=ef_e, ef_s=ef_s)
        sequence = [units[name] for name in TAIL.split()]
        previous = None
        while any(u.stage < u.steps for u in units.values()):
            u = sequence.pop(0) if sequence else next(u for u in units.values() if u.stage < u.steps)
            if u.stage == u.steps:
                continue
            if previous is not None and previous is not u:
                u.follow(previous)
            u.step()
            previous = u
        outs3_sent = exchange([gp_low[r] for r in range(SLOTS)])
        out_latent, out_regressed = spread(me, outs_sent)
        (out_queries,) = spread(me, [o[None] for o in outs2_sent])
        (out_patches,) = spread(me, [o[None] for o in outs3_sent])
        rf_e, rf_s, ra, ef_e, ef_s, ea = (u.result() for u in (rf_e, rf_s, ra, ef_e, ef_s, ea))

        e_f, e_a, r_f, r_a = totals[0:4], totals[4:8], totals[8:12], totals[12:18]
        own = totals[18:].reshape(-1)
        e_inb_g = own[: 2 * cols].reshape(2, cols)
        r_inb_g = own[2 * cols : 4 * cols].reshape(2, cols)
        e_exb_g = own[4 * cols : 4 * cols + hidden]
        r_exb_g = own[4 * cols + hidden :]

        def attention_outputs(shard):
            shard = shard.astype(single)
            return shard[: 3 * cols].reshape(3, cols, width).transpose(0, 2, 1), shard[3 * cols :]

        e_in_g, e_out_g = attention_outputs(ea)
        r_in_g, r_out_g = attention_outputs(ra)
        return (
            out_latent, out_regressed, out_patches, out_queries,
            jnp.stack([e_a[2], e_f[0]]), jnp.stack([e_a[3], e_f[1]]), jnp.stack([e_a[0], e_f[2]]),
            e_in_g, e_inb_g, e_out_g, jnp.stack([e_a[1], e_f[3]]),
            ef_e.astype(single), e_exb_g, ef_s.astype(single),
            jnp.stack([r_a[2], r_a[4], r_f[0]]), jnp.stack([r_a[3], r_a[5], r_f[1]]), jnp.stack([r_a[0], r_f[2]]),
            r_in_g, r_inb_g, r_out_g, jnp.stack([r_a[1], r_f[3]]),
            rf_e.astype(single), r_exb_g, rf_s.astype(single),
        )

    return local


def solution(mesh):
    assert mesh.shape["tensor"] == SLOTS
    rows = P(None, "dp", "tensor", None)

    def block():
        return (
            P(), P(), P(), P(None, None, "tensor"), P(None, "tensor"), P("tensor", None), P(),
            P(None, "tensor"), P("tensor"), P("tensor", None),
        )

    return jax.shard_map(
        make_local(mesh.shape["dp"]),
        mesh=mesh,
        in_specs=(rows, rows, P(None, "dp", None), P(None, "dp"), rows, rows, *block(), *block()),
        out_specs=(rows, rows, rows, rows, *block(), *block()),
        check_vma=False,
    )
```

```python
import functools
import jax
import jax.numpy as jnp
from jax import lax
from jax.experimental import pallas as pl
from jax.experimental.pallas import tpu as pltpu
from jax.sharding import PartitionSpec as P

HDIM = 64
epsilon = 1e-06
bfloat = jnp.bfloat16
single = jnp.float32
SLOTS = 4
GRANT = 40 * 2**20


def dot(a, b, ca, cb):
    return lax.dot_general(a, b, (((ca,), (cb,)), ((), ())), preferred_element_type=single)


def norm_parts(values):
    average = jnp.mean(values, axis=-1, keepdims=True)
    centred = values - average
    variance = jnp.mean(centred * centred, axis=-1, keepdims=True)
    factor = lax.rsqrt(variance + epsilon)
    return centred * factor, factor


def norm_back(gradient, unit, factor, gain_row):
    scaled = gradient * gain_row
    return factor * (
        scaled
        - jnp.mean(scaled, axis=-1, keepdims=True)
        - unit * jnp.mean(scaled * unit, axis=-1, keepdims=True)
    )


def column_sum(values):
    return jnp.sum(values, axis=0, keepdims=True)


def gelu_parts(hidden):
    size = jnp.abs(hidden)
    bell = jnp.exp(-0.5 * hidden * hidden)
    t = 1.0 / (1.0 + (0.3275911 * 0.5**0.5) * size)
    poly = t * (0.127414796 + t * (-0.142248368 + t * (0.7107068705 + t * (-0.7265760135 + t * 0.5307027145))))
    tail = poly * bell
    below = jnp.where(hidden < 0, tail, 1.0 - tail)
    return hidden * below, below + hidden * bell * 0.3989422804


def start_copies(step, sources, buffer, sems):
    @pl.when(step == 0)
    def _():
        for r, source in enumerate(sources):
            pltpu.make_async_copy(source, buffer.at[r], sems.at[r]).start()


def wait_copy(step, sources, buffer, sems):
    for r, source in enumerate(sources):

        @pl.when(step == r)
        def _(r=r, source=source):
            pltpu.make_async_copy(source, buffer.at[r], sems.at[r]).wait()


def whole(shape):
    zeros = (0,) * len(shape)
    return pl.BlockSpec(shape, lambda j: zeros, pipeline_mode=pl.Buffered(1))


def by_slot(shape):
    zeros = (0,) * (len(shape) - 1)
    return pl.BlockSpec((1,) + shape[1:], lambda j: (j,) + zeros)


ANY = pl.BlockSpec(memory_space=pl.ANY)
SEND, KEEP = (1, 3), (0, 2)
BIAS_ROWS = 16
SUMS = 8


def store_blocks(low_refs, values):
    images, part = low_refs[0].shape[:2]
    for r, low_ref in enumerate(low_refs):
        for i in range(images):
            start = (i * SLOTS + r) * part
            low_ref[i] = values[start : start + part].astype(bfloat)


def run(call_inputs, outs, specs, deps, body, **kwargs):
    skip = len(deps)
    return pl.pallas_call(
        lambda *refs: body(*refs[skip:]),
        in_specs=[ANY] * skip + [s for s, _ in call_inputs],
        out_specs=specs,
        out_shape=[jax.ShapeDtypeStruct(s, d) for s, d in outs],
        compiler_params=pltpu.CompilerParams(vmem_limit_bytes=GRANT),
        cost_estimate=pl.CostEstimate(flops=20 * 10**9, bytes_accessed=2**26, transcendentals=0),
        **kwargs,
    )(*deps, *[v for _, v in call_inputs])


def feed_sources(refs):
    near, far = refs[:4], refs[4:]
    return [near[0], near[2], *(f.at[0] for f in far)], [near[1], near[3], *(f.at[1] for f in far)]


def feed_forward_kernel(wide, *refs):
    x_ref, rows_ref = refs[:2]
    expand, shrink = feed_sources(refs[2:8])
    biases = refs[8:12]
    outs = refs[12 : 20 + wide]
    out_ref = outs[0] if wide else None
    low_refs = outs[wide : wide + SLOTS]
    branch_ref, n_ref, act_ref, slope_ref = outs[wide + SLOTS :]
    ebuf, sbuf, bbuf, acc, esem, ssem, bsem = refs[20 + wide :]
    j = pl.program_id(0)
    width = x_ref.shape[1]
    tops = [b.at[pl.ds(width, BIAS_ROWS)] for b in biases]
    start_copies(j, tops, bbuf, bsem)
    start_copies(j, expand, ebuf, esem)
    start_copies(j, shrink, sbuf, ssem)

    @pl.when(j == 0)
    def _():
        unit, _ = norm_parts(x_ref[...])
        n_ref[...] = (unit * rows_ref[0:1] + rows_ref[1:2]).astype(bfloat)
        acc[...] = jnp.zeros_like(acc)

    wait_copy(j, tops, bbuf, bsem)
    wait_copy(j, expand, ebuf, esem)
    bias = bbuf[j].astype(single)
    bias = bias[1:2] + bias[2:3]
    hidden_width = ebuf.shape[2]
    step = 256
    n = n_ref[...]
    for c in range(0, hidden_width, step):
        hidden = dot(n, ebuf[j, :, c : c + step], 1, 0) + bias[:, c : c + step]
        act, slope = gelu_parts(hidden)
        act_ref[0, :, c : c + step] = act.astype(bfloat)
        slope_ref[0, :, c : c + step] = slope.astype(bfloat)
    wait_copy(j, shrink, sbuf, ssem)
    acc[...] += dot(act_ref[0], sbuf[j], 1, 0)

    @pl.when(j == SLOTS - 1)
    def _():
        branch = acc[...] + rows_ref[2:3]
        branch_ref[...] = branch.astype(bfloat)
        out = x_ref[...] + rows_ref[3:4] * branch
        if wide:
            out_ref[...] = out
        store_blocks(low_refs, out)


def feed_forward(x, gain, shift, outbias, scale, weights, biases, blocks, wide, deps=()):
    rows, width = x.shape
    hidden = weights[0].shape[1]
    params = jnp.stack([gain, shift, outbias, scale])
    outs = [((rows, width), single)] if wide else []
    outs += [(blocks, bfloat)] * SLOTS + [((rows, width), bfloat)] * 2 + [((SLOTS, rows, hidden), bfloat)] * 2
    specs = [whole(s) for s, _ in outs[:-2]] + [by_slot(s) for s, _ in outs[-2:]]
    return run(
        [(whole(x.shape), x), (whole(params.shape), params)] + [(ANY, w) for w in (*weights, *biases)],
        outs,
        specs,
        deps,
        body=functools.partial(feed_forward_kernel, wide),
        grid=(SLOTS,),
        name="feed_forward",
        scratch_shapes=[
            pltpu.VMEM((SLOTS, width, hidden), bfloat),
            pltpu.VMEM((SLOTS, hidden, width), bfloat),
            pltpu.VMEM((SLOTS, BIAS_ROWS, width), bfloat),
            pltpu.VMEM((rows, width), single),
            pltpu.SemaphoreType.DMA((SLOTS,)),
            pltpu.SemaphoreType.DMA((SLOTS,)),
            pltpu.SemaphoreType.DMA((SLOTS,)),
        ],
    )


def half_specs(shape, slots):
    zeros = (0,) * (len(shape) - 1)
    first, step = slots[0], slots[1] - slots[0]
    return pl.BlockSpec((1,) + shape[1:], lambda j: (first + step * j,) + zeros)


def feed_grads_kernel(last, *refs):
    g_ref, rows_ref, branch_ref, n_ref, act_ref, slope_ref = refs[:6]
    refs = refs[6:]
    if last:
        x_ref, part_ref = refs[:2]
        refs = refs[2:]
    expand, shrink = (refs[0], refs[2].at[0]), (refs[1], refs[2].at[1])
    h_ref, egrad_ref, sgrad_ref, sums_ref = refs[3:7]
    part_out = h_ref
    refs = refs[7:]
    ebuf, sbuf, gb, nt, acc, esem, ssem = refs
    j = pl.program_id(0)
    start_copies(j, shrink, sbuf, ssem)
    start_copies(j, expand, ebuf, esem)

    @pl.when(j == 0)
    def _():
        g = g_ref[...].astype(single)
        low = (rows_ref[1:2] * g).astype(bfloat)
        gb[...] = low
        nt[...] = n_ref[...].T
        sums_ref[...] = jnp.zeros_like(sums_ref)
        if last:
            sums_ref[4:5] = column_sum(g * branch_ref[...].astype(single))
            sums_ref[5:6] = column_sum(low.astype(single))
            acc[...] = part_ref[...]
        else:
            acc[...] = jnp.zeros_like(acc)

    wait_copy(j, shrink, sbuf, ssem)
    wait_copy(j, expand, ebuf, esem)
    width, hidden = ebuf.shape[1], ebuf.shape[2]
    step = 256
    low = gb[...]
    for c in range(0, hidden, step):
        gact = dot(low, sbuf[j, c : c + step, :], 1, 1)
        gh = (slope_ref[0, :, c : c + step].astype(single) * gact).astype(bfloat)
        sums_ref[pl.ds(j, 1), c : c + step] = column_sum(gh.astype(single))
        acc[...] += dot(gh, ebuf[j, :, c : c + step], 1, 1)
        egrad_ref[0, :, c : c + step] = dot(nt[...], gh, 1, 0).astype(bfloat)
        sgrad_ref[0, c : c + step, :] = dot(act_ref[0, :, c : c + step], low, 0, 0).astype(bfloat)

    @pl.when(j == 1)
    def _():
        gn = acc[...]
        if last:
            unit, factor = norm_parts(x_ref[...])
            sums_ref[2:3] = column_sum(gn * unit)
            sums_ref[3:4] = column_sum(gn)
            h_ref[...] = g_ref[...].astype(single) + norm_back(gn, unit, factor, rows_ref[0:1])
        else:
            part_out[...] = gn


def feed_grads(slots, part, g, x, gain, scale, branch, n, act, slope, weights, deps=()):
    first = 2 if slots == SEND else 0
    weights = (weights[first], weights[first + 1], weights[5 if slots == SEND else 4])
    last = part is not None
    rows, width = n.shape
    hidden = weights[0].shape[1]
    params = jnp.stack([gain, scale])
    unit = (2, width, hidden)
    outs = [((rows, width), single), (unit, bfloat), ((2, hidden, width), bfloat), ((SUMS, width), single)]
    specs = [whole((rows, width)), by_slot(unit), by_slot((2, hidden, width)), whole((SUMS, width))]
    ins = [(whole(v.shape), v) for v in (g, params, branch, n)]
    ins += [(half_specs(v.shape, slots), v) for v in (act, slope)]
    if last:
        ins += [(whole(v.shape), v) for v in (x, part)]
    ins += [(ANY, w) for w in weights]
    return run(
        ins,
        outs,
        specs,
        deps,
        body=functools.partial(feed_grads_kernel, last),
        grid=(2,),
        name="feed_grads",
        scratch_shapes=[
            pltpu.VMEM((2, width, hidden), bfloat),
            pltpu.VMEM((2, hidden, width), bfloat),
            pltpu.VMEM((rows, width), bfloat),
            pltpu.VMEM((width, rows), bfloat),
            pltpu.VMEM((rows, width), single),
            pltpu.SemaphoreType.DMA((2,)),
            pltpu.SemaphoreType.DMA((2,)),
        ],
    )


def attention_kernel(cross, *refs):
    x_ref = refs[0]
    refs = refs[1:]
    if cross:
        latent_ref, seen_ref = refs[:2]
        refs = refs[2:]
    rows_ref, mask_ref = refs[:2]
    weights = refs[2:6]
    mid_ref, branch_ref, qn_ref = refs[6:9]
    refs = refs[9:]
    if cross:
        cn_ref = refs[0]
        refs = refs[1:]
    q_ref, k_ref, v_ref, p_ref, mix_ref, wbuf, acc, wsem = refs
    j = pl.program_id(0)
    start_copies(j, weights, wbuf, wsem)

    @pl.when(j == 0)
    def _():
        x = x_ref[...].astype(single)
        unit, _ = norm_parts(x)
        qn_ref[...] = (unit * rows_ref[0:1] + rows_ref[1:2]).astype(bfloat)
        if cross:
            context = jnp.where(seen_ref[...] > 0, latent_ref[...], x)
            unit, _ = norm_parts(context)
            cn_ref[...] = (unit * rows_ref[4:5] + rows_ref[5:6]).astype(bfloat)
        acc[...] = jnp.zeros_like(acc)

    wait_copy(j, weights, wbuf, wsem)
    qn = qn_ref[...]
    cn = cn_ref[...] if cross else qn
    cols = q_ref.shape[2]
    bias = wbuf[j, 4 * cols : 4 * cols + BIAS_ROWS].astype(single)[0:1]
    bias = bias[:, : 2 * cols] + bias[:, 2 * cols :]
    q = (dot(qn, wbuf[j, :cols], 1, 1) + bias[:, :cols]).astype(bfloat)
    k = dot(cn, wbuf[j, cols : 2 * cols], 1, 1).astype(bfloat)
    v = (dot(cn, wbuf[j, 2 * cols : 3 * cols], 1, 1) + bias[:, cols:]).astype(bfloat)
    q_ref[0] = q
    k_ref[0] = k
    v_ref[0] = v
    images = mask_ref.shape[0]
    patches = mask_ref.shape[2]
    heads = cols // HDIM
    scaled = q * jnp.asarray(HDIM**-0.5, bfloat)
    for i in range(images):
        span = slice(i * patches, (i + 1) * patches)
        mixed = []
        for h in range(heads):
            lanes = slice(h * HDIM, (h + 1) * HDIM)
            scores = dot(scaled[span, lanes], k[span, lanes], 1, 1) + mask_ref[i]
            expo = jnp.exp(scores - jnp.max(scores, axis=-1, keepdims=True))
            probs = (expo * (1.0 / jnp.sum(expo, axis=-1, keepdims=True))).astype(bfloat)
            p_ref[0, i * heads + h] = probs
            mixed.append(dot(probs, v[span, lanes], 1, 0))
        mix_ref[0, span, :] = jnp.concatenate(mixed, axis=1).astype(bfloat)
    acc[...] += dot(mix_ref[0], wbuf[j, 3 * cols : 4 * cols], 1, 0)

    @pl.when(j == SLOTS - 1)
    def _():
        branch = acc[...] + rows_ref[2:3]
        branch_ref[...] = branch.astype(bfloat)
        mid_ref[...] = x_ref[...].astype(single) + rows_ref[3:4] * branch


def attention(x, cross, gains, shifts, outbias, scale, mask, weights, deps=()):
    rows, width = x.shape
    cols = (weights[0].shape[0] - BIAS_ROWS) // 4
    images, _, patches = mask.shape
    heads = cols // HDIM
    params = [gains[0], shifts[0], outbias, scale] + ([gains[1], shifts[1]] if cross else [])
    params = jnp.stack(params)
    extra = list(cross) if cross else []
    outs = [((rows, width), single), ((rows, width), bfloat), ((rows, width), bfloat)]
    outs += [((rows, width), bfloat)] if cross else []
    outs += [((SLOTS, rows, cols), bfloat)] * 3
    outs += [((SLOTS, images * heads, patches, patches), bfloat), ((SLOTS, rows, cols), bfloat)]
    return run(
        [(whole(v.shape), v) for v in (x, *extra, params, mask)] + [(ANY, w) for w in weights],
        outs,
        [whole(s) if len(s) == 2 else by_slot(s) for s, _ in outs],
        deps,
        body=functools.partial(attention_kernel, bool(cross)),
        grid=(SLOTS,),
        name="attention",
        scratch_shapes=[
            pltpu.VMEM((SLOTS,) + weights[0].shape, bfloat),
            pltpu.VMEM((rows, width), single),
            pltpu.SemaphoreType.DMA((SLOTS,)),
        ],
    )


def attention_grads_kernel(cross, last, *refs):
    refs = list(refs)
    take = lambda n: [refs.pop(0) for _ in range(n)]
    h_ref, rows_ref, branch_ref, qn_ref = take(4)
    cn_ref = take(1)[0] if cross else qn_ref
    q_ref, k_ref, v_ref, p_ref, mix_ref = take(5)
    if last:
        x_ref, parta_ref = take(2)
        if cross:
            partb_ref, latent_ref, seen_ref, dlat_ref = take(4)
    weights = take(2)
    outa_refs = take(SLOTS if last else 1)
    outb_ref = take(1)[0] if cross else None
    pack_ref, sums_ref = take(2)
    wbuf, ga, acc_a = take(3)
    acc_b = take(1)[0] if cross else None
    (wsem,) = take(1)
    j = pl.program_id(0)
    start_copies(j, weights, wbuf, wsem)

    @pl.when(j == 0)
    def _():
        h = h_ref[...]
        low = (rows_ref[0:1] * h).astype(bfloat)
        ga[...] = low
        sums_ref[...] = jnp.zeros_like(sums_ref)
        if last:
            sums_ref[2:3] = column_sum(h * branch_ref[...].astype(single))
            sums_ref[3:4] = column_sum(low.astype(single))
            acc_a[...] = parta_ref[...]
            if cross:
                acc_b[...] = partb_ref[...]
        else:
            acc_a[...] = jnp.zeros_like(acc_a)
            if cross:
                acc_b[...] = jnp.zeros_like(acc_b)

    wait_copy(j, weights, wbuf, wsem)
    cols = q_ref.shape[2]
    heads = cols // HDIM
    patches = p_ref.shape[2]
    images = p_ref.shape[1] // heads
    scale = HDIM**-0.5
    low = ga[...]
    gm = dot(low, wbuf[j, 3 * cols : 4 * cols], 1, 1).astype(bfloat)
    parts = []
    for i in range(images):
        span = slice(i * patches, (i + 1) * patches)
        q, k, v = q_ref[0, span], k_ref[0, span], v_ref[0, span]
        gmi = gm[span]
        qt, kt, gmt = q.T, k.T, gmi.T
        gqt, gkt, gvt = [], [], []
        for h in range(heads):
            lanes = slice(h * HDIM, (h + 1) * HDIM)
            low_p = p_ref[0, i * heads + h]
            probs = low_p.astype(single)
            product = probs * dot(gmi[:, lanes], v[:, lanes], 1, 1)
            gs = (product - probs * jnp.sum(product, axis=-1, keepdims=True)).astype(bfloat)
            gqt.append(dot(kt[lanes], gs, 1, 1))
            gkt.append(dot(qt[lanes], gs, 1, 0))
            gvt.append(dot(gmt[lanes], low_p, 1, 0))
        gqt = (jnp.concatenate(gqt, 0) * scale).astype(bfloat)
        gkt = (jnp.concatenate(gkt, 0) * scale).astype(bfloat)
        gvt = jnp.concatenate(gvt, 0).astype(bfloat)
        parts.append((gqt, gkt, gvt))
        a = acc_a[span] + dot(gqt.T, wbuf[j, :cols], 1, 0)
        b = dot(gkt.T, wbuf[j, cols : 2 * cols], 1, 0) + dot(gvt.T, wbuf[j, 2 * cols : 3 * cols], 1, 0)
        if cross:
            acc_a[span] = a
            acc_b[span] += b
        else:
            acc_a[span] = a + b
    gqt, gkt, gvt = (jnp.concatenate([p[n] for p in parts], 1) for n in range(3))
    ones = jnp.ones((8, images * patches), bfloat)
    sums_ref[pl.ds(j, 1), :cols] = dot(ones, gqt, 1, 1)[0:1]
    sums_ref[pl.ds(j, 1), cols : 2 * cols] = dot(ones, gvt, 1, 1)[0:1]
    qn = qn_ref[...]
    cn = cn_ref[...] if cross else qn
    pack_ref[0, 0:cols] = dot(gqt, qn, 1, 0).astype(bfloat)
    pack_ref[0, cols : 2 * cols] = dot(gkt, cn, 1, 0).astype(bfloat)
    pack_ref[0, 2 * cols : 3 * cols] = dot(gvt, cn, 1, 0).astype(bfloat)
    pack_ref[0, 3 * cols :] = dot(mix_ref[0], low, 0, 0).astype(bfloat)

    @pl.when(j == 1)
    def _():
        gn = acc_a[...]
        if not last:
            outa_refs[0][...] = gn
            if cross:
                outb_ref[...] = acc_b[...]
            return
        x = x_ref[...].astype(single)
        unit, factor = norm_parts(x)
        sums_ref[4:5] = column_sum(gn * unit)
        sums_ref[5:6] = column_sum(gn)
        gx = h_ref[...] + norm_back(gn, unit, factor, rows_ref[1:2])
        if cross:
            seen = seen_ref[...] > 0
            unit, factor = norm_parts(jnp.where(seen, latent_ref[...], x))
            gn = acc_b[...]
            sums_ref[6:7] = column_sum(gn * unit)
            sums_ref[7:8] = column_sum(gn)
            flow = norm_back(gn, unit, factor, rows_ref[2:3])
            gx = gx + jnp.where(seen, 0.0, flow)
            outb_ref[...] = dlat_ref[...].astype(single) + jnp.where(seen, flow, 0.0)
        store_blocks(outa_refs, gx)


def attention_grads(slots, parts, h, x, cross, gains, scale, branch, qn, cn, q, k, v, p, mix, weights, blocks, deps=()):
    last = parts is not None
    rows, width = x.shape
    cols = q.shape[2]
    params = jnp.stack([scale, gains[0]] + ([gains[1]] if cross else []))
    pack = (2, 4 * cols, width)
    ins = [(whole(v.shape), v) for v in (h, params, branch, qn) + ((cn,) if cross else ())]
    ins += [(half_specs(e.shape, slots), e) for e in (q, k, v, p, mix)]
    if last:
        ins += [(whole(e.shape), e) for e in (x, *parts, *(cross or ()))]
    ins += [(ANY, weights[r]) for r in slots]
    outs = [(blocks, bfloat)] * SLOTS if last else [((rows, width), single)]
    outs += [((rows, width), single)] if cross else []
    specs = [whole(s) for s, _ in outs] + [by_slot(pack), whole((SUMS, width))]
    outs += [(pack, bfloat), ((SUMS, width), single)]
    accs = [pltpu.VMEM((rows, width), single)] * (2 if cross else 1)
    return run(
        ins,
        outs,
        specs,
        deps,
        body=functools.partial(attention_grads_kernel, bool(cross), last),
        grid=(2,),
        name="attention_grads",
        scratch_shapes=[
            pltpu.VMEM((2,) + weights[0].shape, bfloat),
            pltpu.VMEM((rows, width), bfloat),
            *accs,
            pltpu.SemaphoreType.DMA((2,)),
        ],
    )


def spread_kernel(me_ref, *refs):
    j = pl.program_id(0)
    for r in range(SLOTS):

        @pl.when(j == r)
        def _(r=r):
            refs[SLOTS][0] = refs[r][...].astype(single)


def spread(me, pieces):
    block = pieces[0].shape
    return pl.pallas_call(
        spread_kernel,
        grid_spec=pltpu.PrefetchScalarGridSpec(
            num_scalar_prefetch=1,
            grid=(SLOTS,),
            in_specs=[pl.BlockSpec(block, lambda j, me_ref: (0, 0, 0))] * SLOTS,
            out_specs=pl.BlockSpec((1, *block), lambda j, me_ref: (me_ref[0] ^ j, 0, 0, 0)),
        ),
        out_shape=jax.ShapeDtypeStruct((SLOTS, *block), single),
        name="spread",
    )(me.reshape(1), *pieces)


def pack_kernel(skip, *refs):
    in_ref, out_ref, inbias_ref, expbias_ref, pack_ref = refs[skip:]
    cols = in_ref.shape[2]
    width = in_ref.shape[1]
    for n in range(3):
        pack_ref[n * cols : (n + 1) * cols] = in_ref[n].T
    pack_ref[3 * cols : 4 * cols] = out_ref[...]

    def halves(values):
        high = values.astype(bfloat).astype(single)
        return high, values - high

    lines = [*halves(inbias_ref[...]), *halves(expbias_ref[...])]
    lines = [jnp.concatenate(lines[:2], 1)] + lines[2:] + [jnp.zeros((BIAS_ROWS - 3, width), single)]
    pack_ref[4 * cols :] = jnp.concatenate(lines, 0).astype(bfloat)


def attention_pack(inproj, outproj, inbias, expbias, deps):
    cols, width = outproj.shape
    return pl.pallas_call(
        functools.partial(pack_kernel, len(deps)),
        in_specs=[ANY] * len(deps) + [pl.BlockSpec(memory_space=pltpu.VMEM)] * 4,
        out_shape=jax.ShapeDtypeStruct((4 * cols + BIAS_ROWS, width), bfloat),
        name="pack",
    )(*deps, inproj, outproj, inbias.reshape(1, -1), expbias.reshape(1, -1))


def combine_kernel(counts, sel_ref, *refs):
    terms, outs = list(refs[: sum(map(sum, counts))]), refs[sum(map(sum, counts)) :]
    for out_ref, parts in zip(outs, counts):
        for n, count in enumerate(parts):
            total = terms.pop(0)[...].astype(single)
            for _ in range(count - 1):
                total = total + terms.pop(0)[...].astype(single)
            out_ref[n] = total.astype(bfloat)


def combine(sel, outs):
    def size_of(term):
        return term[0].shape[-2] >> len(term[2])

    sizes = [size_of(parts[0][0]) for parts in outs]
    width = outs[0][0][0][0].shape[-1]
    steps = 2 if all(size % 32 == 0 for size in sizes) else 1
    if any(size % 16 for size in sizes):
        return [jnp.stack([combine_plain(sel, terms) for terms in parts]) for parts in outs]

    def spec_of(term, size):
        array, lead, path = term

        def index(j, sel_ref):
            block = 0
            for entry in path:
                block = block * 2 + sel_ref[entry]
            return (*lead, block * steps + j, 0)

        return pl.BlockSpec((None,) * len(lead) + (size // steps, width), index)

    specs = [spec_of(t, size) for parts, size in zip(outs, sizes) for terms in parts for t in terms]
    arrays = [t[0] for parts in outs for terms in parts for t in terms]
    return pl.pallas_call(
        functools.partial(combine_kernel, [[len(terms) for terms in parts] for parts in outs]),
        grid_spec=pltpu.PrefetchScalarGridSpec(
            num_scalar_prefetch=1,
            grid=(steps,),
            in_specs=specs,
            out_specs=[
                pl.BlockSpec((len(parts), size // steps, width), lambda j, sel_ref: (0, j, 0))
                for parts, size in zip(outs, sizes)
            ],
        ),
        out_shape=[jax.ShapeDtypeStruct((len(parts), size, width), bfloat) for parts, size in zip(outs, sizes)],
        compiler_params=pltpu.CompilerParams(vmem_limit_bytes=GRANT),
        name="combine",
    )(sel, *arrays)


def combine_plain(sel, terms):
    values = []
    for array, lead, path in terms:
        array = array[lead]
        for entry in path:
            array = part_at(array, sel[entry], 2)
        values.append(array)
    return add_low(*values)


def place_kernel(count, split, mine_ref, *refs):
    j = pl.program_id(0)
    for hop in range(count):

        @pl.when(j == hop)
        def _(hop=hop):
            if split:
                for n, out_ref in enumerate(refs[count:]):
                    out_ref[...] = refs[hop][n].astype(out_ref.dtype)
            else:
                refs[count][...] = refs[hop][...]


def place(mine, pieces, split=False):
    count = len(pieces)
    n, size, width = pieces[0].shape
    if size % 16:
        whole_array = jnp.zeros((n, count * size, width), pieces[0].dtype)
        for hop, piece in enumerate(pieces):
            whole_array = lax.dynamic_update_slice_in_dim(whole_array, piece, (mine ^ hop) * size, 1)
        return [w.astype(single) for w in whole_array] if split else whole_array
    if split:
        outs = [jax.ShapeDtypeStruct((count * size, width), single)] * n
        specs = [pl.BlockSpec((size, width), lambda j, mine_ref: (mine_ref[0] ^ j, 0))] * n
    else:
        outs = [jax.ShapeDtypeStruct((n, count * size, width), pieces[0].dtype)]
        specs = [pl.BlockSpec((n, size, width), lambda j, mine_ref: (0, mine_ref[0] ^ j, 0))]
    result = pl.pallas_call(
        functools.partial(place_kernel, count, split),
        grid_spec=pltpu.PrefetchScalarGridSpec(
            num_scalar_prefetch=1,
            grid=(count,),
            in_specs=[pl.BlockSpec(p.shape, lambda j, mine_ref: (0, 0, 0)) for p in pieces],
            out_specs=specs,
        ),
        out_shape=outs,
        compiler_params=pltpu.CompilerParams(vmem_limit_bytes=GRANT),
        name="place",
    )(mine.reshape(1), *pieces)
    return result if split else result[0]


def swap(values, axis, count, bit):
    return lax.ppermute(values, axis, [(i, i ^ bit) for i in range(count)])


def near_core(values):
    return swap(values, "tensor", SLOTS, 1)


def over_chip(values):
    return swap(values, "tensor", SLOTS, 2)


def part_at(values, index, parts, axis=0):
    size = values.shape[axis] // parts
    return lax.dynamic_slice_in_dim(values, index * size, size, axis)


def add_low(*terms):
    total = terms[0].astype(single)
    for term in terms[1:]:
        total = total + term.astype(single)
    return total.astype(bfloat)


def tie(*values):
    return lax.optimization_barrier(values)


def gather_stages(count):
    stages, stride = [], 1
    while stride < count:
        radix = 2 if stride == 1 else min(4, count // stride)
        stages.append((radix, stride))
        stride *= radix
    return stages


def gather_piece(count):
    place, piece = lax.axis_index("dp"), 0
    for radix, stride in gather_stages(count):
        piece = piece * radix + (place // stride) % radix
    return piece


def gather_send(values, count, stage):
    radix, stride = gather_stages(count)[stage]
    return [values] + [swap(values, "dp", count, hop * stride) for hop in range(1, radix)]


def gather_join(pieces, count, stage):
    radix, stride = gather_stages(count)[stage]
    return place((lax.axis_index("dp") // stride) % radix, pieces)


class Unit:
    def __init__(self, count, sends, orders):
        self.count, self.orders = count, orders
        self.near = [near_core(send) for send in sends]
        self.pending = self.near
        self.strides = []
        stride = 1
        while stride < count:
            self.strides.append(stride)
            stride *= 2
        place_now = lax.axis_index("dp")
        self.bits = [(place_now // stride) % 2 for stride in self.strides]
        self.sel = jnp.stack([b ^ flip for b in self.bits for flip in (0, 1)]).astype(jnp.int32)
        self.stage = 0
        self.steps = 3 + 2 * (len(self.strides) - 1)

    def hop(self, values, n):
        return swap(values, "dp", self.count, self.strides[n])

    def kept(self):
        return (self.near, getattr(self, "first", None), getattr(self, "value", None))[min(self.stage - 1, 2)]

    def keep_tied(self, kept):
        setattr(self, ("near", "first", "value")[min(self.stage - 1, 2)], kept)

    def follow(self, previous):
        self.pending, kept = lax.optimization_barrier((self.pending, previous.kept()))
        previous.keep_tied(kept)

    def base(self, n, slot, path):
        return [(self.keep[n], (slot,), path), (self.near[n], (slot,), path)]

    def step(self):
        pending = self.pending
        stage, last = self.stage, len(self.strides) - 1
        self.stage += 1
        count = len(self.orders)
        if stage == 0:
            self.near = pending
            outs = [
                [self.base(n, 1, ())] if across else [self.base(n, s, (1,)) for s in (0, 1)]
                for n, across in enumerate(self.orders)
            ]
            sent = combine(self.sel, outs)
            self.pending = [over_chip(v) if across else self.hop(v, 0) for v, across in zip(sent, self.orders)]
        elif stage == 1:
            self.first = pending
            outs = [
                [self.base(n, 0, (1,)) + [(pending[n], (0,), (1,))]]
                if across
                else [self.base(n, 1, (0,)) + [(pending[n], (1,), ())]]
                for n, across in enumerate(self.orders)
            ]
            sent = combine(self.sel, outs)
            self.pending = [self.hop(v, 0) if across else over_chip(v) for v, across in zip(sent, self.orders)]
        elif stage == 2:

            def terms(n, tail):
                first = (0,) + tail if self.orders[n] else tail
                return self.base(n, 0, (0,) + tail) + [(self.first[n], (0,), first), (pending[n], (0,), tail)]

            value, sent = combine(self.sel, [[terms(n, (flip + 2,)) for n in range(count)] for flip in (0, 1)])
            self.value, sent = [value], [sent]
            self.pending = [self.hop(sent[0], 1)]
        elif stage < 2 + last:
            n = stage - 1
            value, sent = combine(
                self.sel,
                [
                    [[(v, (m,), (2 * n + flip,)) for v in (self.value[0], pending[0])] for m in range(count)]
                    for flip in (0, 1)
                ],
            )
            self.value, sent = [value], [sent]
            self.pending = [self.hop(sent[0], n)]
        elif stage == 2 + last:
            self.value = sent = combine(
                self.sel, [[[(v, (m,), ()) for v in (self.value[0], pending[0])] for m in range(count)]]
            )
            self.pending = [self.hop(sent[0], last)]
        else:
            n = last - (stage - 3 - last)
            self.value = sent = [place(self.bits[n], [self.value[0], pending[0]])]
            self.pending = [self.hop(sent[0], n - 1)]
        return sent

    def result(self):
        return place(self.bits[0], [self.value[0], self.pending[0]], True)


def steps_after(done, units):
    sent = []
    for n, u in enumerate(units):
        if n:
            u.follow(units[n - 1])
        else:
            u.pending, done = lax.optimization_barrier((u.pending, done))
        sent += u.step()
    return done, sent


TAIL = (
    "ea", "ef", "rf", "ra", "ef", "rf", "ra", "ea", "rf", "ef", "ra", "ea", "ef", "ra", "ea", "ef", "ra", "ea", "ef",
    "ea", "ef", "ea",
)


def make_local(count):
    def local(
        patches, mask_queries, visible, lengths, d_latent, d_regress,
        e_gain, e_shift, e_scale, e_inproj, e_inbias, e_outproj, e_outbias, e_expand, e_expbias, e_shrink,
        r_gain, r_shift, r_scale, r_inproj, r_inbias, r_outproj, r_outbias, r_expand, r_expbias, r_shrink,
    ):
        micro, images, part, width = patches.shape
        patch_count = visible.shape[2]
        rows = images * patch_count
        cols = e_inbias.shape[1]
        hidden = e_expbias.shape[0]
        block_shape = (images, part, width)
        me = lax.axis_index("tensor")

        def pieces_of(*arrays):
            taken = []
            for r in range(SLOTS):
                one = [lax.dynamic_index_in_dim(a, me ^ r, 0, keepdims=False).astype(bfloat) for a in arrays]
                taken.append(jnp.stack(one) if len(one) > 1 else one[0])
            return taken

        def exchange(pieces):
            return [swap(p, "tensor", SLOTS, r) if r else p for r, p in enumerate(pieces)]

        def join(pieces):
            return jnp.stack(pieces, 1).reshape(rows, width)

        pieces = pieces_of(patches)
        tokens_sent = exchange(pieces)
        piece = gather_piece(count)
        stages = len(gather_stages(count))

        def feed_piece(expand, shrink):
            return jnp.stack([part_at(expand, piece, count), part_at(shrink, piece, count)])

        def gather_to_last(sent):
            for stage in range(stages - 1, 0, -1):
                joined = gather_join(sent, count, stage)
                sent = gather_send(joined, count, stage - 1)
            return joined, sent

        e_piece, r_piece = feed_piece(e_expand, e_shrink), feed_piece(r_expand, r_shrink)
        e_slice = over_chip(e_piece)
        e_pack = attention_pack(e_inproj, e_outproj, e_inbias, e_expbias, [*pieces[1:], e_piece])
        e_pack_t, r_piece, *tokens_sent = tie(e_pack, r_piece, *tokens_sent)
        e_pack1, e_pack2 = near_core(e_pack_t), over_chip(e_pack_t)
        r_slice = over_chip(r_piece)
        e_gathered, e_half = gather_to_last(gather_send(e_slice, count, stages - 1))
        r_slice, e_gathered = tie(r_slice, e_gathered)

        tensor_order = jnp.stack([me ^ r for r in range(SLOTS)])
        position = (tensor_order[:, None] * part + jnp.arange(part)[None, :]).reshape(-1)
        my_lengths = lax.dynamic_index_in_dim(lengths, me, 0, keepdims=False)
        my_visible = lax.dynamic_index_in_dim(visible, me, 0, keepdims=False)
        my_visible = jnp.concatenate([part_at(my_visible, me ^ r, SLOTS, 1) for r in range(SLOTS)], 1)
        valid = position[None, :] < my_lengths[:, None]
        seen = (my_visible == 1) | (position[None, :] == 0)
        seen_rows = seen.reshape(rows, 1).astype(single)
        e_mask = jnp.where(valid & seen, 0.0, -1e30).astype(single)[:, None, :]
        r_mask = jnp.where(valid, 0.0, -1e30).astype(single)[:, None, :]

        tokens = join(tokens_sent)
        r_pack = attention_pack(r_inproj, r_outproj, r_inbias, r_expbias, [e_pack])
        q_pieces = pieces_of(mask_queries)
        g_pieces = pieces_of(d_regress, d_latent)
        e_pack2, e_gathered, r_pack_t = tie(e_pack2, e_gathered, r_pack)
        e_pack3 = near_core(e_pack2)
        r_pack2 = over_chip(r_pack_t)
        e_packs = [e_pack, e_pack1, e_pack2, e_pack3]
        e_mid, e_ba, n0, q0, k0, v0, p0, mix0 = attention(
            tokens, None, e_gain, e_shift, e_outbias[0], e_scale[0], e_mask, e_packs,
            [e_gathered, r_pack, *q_pieces, *g_pieces],
        )

        e_mid, e_half[1], e_exp_t, e_shr_t, r_pack1_t, r_slice, *q_pieces = tie(
            e_mid, e_half[1], e_expand, e_shrink, r_pack, r_slice, *q_pieces
        )
        r_pack1 = near_core(r_pack1_t)
        r_sent = gather_send(r_slice, count, stages - 1)
        e_feed2 = gather_join(e_half, count, 0)
        e_feed3 = near_core(e_feed2)
        e_exp1, e_shr1 = near_core(e_exp_t), near_core(e_shr_t)
        queries_sent = exchange(q_pieces)
        e_feeds = [e_expand, e_shrink, e_exp1, e_shr1, e_feed2, e_feed3]
        latent, *latent_low, e_bf, n1, e_act, e_slope = feed_forward(
            e_mid, e_gain[1], e_shift[1], e_outbias[1], e_scale[1], e_feeds, e_packs, block_shape, True,
            [r_slice, r_pack1],
        )

        hops = len(r_sent)
        latent, r_pack2, *rest = tie(latent, r_pack2, *r_sent, *g_pieces)
        r_gathered, r_half = gather_to_last(rest[:hops])
        g_pieces = rest[hops:]
        r_pack3 = near_core(r_pack2)
        queries = join(queries_sent)
        r_packs = [r_pack, r_pack1, r_pack2, r_pack3]
        r_mid, r_ba, qn, cn, q1, k1, v1, p1, mix1 = attention(
            queries, (latent, seen_rows), r_gain, r_shift, r_outbias[0], r_scale[0], r_mask, r_packs, [r_gathered]
        )

        g_sent = exchange(g_pieces)
        latent_sent = exchange(latent_low)
        r_mid, r_half[1], r_exp_t, r_shr_t = tie(r_mid, r_half[1], r_expand, r_shrink)
        r_feed2 = gather_join(r_half, count, 0)
        r_feed3 = near_core(r_feed2)
        r_exp1, r_shr1 = near_core(r_exp_t), near_core(r_shr_t)
        r_feeds = [r_expand, r_shrink, r_exp1, r_shr1, r_feed2, r_feed3]
        *regressed_low, r_bf, n2, r_act, r_slope = feed_forward(
            r_mid, r_gain[2], r_shift[2], r_outbias[1], r_scale[1], r_feeds, r_packs, block_shape, False
        )

        n2, *g_sent = tie(n2, *g_sent)
        g_regress = join([g[0] for g in g_sent])
        g_latent = join([g[1] for g in g_sent])
        regressed_sent = exchange(regressed_low)

        def feed_back(orders, g, x, gain, scale, branch, n, act, slope, feed, deps):
            part_sum, send_e, send_s, sums_send = feed_grads(
                SEND, None, g, x, gain, scale, branch, n, act, slope, feed, deps
            )
            unit = Unit(count, [send_e, send_s], orders)
            h, keep_e, keep_s, sums_keep = feed_grads(KEEP, part_sum, g, x, gain, scale, branch, n, act, slope, feed)
            unit.keep = [keep_e, keep_s]
            return h, unit, (sums_send, sums_keep)

        h, rf, sums_rf = feed_back(
            (True, False), g_regress, r_mid, r_gain[2], r_scale[1], r_bf, n2, r_act, r_slope, r_feeds, []
        )
        h, sent = steps_after(h, [rf])
        args = (h, queries, (latent, seen_rows, g_latent), r_gain, r_scale[0], r_ba, qn, cn, q1, k1, v1, p1, mix1, r_packs, block_shape)
        part_a, part_b, send, sums_send = attention_grads(SEND, None, *args, sent)
        ra = Unit(count, [send], (True,))
        *gq_low, g, keep, sums_keep = attention_grads(
            KEEP, (part_a, part_b), *args, [*latent_sent[1:], *regressed_sent[1:]]
        )
        ra.keep, sums_ra = [keep], (sums_send, sums_keep)

        g, sent = steps_after(g, [ra, rf])
        gq_sent = exchange(gq_low)
        h, ef, sums_ef = feed_back(
            (False, True), g, e_mid, e_gain[1], e_scale[1], e_bf, n1, e_act, e_slope, e_feeds, sent
        )
        h, sent = steps_after(h, [rf, ef])
        args = (h, tokens, None, e_gain, e_scale[0], e_ba, n0, None, q0, k0, v0, p0, mix0, e_packs, block_shape)
        part_a, send, sums_send = attention_grads(SEND, None, *args, sent)
        ea = Unit(count, [send], (False,))
        part_a, sent = steps_after(part_a, [rf, ra])
        *gp_low, keep, sums_keep = attention_grads(KEEP, (part_a,), *args, [*sent, *gq_sent[1:]])
        ea.keep, sums_ea = [keep], (sums_send, sums_keep)

        pairs = (sums_ef, sums_ea, sums_rf, sums_ra)
        small = jnp.stack([p[n] for n in (1, 0) for p in pairs])
        near = near_core(small)
        line = lax.broadcasted_iota(jnp.int32, (1, SUMS, 1), 1)
        totals = small[:4] + jnp.where(line < 2, near[4:], near[:4])
        far = over_chip(totals)
        totals = totals + jnp.where(line == 0, far[:, 1:2], far)
        for n in range(count.bit_length() - 1):
            totals = totals + swap(totals, "dp", count, 2**n)

        units = dict(ea=ea, rf=rf, ra=ra, ef=ef)
        sequence = [units[name] for name in TAIL]
        previous, turn = None, 0
        while any(u.stage < u.steps for u in units.values()):
            u = sequence.pop(0) if sequence else next(u for u in units.values() if u.stage < u.steps)
            if u.stage == u.steps:
                continue
            if previous is not None and previous is not u:
                u.follow(previous)
            u.step()
            previous = u
            turn += 1
            if turn == 9:
                kept, *late = tie(u.kept()[0], *latent_sent, *regressed_sent, *gq_sent)
                u.keep_tied([kept])
                latent_sent, regressed_sent, gq_sent = (late[n * SLOTS : (n + 1) * SLOTS] for n in range(3))
        gp_sent = exchange(gp_low)
        out_latent, out_regressed, out_queries, out_patches = (
            spread(me, sent) for sent in (latent_sent, regressed_sent, gq_sent, gp_sent)
        )
        (rf_e, rf_s), (ra,), (ef_e, ef_s), (ea,) = (u.result() for u in (rf, ra, ef, ea))
        e_f, e_a, r_f, r_a = totals
        e_inb_g = e_a[0, : 2 * cols].reshape(2, cols)
        r_inb_g = r_a[0, : 2 * cols].reshape(2, cols)
        e_exb_g, r_exb_g = e_f[0], r_f[0]

        def attention_outputs(shard):
            return shard[: 3 * cols].reshape(3, cols, width).transpose(0, 2, 1), shard[3 * cols :]

        e_in_g, e_out_g = attention_outputs(ea)
        r_in_g, r_out_g = attention_outputs(ra)
        return (
            out_latent, out_regressed, out_patches, out_queries,
            jnp.stack([e_a[4], e_f[2]]), jnp.stack([e_a[5], e_f[3]]), jnp.stack([e_a[2], e_f[4]]),
            e_in_g, e_inb_g, e_out_g, jnp.stack([e_a[3], e_f[5]]), ef_e, e_exb_g, ef_s,
            jnp.stack([r_a[4], r_a[6], r_f[2]]), jnp.stack([r_a[5], r_a[7], r_f[3]]), jnp.stack([r_a[2], r_f[4]]),
            r_in_g, r_inb_g, r_out_g, jnp.stack([r_a[3], r_f[5]]), rf_e, r_exb_g, rf_s,
        )

    return local


def solution(mesh):
    assert mesh.shape["tensor"] == SLOTS
    rows = P(None, "dp", "tensor", None)

    def block():
        return (
            P(), P(), P(), P(None, None, "tensor"), P(None, "tensor"), P("tensor", None), P(),
            P(None, "tensor"), P("tensor"), P("tensor", None),
        )

    return jax.shard_map(
        make_local(mesh.shape["dp"]),
        mesh=mesh,
        in_specs=(rows, rows, P(None, "dp", None), P(None, "dp"), rows, rows, *block(), *block()),
        out_specs=(rows, rows, rows, rows, *block(), *block()),
        check_vma=False,
    )
```

```python
import functools
import jax
import jax.numpy as jnp
from jax import lax
from jax.experimental import pallas as pl
from jax.experimental.pallas import tpu as pltpu
from jax.sharding import PartitionSpec as P

HDIM = 64
epsilon = 1e-06
bfloat = jnp.bfloat16
single = jnp.float32
SLOTS = 4
GRANT = 24 * 2**20


def dot(a, b, ca, cb):
    return lax.dot_general(a, b, (((ca,), (cb,)), ((), ())), preferred_element_type=single)


def norm_parts(values):
    average = jnp.mean(values, axis=-1, keepdims=True)
    centred = values - average
    variance = jnp.mean(centred * centred, axis=-1, keepdims=True)
    factor = lax.rsqrt(variance + epsilon)
    return centred * factor, factor


def norm_back(gradient, unit, factor, gain_row):
    scaled = gradient * gain_row
    return factor * (
        scaled
        - jnp.mean(scaled, axis=-1, keepdims=True)
        - unit * jnp.mean(scaled * unit, axis=-1, keepdims=True)
    )


def column_sum(values):
    return jnp.sum(values, axis=0, keepdims=True)


def gelu_parts(hidden):
    size = jnp.abs(hidden)
    bell = jnp.exp(-0.5 * hidden * hidden)
    t = 1.0 / (1.0 + (0.3275911 * 0.5**0.5) * size)
    poly = t * (0.127414796 + t * (-0.142248368 + t * (0.7107068705 + t * (-0.7265760135 + t * 0.5307027145))))
    tail = poly * bell
    below = jnp.where(hidden < 0, tail, 1.0 - tail)
    return hidden * below, below + hidden * bell * 0.3989422804


def start_copies(step, sources, buffer, sems):
    @pl.when(step == 0)
    def _():
        for r, source in enumerate(sources):
            pltpu.make_async_copy(source, buffer.at[r], sems.at[r]).start()


def wait_copy(step, sources, buffer, sems):
    for r, source in enumerate(sources):

        @pl.when(step == r)
        def _(r=r, source=source):
            pltpu.make_async_copy(source, buffer.at[r], sems.at[r]).wait()


def whole(shape):
    zeros = (0,) * len(shape)
    return pl.BlockSpec(shape, lambda j: zeros, pipeline_mode=pl.Buffered(1))


def by_slot(shape):
    zeros = (0,) * (len(shape) - 1)
    return pl.BlockSpec((1,) + shape[1:], lambda j: (j,) + zeros)


ANY = pl.BlockSpec(memory_space=pl.ANY)
SEND, KEEP = (1, 3), (0, 2)
BIAS_ROWS = 16
SUMS = 8


def store_blocks(low_ref, values):
    blocks, images, part = low_ref.shape[:3]
    for r in range(blocks):
        for i in range(images):
            start = (i * blocks + r) * part
            low_ref[r, i] = values[start : start + part].astype(bfloat)


def run(call_inputs, outs, specs, deps, body, **kwargs):
    skip = len(deps)
    return pl.pallas_call(
        lambda *refs: body(*refs[skip:]),
        in_specs=[ANY] * skip + [s for s, _ in call_inputs],
        out_specs=specs,
        out_shape=[jax.ShapeDtypeStruct(s, d) for s, d in outs],
        compiler_params=pltpu.CompilerParams(vmem_limit_bytes=GRANT),
        cost_estimate=pl.CostEstimate(flops=20 * 10**9, bytes_accessed=2**26, transcendentals=0),
        **kwargs,
    )(*deps, *[v for _, v in call_inputs])


def feed_sources(refs):
    near, far = refs[:4], refs[4:]
    return [near[0], near[2], *(f.at[0] for f in far)], [near[1], near[3], *(f.at[1] for f in far)]


def feed_forward_kernel(wide, *refs):
    x_ref, rows_ref = refs[:2]
    expand, shrink = feed_sources(refs[2:8])
    biases = refs[8:12]
    outs = refs[12 : 17 + wide]
    out_ref = outs[0] if wide else None
    low_ref, branch_ref, n_ref, act_ref, slope_ref = outs[wide:]
    ebuf, sbuf, bbuf, acc, esem, ssem, bsem = refs[17 + wide :]
    j = pl.program_id(0)
    width = x_ref.shape[1]
    tops = [b.at[pl.ds(width, BIAS_ROWS)] for b in biases]
    start_copies(j, tops, bbuf, bsem)
    start_copies(j, expand, ebuf, esem)
    start_copies(j, shrink, sbuf, ssem)

    @pl.when(j == 0)
    def _():
        unit, _ = norm_parts(x_ref[...])
        n_ref[...] = (unit * rows_ref[0:1] + rows_ref[1:2]).astype(bfloat)
        acc[...] = jnp.zeros_like(acc)

    wait_copy(j, tops, bbuf, bsem)
    wait_copy(j, expand, ebuf, esem)
    bias = bbuf[j].astype(single)
    bias = bias[1:2] + bias[2:3]
    hidden_width = ebuf.shape[2]
    step = 256
    n = n_ref[...]
    for c in range(0, hidden_width, step):
        hidden = dot(n, ebuf[j, :, c : c + step], 1, 0) + bias[:, c : c + step]
        act, slope = gelu_parts(hidden)
        act_ref[0, :, c : c + step] = act.astype(bfloat)
        slope_ref[0, :, c : c + step] = slope.astype(bfloat)
    wait_copy(j, shrink, sbuf, ssem)
    acc[...] += dot(act_ref[0], sbuf[j], 1, 0)

    @pl.when(j == SLOTS - 1)
    def _():
        branch = acc[...] + rows_ref[2:3]
        branch_ref[...] = branch.astype(bfloat)
        out = x_ref[...] + rows_ref[3:4] * branch
        if wide:
            out_ref[...] = out
        store_blocks(low_ref, out)


def feed_forward(x, gain, shift, outbias, scale, weights, biases, blocks, wide, deps=()):
    rows, width = x.shape
    hidden = weights[0].shape[1]
    params = jnp.stack([gain, shift, outbias, scale])
    outs = [((rows, width), single)] if wide else []
    outs += [(blocks, bfloat)] + [((rows, width), bfloat)] * 2 + [((SLOTS, rows, hidden), bfloat)] * 2
    specs = [whole(s) for s, _ in outs[:-2]] + [by_slot(s) for s, _ in outs[-2:]]
    return run(
        [(whole(x.shape), x), (whole(params.shape), params)] + [(ANY, w) for w in (*weights, *biases)],
        outs,
        specs,
        deps,
        body=functools.partial(feed_forward_kernel, wide),
        grid=(SLOTS,),
        name="feed_forward",
        scratch_shapes=[
            pltpu.VMEM((SLOTS, width, hidden), bfloat),
            pltpu.VMEM((SLOTS, hidden, width), bfloat),
            pltpu.VMEM((SLOTS, BIAS_ROWS, width), bfloat),
            pltpu.VMEM((rows, width), single),
            pltpu.SemaphoreType.DMA((SLOTS,)),
            pltpu.SemaphoreType.DMA((SLOTS,)),
            pltpu.SemaphoreType.DMA((SLOTS,)),
        ],
    )


def half_specs(shape, slots):
    zeros = (0,) * (len(shape) - 1)
    first, step = slots[0], slots[1] - slots[0]
    return pl.BlockSpec((1,) + shape[1:], lambda j: (first + step * j,) + zeros)


def feed_grads_kernel(last, *refs):
    g_ref, rows_ref, branch_ref, n_ref, act_ref, slope_ref = refs[:6]
    refs = refs[6:]
    if last:
        x_ref, part_ref = refs[:2]
        refs = refs[2:]
    expand, shrink = (refs[0], refs[2].at[0]), (refs[1], refs[2].at[1])
    h_ref, egrad_ref, sgrad_ref, sums_ref = refs[3:7]
    part_out = h_ref
    refs = refs[7:]
    ebuf, sbuf, gb, nt, acc, esem, ssem = refs
    j = pl.program_id(0)
    start_copies(j, shrink, sbuf, ssem)
    start_copies(j, expand, ebuf, esem)

    @pl.when(j == 0)
    def _():
        g = g_ref[...].astype(single)
        low = (rows_ref[1:2] * g).astype(bfloat)
        gb[...] = low
        nt[...] = n_ref[...].T
        sums_ref[...] = jnp.zeros_like(sums_ref)
        if last:
            sums_ref[4:5] = column_sum(g * branch_ref[...].astype(single))
            sums_ref[5:6] = column_sum(low.astype(single))
            acc[...] = part_ref[...]
        else:
            acc[...] = jnp.zeros_like(acc)

    wait_copy(j, shrink, sbuf, ssem)
    wait_copy(j, expand, ebuf, esem)
    width, hidden = ebuf.shape[1], ebuf.shape[2]
    step = 256
    low = gb[...]
    for c in range(0, hidden, step):
        gact = dot(low, sbuf[j, c : c + step, :], 1, 1)
        gh = (slope_ref[0, :, c : c + step].astype(single) * gact).astype(bfloat)
        sums_ref[pl.ds(j, 1), c : c + step] = column_sum(gh.astype(single))
        acc[...] += dot(gh, ebuf[j, :, c : c + step], 1, 1)
        egrad_ref[0, :, c : c + step] = dot(nt[...], gh, 1, 0).astype(bfloat)
        sgrad_ref[0, c : c + step, :] = dot(act_ref[0, :, c : c + step], low, 0, 0).astype(bfloat)

    @pl.when(j == 1)
    def _():
        gn = acc[...]
        if last:
            unit, factor = norm_parts(x_ref[...])
            sums_ref[2:3] = column_sum(gn * unit)
            sums_ref[3:4] = column_sum(gn)
            h_ref[...] = g_ref[...].astype(single) + norm_back(gn, unit, factor, rows_ref[0:1])
        else:
            part_out[...] = gn


def feed_grads(slots, part, g, x, gain, scale, branch, n, act, slope, weights, deps=()):
    first = 2 if slots == SEND else 0
    weights = (weights[first], weights[first + 1], weights[5 if slots == SEND else 4])
    last = part is not None
    rows, width = n.shape
    hidden = weights[0].shape[1]
    params = jnp.stack([gain, scale])
    unit = (2, width, hidden)
    outs = [((rows, width), single), (unit, bfloat), ((2, hidden, width), bfloat), ((SUMS, width), single)]
    specs = [whole((rows, width)), by_slot(unit), by_slot((2, hidden, width)), whole((SUMS, width))]
    ins = [(whole(v.shape), v) for v in (g, params, branch, n)]
    ins += [(half_specs(v.shape, slots), v) for v in (act, slope)]
    if last:
        ins += [(whole(v.shape), v) for v in (x, part)]
    ins += [(ANY, w) for w in weights]
    return run(
        ins,
        outs,
        specs,
        deps,
        body=functools.partial(feed_grads_kernel, last),
        grid=(2,),
        name="feed_grads",
        scratch_shapes=[
            pltpu.VMEM((2, width, hidden), bfloat),
            pltpu.VMEM((2, hidden, width), bfloat),
            pltpu.VMEM((rows, width), bfloat),
            pltpu.VMEM((width, rows), bfloat),
            pltpu.VMEM((rows, width), single),
            pltpu.SemaphoreType.DMA((2,)),
            pltpu.SemaphoreType.DMA((2,)),
        ],
    )


def attention_kernel(cross, *refs):
    x_ref = refs[0]
    refs = refs[1:]
    if cross:
        latent_ref, seen_ref = refs[:2]
        refs = refs[2:]
    rows_ref, mask_ref = refs[:2]
    weights = refs[2:6]
    mid_ref, branch_ref, qn_ref = refs[6:9]
    refs = refs[9:]
    if cross:
        cn_ref = refs[0]
        refs = refs[1:]
    q_ref, k_ref, v_ref, p_ref, mix_ref, wbuf, acc, wsem = refs
    j = pl.program_id(0)
    start_copies(j, weights, wbuf, wsem)

    @pl.when(j == 0)
    def _():
        x = x_ref[...].astype(single)
        unit, _ = norm_parts(x)
        qn_ref[...] = (unit * rows_ref[0:1] + rows_ref[1:2]).astype(bfloat)
        if cross:
            context = jnp.where(seen_ref[...] > 0, latent_ref[...], x)
            unit, _ = norm_parts(context)
            cn_ref[...] = (unit * rows_ref[4:5] + rows_ref[5:6]).astype(bfloat)
        acc[...] = jnp.zeros_like(acc)

    wait_copy(j, weights, wbuf, wsem)
    qn = qn_ref[...]
    cn = cn_ref[...] if cross else qn
    cols = q_ref.shape[2]
    bias = wbuf[j, 4 * cols : 4 * cols + BIAS_ROWS].astype(single)[0:1]
    bias = bias[:, : 2 * cols] + bias[:, 2 * cols :]
    q = (dot(qn, wbuf[j, :cols], 1, 1) + bias[:, :cols]).astype(bfloat)
    k = dot(cn, wbuf[j, cols : 2 * cols], 1, 1).astype(bfloat)
    v = (dot(cn, wbuf[j, 2 * cols : 3 * cols], 1, 1) + bias[:, cols:]).astype(bfloat)
    q_ref[0] = q
    k_ref[0] = k
    v_ref[0] = v
    images = mask_ref.shape[0]
    patches = mask_ref.shape[2]
    heads = cols // HDIM
    scaled = q * jnp.asarray(HDIM**-0.5, bfloat)
    for i in range(images):
        span = slice(i * patches, (i + 1) * patches)
        mixed = []
        for h in range(heads):
            lanes = slice(h * HDIM, (h + 1) * HDIM)
            scores = dot(scaled[span, lanes], k[span, lanes], 1, 1) + mask_ref[i]
            expo = jnp.exp(scores - jnp.max(scores, axis=-1, keepdims=True))
            probs = (expo * (1.0 / jnp.sum(expo, axis=-1, keepdims=True))).astype(bfloat)
            p_ref[0, i * heads + h] = probs
            mixed.append(dot(probs, v[span, lanes], 1, 0))
        mix_ref[0, span, :] = jnp.concatenate(mixed, axis=1).astype(bfloat)
    acc[...] += dot(mix_ref[0], wbuf[j, 3 * cols : 4 * cols], 1, 0)

    @pl.when(j == SLOTS - 1)
    def _():
        branch = acc[...] + rows_ref[2:3]
        branch_ref[...] = branch.astype(bfloat)
        mid_ref[...] = x_ref[...].astype(single) + rows_ref[3:4] * branch


def attention(x, cross, gains, shifts, outbias, scale, mask, weights, deps=()):
    rows, width = x.shape
    cols = (weights[0].shape[0] - BIAS_ROWS) // 4
    images, _, patches = mask.shape
    heads = cols // HDIM
    params = [gains[0], shifts[0], outbias, scale] + ([gains[1], shifts[1]] if cross else [])
    params = jnp.stack(params)
    extra = list(cross) if cross else []
    outs = [((rows, width), single), ((rows, width), bfloat), ((rows, width), bfloat)]
    outs += [((rows, width), bfloat)] if cross else []
    outs += [((SLOTS, rows, cols), bfloat)] * 3
    outs += [((SLOTS, images * heads, patches, patches), bfloat), ((SLOTS, rows, cols), bfloat)]
    return run(
        [(whole(v.shape), v) for v in (x, *extra, params, mask)] + [(ANY, w) for w in weights],
        outs,
        [whole(s) if len(s) == 2 else by_slot(s) for s, _ in outs],
        deps,
        body=functools.partial(attention_kernel, bool(cross)),
        grid=(SLOTS,),
        name="attention",
        scratch_shapes=[
            pltpu.VMEM((SLOTS,) + weights[0].shape, bfloat),
            pltpu.VMEM((rows, width), single),
            pltpu.SemaphoreType.DMA((SLOTS,)),
        ],
    )


def attention_grads_kernel(cross, last, *refs):
    refs = list(refs)
    take = lambda n: [refs.pop(0) for _ in range(n)]
    h_ref, rows_ref, branch_ref, qn_ref = take(4)
    cn_ref = take(1)[0] if cross else qn_ref
    q_ref, k_ref, v_ref, p_ref, mix_ref = take(5)
    if last:
        x_ref, parta_ref = take(2)
        if cross:
            partb_ref, latent_ref, seen_ref, dlat_ref = take(4)
    weights = take(2)
    outa_ref = take(1)[0]
    outb_ref = take(1)[0] if cross else None
    pack_ref, sums_ref = take(2)
    wbuf, ga, acc_a = take(3)
    acc_b = take(1)[0] if cross else None
    (wsem,) = take(1)
    j = pl.program_id(0)
    start_copies(j, weights, wbuf, wsem)

    @pl.when(j == 0)
    def _():
        h = h_ref[...]
        low = (rows_ref[0:1] * h).astype(bfloat)
        ga[...] = low
        sums_ref[...] = jnp.zeros_like(sums_ref)
        if last:
            sums_ref[2:3] = column_sum(h * branch_ref[...].astype(single))
            sums_ref[3:4] = column_sum(low.astype(single))
            acc_a[...] = parta_ref[...]
            if cross:
                acc_b[...] = partb_ref[...]
        else:
            acc_a[...] = jnp.zeros_like(acc_a)
            if cross:
                acc_b[...] = jnp.zeros_like(acc_b)

    wait_copy(j, weights, wbuf, wsem)
    cols = q_ref.shape[2]
    heads = cols // HDIM
    patches = p_ref.shape[2]
    images = p_ref.shape[1] // heads
    scale = HDIM**-0.5
    low = ga[...]
    gm = dot(low, wbuf[j, 3 * cols : 4 * cols], 1, 1).astype(bfloat)
    parts = []
    for i in range(images):
        span = slice(i * patches, (i + 1) * patches)
        q, k, v = q_ref[0, span], k_ref[0, span], v_ref[0, span]
        gmi = gm[span]
        qt, kt, gmt = q.T, k.T, gmi.T
        gqt, gkt, gvt = [], [], []
        for h in range(heads):
            lanes = slice(h * HDIM, (h + 1) * HDIM)
            low_p = p_ref[0, i * heads + h]
            probs = low_p.astype(single)
            product = probs * dot(gmi[:, lanes], v[:, lanes], 1, 1)
            gs = (product - probs * jnp.sum(product, axis=-1, keepdims=True)).astype(bfloat)
            gqt.append(dot(kt[lanes], gs, 1, 1))
            gkt.append(dot(qt[lanes], gs, 1, 0))
            gvt.append(dot(gmt[lanes], low_p, 1, 0))
        gqt = (jnp.concatenate(gqt, 0) * scale).astype(bfloat)
        gkt = (jnp.concatenate(gkt, 0) * scale).astype(bfloat)
        gvt = jnp.concatenate(gvt, 0).astype(bfloat)
        parts.append((gqt, gkt, gvt))
        a = acc_a[span] + dot(gqt.T, wbuf[j, :cols], 1, 0)
        b = dot(gkt.T, wbuf[j, cols : 2 * cols], 1, 0) + dot(gvt.T, wbuf[j, 2 * cols : 3 * cols], 1, 0)
        if cross:
            acc_a[span] = a
            acc_b[span] += b
        else:
            acc_a[span] = a + b
    gqt, gkt, gvt = (jnp.concatenate([p[n] for p in parts], 1) for n in range(3))
    ones = jnp.ones((8, images * patches), bfloat)
    sums_ref[pl.ds(j, 1), :cols] = dot(ones, gqt, 1, 1)[0:1]
    sums_ref[pl.ds(j, 1), cols : 2 * cols] = dot(ones, gvt, 1, 1)[0:1]
    qn = qn_ref[...]
    cn = cn_ref[...] if cross else qn
    pack_ref[0, 0:cols] = dot(gqt, qn, 1, 0).astype(bfloat)
    pack_ref[0, cols : 2 * cols] = dot(gkt, cn, 1, 0).astype(bfloat)
    pack_ref[0, 2 * cols : 3 * cols] = dot(gvt, cn, 1, 0).astype(bfloat)
    pack_ref[0, 3 * cols :] = dot(mix_ref[0], low, 0, 0).astype(bfloat)

    @pl.when(j == 1)
    def _():
        gn = acc_a[...]
        if not last:
            outa_ref[...] = gn
            if cross:
                outb_ref[...] = acc_b[...]
            return
        x = x_ref[...].astype(single)
        unit, factor = norm_parts(x)
        sums_ref[4:5] = column_sum(gn * unit)
        sums_ref[5:6] = column_sum(gn)
        gx = h_ref[...] + norm_back(gn, unit, factor, rows_ref[1:2])
        if cross:
            seen = seen_ref[...] > 0
            unit, factor = norm_parts(jnp.where(seen, latent_ref[...], x))
            gn = acc_b[...]
            sums_ref[6:7] = column_sum(gn * unit)
            sums_ref[7:8] = column_sum(gn)
            flow = norm_back(gn, unit, factor, rows_ref[2:3])
            gx = gx + jnp.where(seen, 0.0, flow)
            outb_ref[...] = dlat_ref[...].astype(single) + jnp.where(seen, flow, 0.0)
        store_blocks(outa_ref, gx)


def attention_grads(slots, parts, h, x, cross, gains, scale, branch, qn, cn, q, k, v, p, mix, weights, blocks, deps=()):
    last = parts is not None
    rows, width = x.shape
    cols = q.shape[2]
    params = jnp.stack([scale, gains[0]] + ([gains[1]] if cross else []))
    pack = (2, 4 * cols, width)
    ins = [(whole(v.shape), v) for v in (h, params, branch, qn) + ((cn,) if cross else ())]
    ins += [(half_specs(e.shape, slots), e) for e in (q, k, v, p, mix)]
    if last:
        ins += [(whole(e.shape), e) for e in (x, *parts, *(cross or ()))]
    ins += [(ANY, weights[r]) for r in slots]
    outs = [(blocks, bfloat) if last else ((rows, width), single)]
    outs += [((rows, width), single)] if cross else []
    specs = [whole(s) for s, _ in outs] + [by_slot(pack), whole((SUMS, width))]
    outs += [(pack, bfloat), ((SUMS, width), single)]
    accs = [pltpu.VMEM((rows, width), single)] * (2 if cross else 1)
    return run(
        ins,
        outs,
        specs,
        deps,
        body=functools.partial(attention_grads_kernel, bool(cross), last),
        grid=(2,),
        name="attention_grads",
        scratch_shapes=[
            pltpu.VMEM((2,) + weights[0].shape, bfloat),
            pltpu.VMEM((rows, width), bfloat),
            *accs,
            pltpu.SemaphoreType.DMA((2,)),
        ],
    )


def spread_kernel(names, me_ref, *refs):
    j = pl.program_id(0)
    count = len(refs) - names
    for r in range(count):

        @pl.when(j == r)
        def _(r=r):
            for n in range(names):
                refs[count + n][0] = refs[r][n].astype(single)


def spread(me, pieces):
    names, *block = pieces[0].shape
    zeros = (0,) * len(block)
    spec = pl.BlockSpec((1, *block), lambda j, me_ref: (me_ref[0] ^ j,) + zeros)
    return pl.pallas_call(
        functools.partial(spread_kernel, names),
        grid_spec=pltpu.PrefetchScalarGridSpec(
            num_scalar_prefetch=1,
            grid=(len(pieces),),
            in_specs=[pl.BlockSpec(p.shape, lambda j, me_ref: (0,) + zeros) for p in pieces],
            out_specs=[spec] * names,
        ),
        out_shape=[jax.ShapeDtypeStruct((len(pieces), *block), single)] * names,
        name="spread",
    )(me.reshape(1), *pieces)


def pack_kernel(skip, *refs):
    in_ref, out_ref, inbias_ref, expbias_ref, pack_ref = refs[skip:]
    cols = in_ref.shape[2]
    width = in_ref.shape[1]
    for n in range(3):
        pack_ref[n * cols : (n + 1) * cols] = in_ref[n].T
    pack_ref[3 * cols : 4 * cols] = out_ref[...]

    def halves(values):
        high = values.astype(bfloat).astype(single)
        return high, values - high

    lines = [*halves(inbias_ref[...]), *halves(expbias_ref[...])]
    lines = [jnp.concatenate(lines[:2], 1)] + lines[2:] + [jnp.zeros((BIAS_ROWS - 3, width), single)]
    pack_ref[4 * cols :] = jnp.concatenate(lines, 0).astype(bfloat)


def attention_pack(inproj, outproj, inbias, expbias, deps):
    cols, width = outproj.shape
    return pl.pallas_call(
        functools.partial(pack_kernel, len(deps)),
        in_specs=[ANY] * len(deps) + [pl.BlockSpec(memory_space=pltpu.VMEM)] * 4,
        out_shape=jax.ShapeDtypeStruct((4 * cols + BIAS_ROWS, width), bfloat),
        name="pack",
    )(*deps, inproj, outproj, inbias.reshape(1, -1), expbias.reshape(1, -1))


def swap(values, axis, count, bit):
    return lax.ppermute(values, axis, [(i, i ^ bit) for i in range(count)])


def near_core(values):
    return swap(values, "tensor", SLOTS, 1)


def over_chip(values):
    return swap(values, "tensor", SLOTS, 2)


def part_at(values, index, parts, axis=0):
    size = values.shape[axis] // parts
    return lax.dynamic_slice_in_dim(values, index * size, size, axis)


def add_low(*terms):
    total = terms[0].astype(single)
    for term in terms[1:]:
        total = total + term.astype(single)
    return total.astype(bfloat)


def placed(mine, own, other):
    first = mine == 0
    return jnp.concatenate([jnp.where(first, own, other), jnp.where(first, other, own)], 0)


def tie(*values):
    return lax.optimization_barrier(values)


def gather_stages(count):
    stages, stride = [], 1
    while stride < count:
        radix = 2 if stride == 1 else min(4, count // stride)
        stages.append((radix, stride))
        stride *= radix
    return stages


def gather_piece(count):
    place, piece = lax.axis_index("dp"), 0
    for radix, stride in gather_stages(count):
        piece = piece * radix + (place // stride) % radix
    return piece


def gather_send(values, count, stage):
    radix, stride = gather_stages(count)[stage]
    return [values] + [swap(values, "dp", count, hop * stride) for hop in range(1, radix)]


def gather_join(pieces, count, stage, axis):
    radix, stride = gather_stages(count)[stage]
    mine = (lax.axis_index("dp") // stride) % radix
    size = pieces[0].shape[axis]
    shape = list(pieces[0].shape)
    shape[axis] = size * radix
    whole_array = jnp.zeros(shape, pieces[0].dtype)
    for hop, piece in enumerate(pieces):
        whole_array = lax.dynamic_update_slice_in_dim(whole_array, piece, (mine ^ hop) * size, axis)
    return whole_array


class Unit:
    def __init__(self, count, send, across_first):
        self.count, self.across_first = count, across_first
        self.pending = near_core(send)
        self.bits = []
        stride = 1
        while stride < count:
            self.bits.append(stride)
            stride *= 2
        self.stage = 0
        self.steps = 3 + 2 * (len(self.bits) - 1)

    def bit(self, n):
        return (lax.axis_index("dp") // self.bits[n]) % 2

    def hop(self, values, n):
        return swap(values, "dp", self.count, self.bits[n])

    def kept(self):
        return (self.near, getattr(self, "first", None), getattr(self, "value", None))[min(self.stage - 1, 2)]

    def keep_tied(self, kept):
        setattr(self, ("near", "first", "value")[min(self.stage - 1, 2)], kept)

    def follow(self, previous):
        self.pending, kept = tie(self.pending, previous.kept())
        previous.keep_tied(kept)

    def step(self):
        pending = self.pending
        stage, last = self.stage, len(self.bits) - 1
        self.stage += 1
        x = self.bit(0)
        if stage == 0:
            self.near = near = pending
            keep = self.keep
            if self.across_first:
                sent = add_low(keep[1], near[1])
                self.pending = over_chip(sent)
            else:
                sent = add_low(part_at(keep, 1 - x, 2, 1), part_at(near, 1 - x, 2, 1))
                self.pending = self.hop(sent, 0)
        elif stage == 1:
            keep, near = self.keep, self.near
            self.first = pending
            if self.across_first:
                sent = add_low(*(part_at(v, 1 - x, 2) for v in (keep[0], near[0], pending)))
                self.pending = self.hop(sent, 0)
            else:
                sent = add_low(part_at(keep[1], x, 2), part_at(near[1], x, 2), pending[1])
                self.pending = over_chip(sent)
        elif stage == 2:
            keep, near = self.keep, self.near
            first = part_at(self.first, x, 2) if self.across_first else self.first[0]
            self.value = add_low(part_at(keep[0], x, 2), part_at(near[0], x, 2), first, pending)
            sent = self.scatter(1)
        elif stage < 2 + last:
            n = stage - 2
            self.value = add_low(part_at(self.value, self.bit(n), 2), pending)
            sent = self.scatter(n + 1)
        elif stage == 2 + last:
            sent = self.value = add_low(part_at(self.value, self.bit(last), 2), pending)
            self.pending = self.hop(sent, last)
        else:
            n = last - (stage - 3 - last)
            sent = self.value = placed(self.bit(n), self.value, pending)
            self.pending = self.hop(sent, n - 1)
        return sent

    def scatter(self, n):
        sent = part_at(self.value, 1 - self.bit(n), 2)
        self.pending = self.hop(sent, n)
        return sent

    def result(self):
        return placed(self.bit(0), self.value, self.pending)


def steps_after(done, units):
    sent = []
    for n, u in enumerate(units):
        if n:
            u.follow(units[n - 1])
        else:
            u.pending, done = tie(u.pending, done)
        sent.append(u.step())
    return done, sent


TAIL = (
    "ea", "ef_e", "rf_s", "ef_s", "rf_e", "ra", "rf_s", "ef_e", "rf_e", "ra", "ea", "rf_s",
    "ef_e", "rf_e", "ra", "ef_s", "rf_s", "ea", "ef_e", "ra", "ef_s", "ea", "ef_e", "ef_s",
    "ea", "ef_e", "ef_s", "ea", "ef_s", "ea",
)


def make_local(count):
    def local(
        patches, mask_queries, visible, lengths, d_latent, d_regress,
        e_gain, e_shift, e_scale, e_inproj, e_inbias, e_outproj, e_outbias, e_expand, e_expbias, e_shrink,
        r_gain, r_shift, r_scale, r_inproj, r_inbias, r_outproj, r_outbias, r_expand, r_expbias, r_shrink,
    ):
        micro, images, part, width = patches.shape
        patch_count = visible.shape[2]
        rows = images * patch_count
        cols = e_inbias.shape[1]
        hidden = e_expbias.shape[0]
        blocks = (SLOTS, images, part, width)
        me = lax.axis_index("tensor")

        def pieces_of(*arrays):
            taken = []
            for r in range(SLOTS):
                one = [lax.dynamic_index_in_dim(a, me ^ r, 0, keepdims=False).astype(bfloat) for a in arrays]
                taken.append(jnp.stack(one) if len(one) > 1 else one[0])
            return taken

        def exchange(pieces):
            return [swap(p, "tensor", SLOTS, r) if r else p for r, p in enumerate(pieces)]

        def join(pieces):
            return jnp.stack(pieces, 1).reshape(rows, width)

        pieces = pieces_of(patches)
        tokens_sent = exchange(pieces)
        piece = gather_piece(count)
        stages = len(gather_stages(count))

        def feed_piece(expand, shrink):
            return jnp.stack([part_at(expand, piece, count), part_at(shrink, piece, count)])

        def gather_to_last(sent):
            for stage in range(stages - 1, 0, -1):
                joined = gather_join(sent, count, stage, 1)
                sent = gather_send(joined, count, stage - 1)
            return joined, sent

        e_piece, r_piece = feed_piece(e_expand, e_shrink), feed_piece(r_expand, r_shrink)
        e_slice = over_chip(e_piece)
        e_pack = attention_pack(e_inproj, e_outproj, e_inbias, e_expbias, [*pieces[1:], e_piece])
        e_pack_t, r_piece, *tokens_sent = tie(e_pack, r_piece, *tokens_sent)
        e_pack1, e_pack2 = near_core(e_pack_t), over_chip(e_pack_t)
        r_slice = over_chip(r_piece)
        e_gathered, e_half = gather_to_last(gather_send(e_slice, count, stages - 1))

        tensor_order = jnp.stack([me ^ r for r in range(SLOTS)])
        position = (tensor_order[:, None] * part + jnp.arange(part)[None, :]).reshape(-1)
        my_lengths = lax.dynamic_index_in_dim(lengths, me, 0, keepdims=False)
        my_visible = lax.dynamic_index_in_dim(visible, me, 0, keepdims=False)
        my_visible = jnp.concatenate([part_at(my_visible, me ^ r, SLOTS, 1) for r in range(SLOTS)], 1)
        valid = position[None, :] < my_lengths[:, None]
        seen = (my_visible == 1) | (position[None, :] == 0)
        seen_rows = seen.reshape(rows, 1).astype(single)
        e_mask = jnp.where(valid & seen, 0.0, -1e30).astype(single)[:, None, :]
        r_mask = jnp.where(valid, 0.0, -1e30).astype(single)[:, None, :]

        tokens = join(tokens_sent)
        r_pack = attention_pack(r_inproj, r_outproj, r_inbias, r_expbias, [e_pack])
        q_pieces = pieces_of(mask_queries)
        g_pieces = pieces_of(d_regress, d_latent)
        e_pack2, e_gathered, r_pack_t = tie(e_pack2, e_gathered, r_pack)
        e_pack3 = near_core(e_pack2)
        r_pack2 = over_chip(r_pack_t)
        e_packs = [e_pack, e_pack1, e_pack2, e_pack3]
        e_mid, e_ba, n0, q0, k0, v0, p0, mix0 = attention(
            tokens, None, e_gain, e_shift, e_outbias[0], e_scale[0], e_mask, e_packs,
            [e_gathered, r_slice, r_pack, *q_pieces, *g_pieces],
        )

        e_mid, e_half[1], e_exp_t, e_shr_t, r_pack1_t, r_slice, *q_pieces = tie(
            e_mid, e_half[1], e_expand, e_shrink, r_pack, r_slice, *q_pieces
        )
        r_pack1 = near_core(r_pack1_t)
        r_sent = gather_send(r_slice, count, stages - 1)
        e_feed2 = gather_join(e_half, count, 0, 1)
        e_feed3 = near_core(e_feed2)
        e_exp1, e_shr1 = near_core(e_exp_t), near_core(e_shr_t)
        queries_sent = exchange(q_pieces)
        e_feeds = [e_expand, e_shrink, e_exp1, e_shr1, e_feed2, e_feed3]
        latent, latent_low, e_bf, n1, e_act, e_slope = feed_forward(
            e_mid, e_gain[1], e_shift[1], e_outbias[1], e_scale[1], e_feeds, e_packs, blocks, True,
            [r_pack1],
        )

        hops = len(r_sent)
        latent, r_pack2, *rest = tie(latent, r_pack2, *r_sent, *g_pieces)
        r_gathered, r_half = gather_to_last(rest[:hops])
        g_pieces = rest[hops:]
        r_pack3 = near_core(r_pack2)
        queries = join(queries_sent)
        r_packs = [r_pack, r_pack1, r_pack2, r_pack3]
        r_mid, r_ba, qn, cn, q1, k1, v1, p1, mix1 = attention(
            queries, (latent, seen_rows), r_gain, r_shift, r_outbias[0], r_scale[0], r_mask, r_packs, [r_gathered]
        )

        g_sent = exchange(g_pieces)
        r_mid, r_half[1], r_exp_t, r_shr_t = tie(r_mid, r_half[1], r_expand, r_shrink)
        r_feed2 = gather_join(r_half, count, 0, 1)
        r_feed3 = near_core(r_feed2)
        r_exp1, r_shr1 = near_core(r_exp_t), near_core(r_shr_t)
        r_feeds = [r_expand, r_shrink, r_exp1, r_shr1, r_feed2, r_feed3]
        regressed_low, r_bf, n2, r_act, r_slope = feed_forward(
            r_mid, r_gain[2], r_shift[2], r_outbias[1], r_scale[1], r_feeds, r_packs, blocks, False
        )

        regressed_low, *g_sent = tie(regressed_low, *g_sent)
        g_regress = join([g[0] for g in g_sent])
        g_latent = join([g[1] for g in g_sent])
        outs_sent = exchange([jnp.stack([latent_low[r], regressed_low[r]]) for r in range(SLOTS)])

        def feed_back(orders, g, x, gain, scale, branch, n, act, slope, feed, deps):
            part_sum, send_e, send_s, sums_send = feed_grads(
                SEND, None, g, x, gain, scale, branch, n, act, slope, feed, deps
            )
            unit_e = Unit(count, send_e, orders[0])
            unit_s = Unit(count, send_s, orders[1])
            h, unit_e.keep, unit_s.keep, sums_keep = feed_grads(
                KEEP, part_sum, g, x, gain, scale, branch, n, act, slope, feed
            )
            return h, unit_e, unit_s, (sums_send, sums_keep)

        h, rf_e, rf_s, sums_rf = feed_back(
            (True, False), g_regress, r_mid, r_gain[2], r_scale[1], r_bf, n2, r_act, r_slope, r_feeds, []
        )
        h, sent = steps_after(h, [rf_e, rf_s])
        args = (h, queries, (latent, seen_rows, g_latent), r_gain, r_scale[0], r_ba, qn, cn, q1, k1, v1, p1, mix1, r_packs, blocks)
        part_a, part_b, send, sums_send = attention_grads(SEND, None, *args, sent)
        ra = Unit(count, send, True)
        gq_low, g, ra.keep, sums_keep = attention_grads(KEEP, (part_a, part_b), *args, outs_sent[1:])
        sums_ra = (sums_send, sums_keep)

        g, sent = steps_after(g, [ra, rf_e, rf_s])
        outs2_sent = exchange([gq_low[r] for r in range(SLOTS)])
        h, ef_e, ef_s, sums_ef = feed_back(
            (False, True), g, e_mid, e_gain[1], e_scale[1], e_bf, n1, e_act, e_slope, e_feeds, sent
        )
        h, sent = steps_after(h, [rf_e, ef_e, ra, ef_s])
        args = (h, tokens, None, e_gain, e_scale[0], e_ba, n0, None, q0, k0, v0, p0, mix0, e_packs, blocks)
        part_a, send, sums_send = attention_grads(SEND, None, *args, sent)
        ea = Unit(count, send, False)
        part_a, sent = steps_after(part_a, [rf_s, rf_e])
        gp_low, ea.keep, sums_keep = attention_grads(KEEP, (part_a,), *args, [*sent, *outs2_sent[1:]])
        sums_ea = (sums_send, sums_keep)

        pairs = (sums_ef, sums_ea, sums_rf, sums_ra)
        small = jnp.stack([p[n] for n in (1, 0) for p in pairs])
        line = lax.broadcasted_iota(jnp.int32, (1, SUMS, 1), 1)
        distances = [2**n for n in range(count.bit_length() - 1)]
        small_now = [small, near_core(small), 0]

        def small_step(u):
            totals, near, stage = small_now
            if near is None:
                return
            near, kept = tie(near, u.kept())
            u.keep_tied(kept)
            if stage == 0:
                totals = totals[:4] + jnp.where(line < 2, near[4:], near[:4])
                near = over_chip(totals)
            else:
                totals = totals + (jnp.where(line == 0, near[:, 1:2], near) if stage == 1 else near)
                near = swap(totals, "dp", count, distances.pop(0)) if distances else None
            small_now[:] = [totals, near, stage + 1]

        ef_e.pending, rf_s.pending, ea.keep = tie(ef_e.pending, rf_s.pending, ea.keep)
        units = dict(ea=ea, rf_e=rf_e, rf_s=rf_s, ra=ra, ef_e=ef_e, ef_s=ef_s)
        sequence = [units[name] for name in TAIL]
        previous, turn = None, 0
        while any(u.stage < u.steps for u in units.values()):
            u = sequence.pop(0) if sequence else next(u for u in units.values() if u.stage < u.steps)
            if u.stage == u.steps:
                continue
            if previous is not None and previous is not u:
                u.follow(previous)
            u.step()
            previous = u
            turn += 1
            if turn >= 4 and turn % 3 == 1:
                small_step(u)
            if turn == 8:
                kept, gp_low = tie(u.kept(), gp_low)
                u.keep_tied(kept)
            if turn == 16:
                kept, *late = tie(u.kept(), *outs_sent, *outs2_sent)
                u.keep_tied(kept)
                outs_sent, outs2_sent = late[:SLOTS], late[SLOTS:]
        while small_now[1] is not None:
            small_step(u)
        totals = small_now[0]
        outs3_sent = exchange([gp_low[r] for r in range(SLOTS)])
        out_latent, out_regressed = spread(me, outs_sent)
        (out_queries,) = spread(me, [o[None] for o in outs2_sent])
        (out_patches,) = spread(me, [o[None] for o in outs3_sent])
        rf_e, rf_s, ra, ef_e, ef_s, ea = (u.result() for u in (rf_e, rf_s, ra, ef_e, ef_s, ea))

        e_f, e_a, r_f, r_a = totals
        e_inb_g = e_a[0, : 2 * cols].reshape(2, cols)
        r_inb_g = r_a[0, : 2 * cols].reshape(2, cols)
        e_exb_g, r_exb_g = e_f[0], r_f[0]

        def attention_outputs(shard):
            shard = shard.astype(single)
            return shard[: 3 * cols].reshape(3, cols, width).transpose(0, 2, 1), shard[3 * cols :]

        e_in_g, e_out_g = attention_outputs(ea)
        r_in_g, r_out_g = attention_outputs(ra)
        return (
            out_latent, out_regressed, out_patches, out_queries,
            jnp.stack([e_a[4], e_f[2]]), jnp.stack([e_a[5], e_f[3]]), jnp.stack([e_a[2], e_f[4]]),
            e_in_g, e_inb_g, e_out_g, jnp.stack([e_a[3], e_f[5]]), ef_e.astype(single), e_exb_g, ef_s.astype(single),
            jnp.stack([r_a[4], r_a[6], r_f[2]]), jnp.stack([r_a[5], r_a[7], r_f[3]]), jnp.stack([r_a[2], r_f[4]]),
            r_in_g, r_inb_g, r_out_g, jnp.stack([r_a[3], r_f[5]]), rf_e.astype(single), r_exb_g, rf_s.astype(single),
        )

    return local


def solution(mesh):
    assert mesh.shape["tensor"] == SLOTS
    rows = P(None, "dp", "tensor", None)

    def block():
        return (
            P(), P(), P(), P(None, None, "tensor"), P(None, "tensor"), P("tensor", None), P(),
            P(None, "tensor"), P("tensor"), P("tensor", None),
        )

    return jax.shard_map(
        make_local(mesh.shape["dp"]),
        mesh=mesh,
        in_specs=(rows, rows, P(None, "dp", None), P(None, "dp"), rows, rows, *block(), *block()),
        out_specs=(rows, rows, rows, rows, *block(), *block()),
        check_vma=False,
    )
```

```python
import functools
import jax
import jax.numpy as jnp
from jax import lax
from jax.experimental import pallas as pl
from jax.experimental.pallas import tpu as pltpu
from jax.sharding import PartitionSpec as P

HDIM = 64
epsilon = 1e-06
bfloat = jnp.bfloat16
single = jnp.float32
SLOTS = 4
GRANT = 24 * 2**20


def dot(a, b, ca, cb):
    return lax.dot_general(a, b, (((ca,), (cb,)), ((), ())), preferred_element_type=single)


def norm_parts(values):
    average = jnp.mean(values, axis=-1, keepdims=True)
    centred = values - average
    variance = jnp.mean(centred * centred, axis=-1, keepdims=True)
    factor = lax.rsqrt(variance + epsilon)
    return centred * factor, factor


def norm_back(gradient, unit, factor, gain_row):
    scaled = gradient * gain_row
    return factor * (
        scaled
        - jnp.mean(scaled, axis=-1, keepdims=True)
        - unit * jnp.mean(scaled * unit, axis=-1, keepdims=True)
    )


def column_sum(values):
    return jnp.sum(values, axis=0, keepdims=True)


def gelu_parts(hidden):
    size = jnp.abs(hidden)
    bell = jnp.exp(-0.5 * hidden * hidden)
    t = 1.0 / (1.0 + (0.3275911 * 0.5**0.5) * size)
    poly = t * (0.127414796 + t * (-0.142248368 + t * (0.7107068705 + t * (-0.7265760135 + t * 0.5307027145))))
    tail = poly * bell
    below = jnp.where(hidden < 0, tail, 1.0 - tail)
    return hidden * below, below + hidden * bell * 0.3989422804


def start_copies(step, sources, buffer, sems):
    @pl.when(step == 0)
    def _():
        for r, source in enumerate(sources):
            pltpu.make_async_copy(source, buffer.at[r], sems.at[r]).start()


def wait_copy(step, sources, buffer, sems):
    for r, source in enumerate(sources):

        @pl.when(step == r)
        def _(r=r, source=source):
            pltpu.make_async_copy(source, buffer.at[r], sems.at[r]).wait()


def whole(shape):
    zeros = (0,) * len(shape)
    return pl.BlockSpec(shape, lambda j: zeros, pipeline_mode=pl.Buffered(1))


def by_slot(shape):
    zeros = (0,) * (len(shape) - 1)
    return pl.BlockSpec((1,) + shape[1:], lambda j: (j,) + zeros)


ANY = pl.BlockSpec(memory_space=pl.ANY)
SEND, KEEP = (1, 3), (0, 2)
BIAS_ROWS = 16
SUMS = 8


def store_blocks(low_ref, values):
    blocks, images, part = low_ref.shape[:3]
    for r in range(blocks):
        for i in range(images):
            start = (i * blocks + r) * part
            low_ref[r, i] = values[start : start + part].astype(bfloat)


def run(call_inputs, outs, specs, deps, body, **kwargs):
    skip = len(deps)
    return pl.pallas_call(
        lambda *refs: body(*refs[skip:]),
        in_specs=[ANY] * skip + [s for s, _ in call_inputs],
        out_specs=specs,
        out_shape=[jax.ShapeDtypeStruct(s, d) for s, d in outs],
        compiler_params=pltpu.CompilerParams(vmem_limit_bytes=GRANT),
        cost_estimate=pl.CostEstimate(flops=40 * 10**9, bytes_accessed=2**27, transcendentals=0),
        **kwargs,
    )(*deps, *[v for _, v in call_inputs])


def feed_sources(refs):
    near, far = refs[:4], refs[4:]
    return [near[0], near[2], *(f.at[0] for f in far)], [near[1], near[3], *(f.at[1] for f in far)]


def feed_forward_kernel(wide, *refs):
    x_ref, rows_ref = refs[:2]
    expand, shrink = feed_sources(refs[2:8])
    biases = refs[8:12]
    outs = refs[12 : 17 + wide]
    out_ref = outs[0] if wide else None
    low_ref, branch_ref, n_ref, act_ref, slope_ref = outs[wide:]
    ebuf, sbuf, bbuf, acc, esem, ssem, bsem = refs[17 + wide :]
    j = pl.program_id(0)
    width = x_ref.shape[1]
    tops = [b.at[pl.ds(width, BIAS_ROWS)] for b in biases]
    start_copies(j, tops, bbuf, bsem)
    start_copies(j, expand, ebuf, esem)
    start_copies(j, shrink, sbuf, ssem)

    @pl.when(j == 0)
    def _():
        unit, _ = norm_parts(x_ref[...])
        n_ref[...] = (unit * rows_ref[0:1] + rows_ref[1:2]).astype(bfloat)
        acc[...] = jnp.zeros_like(acc)

    wait_copy(j, tops, bbuf, bsem)
    wait_copy(j, expand, ebuf, esem)
    bias = bbuf[j].astype(single)
    bias = bias[1:2] + bias[2:3]
    hidden_width = ebuf.shape[2]
    step = 256
    n = n_ref[...]
    for c in range(0, hidden_width, step):
        hidden = dot(n, ebuf[j, :, c : c + step], 1, 0) + bias[:, c : c + step]
        act, slope = gelu_parts(hidden)
        act_ref[0, :, c : c + step] = act.astype(bfloat)
        slope_ref[0, :, c : c + step] = slope.astype(bfloat)
    wait_copy(j, shrink, sbuf, ssem)
    acc[...] += dot(act_ref[0], sbuf[j], 1, 0)

    @pl.when(j == SLOTS - 1)
    def _():
        branch = acc[...] + rows_ref[2:3]
        branch_ref[...] = branch.astype(bfloat)
        out = x_ref[...] + rows_ref[3:4] * branch
        if wide:
            out_ref[...] = out
        store_blocks(low_ref, out)


def feed_forward(x, gain, shift, outbias, scale, weights, biases, blocks, wide, deps=()):
    rows, width = x.shape
    hidden = weights[0].shape[1]
    params = jnp.stack([gain, shift, outbias, scale])
    outs = [((rows, width), single)] if wide else []
    outs += [(blocks, bfloat)] + [((rows, width), bfloat)] * 2 + [((SLOTS, rows, hidden), bfloat)] * 2
    specs = [whole(s) for s, _ in outs[:-2]] + [by_slot(s) for s, _ in outs[-2:]]
    return run(
        [(whole(x.shape), x), (whole(params.shape), params)] + [(ANY, w) for w in (*weights, *biases)],
        outs,
        specs,
        deps,
        body=functools.partial(feed_forward_kernel, wide),
        grid=(SLOTS,),
        name="feed_forward",
        scratch_shapes=[
            pltpu.VMEM((SLOTS, width, hidden), bfloat),
            pltpu.VMEM((SLOTS, hidden, width), bfloat),
            pltpu.VMEM((SLOTS, BIAS_ROWS, width), bfloat),
            pltpu.VMEM((rows, width), single),
            pltpu.SemaphoreType.DMA((SLOTS,)),
            pltpu.SemaphoreType.DMA((SLOTS,)),
            pltpu.SemaphoreType.DMA((SLOTS,)),
        ],
    )


def half_specs(shape, slots):
    zeros = (0,) * (len(shape) - 1)
    first, step = slots[0], slots[1] - slots[0]
    return pl.BlockSpec((1,) + shape[1:], lambda j: (first + step * j,) + zeros)


def feed_grads_kernel(last, *refs):
    g_ref, rows_ref, branch_ref, n_ref, act_ref, slope_ref = refs[:6]
    refs = refs[6:]
    if last:
        x_ref, part_ref = refs[:2]
        refs = refs[2:]
    expand, shrink = (refs[0], refs[2].at[0]), (refs[1], refs[2].at[1])
    h_ref, egrad_ref, sgrad_ref, sums_ref = refs[3:7]
    part_out = h_ref
    refs = refs[7:]
    ebuf, sbuf, gb, nt, acc, esem, ssem = refs
    j = pl.program_id(0)
    start_copies(j, shrink, sbuf, ssem)
    start_copies(j, expand, ebuf, esem)

    @pl.when(j == 0)
    def _():
        g = g_ref[...].astype(single)
        low = (rows_ref[1:2] * g).astype(bfloat)
        gb[...] = low
        nt[...] = n_ref[...].T
        sums_ref[...] = jnp.zeros_like(sums_ref)
        if last:
            sums_ref[4:5] = column_sum(g * branch_ref[...].astype(single))
            sums_ref[5:6] = column_sum(low.astype(single))
            acc[...] = part_ref[...]
        else:
            acc[...] = jnp.zeros_like(acc)

    wait_copy(j, shrink, sbuf, ssem)
    wait_copy(j, expand, ebuf, esem)
    width, hidden = ebuf.shape[1], ebuf.shape[2]
    step = 256
    low = gb[...]
    for c in range(0, hidden, step):
        gact = dot(low, sbuf[j, c : c + step, :], 1, 1)
        gh = (slope_ref[0, :, c : c + step].astype(single) * gact).astype(bfloat)
        sums_ref[pl.ds(j, 1), c : c + step] = column_sum(gh.astype(single))
        acc[...] += dot(gh, ebuf[j, :, c : c + step], 1, 1)
        egrad_ref[0, :, c : c + step] = dot(nt[...], gh, 1, 0).astype(bfloat)
        sgrad_ref[0, c : c + step, :] = dot(act_ref[0, :, c : c + step], low, 0, 0).astype(bfloat)

    @pl.when(j == 1)
    def _():
        gn = acc[...]
        if last:
            unit, factor = norm_parts(x_ref[...])
            sums_ref[2:3] = column_sum(gn * unit)
            sums_ref[3:4] = column_sum(gn)
            h_ref[...] = g_ref[...].astype(single) + norm_back(gn, unit, factor, rows_ref[0:1])
        else:
            part_out[...] = gn


def feed_grads(slots, part, g, x, gain, scale, branch, n, act, slope, weights, deps=()):
    first = 2 if slots == SEND else 0
    weights = (weights[first], weights[first + 1], weights[5 if slots == SEND else 4])
    last = part is not None
    rows, width = n.shape
    hidden = weights[0].shape[1]
    params = jnp.stack([gain, scale])
    unit = (2, width, hidden)
    outs = [((rows, width), single), (unit, bfloat), ((2, hidden, width), bfloat), ((SUMS, width), single)]
    specs = [whole((rows, width)), by_slot(unit), by_slot((2, hidden, width)), whole((SUMS, width))]
    ins = [(whole(v.shape), v) for v in (g, params, branch, n)]
    ins += [(half_specs(v.shape, slots), v) for v in (act, slope)]
    if last:
        ins += [(whole(v.shape), v) for v in (x, part)]
    ins += [(ANY, w) for w in weights]
    return run(
        ins,
        outs,
        specs,
        deps,
        body=functools.partial(feed_grads_kernel, last),
        grid=(2,),
        name="feed_grads",
        scratch_shapes=[
            pltpu.VMEM((2, width, hidden), bfloat),
            pltpu.VMEM((2, hidden, width), bfloat),
            pltpu.VMEM((rows, width), bfloat),
            pltpu.VMEM((width, rows), bfloat),
            pltpu.VMEM((rows, width), single),
            pltpu.SemaphoreType.DMA((2,)),
            pltpu.SemaphoreType.DMA((2,)),
        ],
    )


def attention_kernel(cross, *refs):
    x_ref = refs[0]
    refs = refs[1:]
    if cross:
        latent_ref, seen_ref = refs[:2]
        refs = refs[2:]
    rows_ref, mask_ref = refs[:2]
    weights = refs[2:6]
    mid_ref, branch_ref, qn_ref = refs[6:9]
    refs = refs[9:]
    if cross:
        cn_ref = refs[0]
        refs = refs[1:]
    q_ref, k_ref, v_ref, p_ref, mix_ref, wbuf, acc, wsem = refs
    j = pl.program_id(0)
    start_copies(j, weights, wbuf, wsem)

    @pl.when(j == 0)
    def _():
        x = x_ref[...].astype(single)
        unit, _ = norm_parts(x)
        qn_ref[...] = (unit * rows_ref[0:1] + rows_ref[1:2]).astype(bfloat)
        if cross:
            context = jnp.where(seen_ref[...] > 0, latent_ref[...], x)
            unit, _ = norm_parts(context)
            cn_ref[...] = (unit * rows_ref[4:5] + rows_ref[5:6]).astype(bfloat)
        acc[...] = jnp.zeros_like(acc)

    wait_copy(j, weights, wbuf, wsem)
    qn = qn_ref[...]
    cn = cn_ref[...] if cross else qn
    cols = q_ref.shape[2]
    bias = wbuf[j, 4 * cols : 4 * cols + BIAS_ROWS].astype(single)[0:1]
    bias = bias[:, : 2 * cols] + bias[:, 2 * cols :]
    q = (dot(qn, wbuf[j, :cols], 1, 1) + bias[:, :cols]).astype(bfloat)
    k = dot(cn, wbuf[j, cols : 2 * cols], 1, 1).astype(bfloat)
    v = (dot(cn, wbuf[j, 2 * cols : 3 * cols], 1, 1) + bias[:, cols:]).astype(bfloat)
    q_ref[0] = q
    k_ref[0] = k
    v_ref[0] = v
    images = mask_ref.shape[0]
    patches = mask_ref.shape[2]
    heads = cols // HDIM
    scaled = q * jnp.asarray(HDIM**-0.5, bfloat)
    for i in range(images):
        span = slice(i * patches, (i + 1) * patches)
        mixed = []
        for h in range(heads):
            lanes = slice(h * HDIM, (h + 1) * HDIM)
            scores = dot(scaled[span, lanes], k[span, lanes], 1, 1) + mask_ref[i]
            expo = jnp.exp(scores - jnp.max(scores, axis=-1, keepdims=True))
            probs = (expo * (1.0 / jnp.sum(expo, axis=-1, keepdims=True))).astype(bfloat)
            p_ref[0, i * heads + h] = probs
            mixed.append(dot(probs, v[span, lanes], 1, 0))
        mix_ref[0, span, :] = jnp.concatenate(mixed, axis=1).astype(bfloat)
    acc[...] += dot(mix_ref[0], wbuf[j, 3 * cols : 4 * cols], 1, 0)

    @pl.when(j == SLOTS - 1)
    def _():
        branch = acc[...] + rows_ref[2:3]
        branch_ref[...] = branch.astype(bfloat)
        mid_ref[...] = x_ref[...].astype(single) + rows_ref[3:4] * branch


def attention(x, cross, gains, shifts, outbias, scale, mask, weights, deps=()):
    rows, width = x.shape
    cols = (weights[0].shape[0] - BIAS_ROWS) // 4
    images, _, patches = mask.shape
    heads = cols // HDIM
    params = [gains[0], shifts[0], outbias, scale] + ([gains[1], shifts[1]] if cross else [])
    params = jnp.stack(params)
    extra = list(cross) if cross else []
    outs = [((rows, width), single), ((rows, width), bfloat), ((rows, width), bfloat)]
    outs += [((rows, width), bfloat)] if cross else []
    outs += [((SLOTS, rows, cols), bfloat)] * 3
    outs += [((SLOTS, images * heads, patches, patches), bfloat), ((SLOTS, rows, cols), bfloat)]
    return run(
        [(whole(v.shape), v) for v in (x, *extra, params, mask)] + [(ANY, w) for w in weights],
        outs,
        [whole(s) if len(s) == 2 else by_slot(s) for s, _ in outs],
        deps,
        body=functools.partial(attention_kernel, bool(cross)),
        grid=(SLOTS,),
        name="attention",
        scratch_shapes=[
            pltpu.VMEM((SLOTS,) + weights[0].shape, bfloat),
            pltpu.VMEM((rows, width), single),
            pltpu.SemaphoreType.DMA((SLOTS,)),
        ],
    )


def attention_grads_kernel(cross, last, *refs):
    refs = list(refs)
    take = lambda n: [refs.pop(0) for _ in range(n)]
    h_ref, rows_ref, branch_ref, qn_ref = take(4)
    cn_ref = take(1)[0] if cross else qn_ref
    q_ref, k_ref, v_ref, p_ref, mix_ref = take(5)
    if last:
        x_ref, parta_ref = take(2)
        if cross:
            partb_ref, latent_ref, seen_ref, dlat_ref = take(4)
    weights = take(2)
    outa_ref = take(1)[0]
    outb_ref = take(1)[0] if cross else None
    pack_ref, sums_ref = take(2)
    wbuf, ga, acc_a = take(3)
    acc_b = take(1)[0] if cross else None
    (wsem,) = take(1)
    j = pl.program_id(0)
    start_copies(j, weights, wbuf, wsem)

    @pl.when(j == 0)
    def _():
        h = h_ref[...]
        low = (rows_ref[0:1] * h).astype(bfloat)
        ga[...] = low
        sums_ref[...] = jnp.zeros_like(sums_ref)
        if last:
            sums_ref[2:3] = column_sum(h * branch_ref[...].astype(single))
            sums_ref[3:4] = column_sum(low.astype(single))
            acc_a[...] = parta_ref[...]
            if cross:
                acc_b[...] = partb_ref[...]
        else:
            acc_a[...] = jnp.zeros_like(acc_a)
            if cross:
                acc_b[...] = jnp.zeros_like(acc_b)

    wait_copy(j, weights, wbuf, wsem)
    cols = q_ref.shape[2]
    heads = cols // HDIM
    patches = p_ref.shape[2]
    images = p_ref.shape[1] // heads
    scale = HDIM**-0.5
    low = ga[...]
    gm = dot(low, wbuf[j, 3 * cols : 4 * cols], 1, 1).astype(bfloat)
    parts = []
    for i in range(images):
        span = slice(i * patches, (i + 1) * patches)
        q, k, v = q_ref[0, span], k_ref[0, span], v_ref[0, span]
        gmi = gm[span]
        qt, kt, gmt = q.T, k.T, gmi.T
        gqt, gkt, gvt = [], [], []
        for h in range(heads):
            lanes = slice(h * HDIM, (h + 1) * HDIM)
            low_p = p_ref[0, i * heads + h]
            probs = low_p.astype(single)
            product = probs * dot(gmi[:, lanes], v[:, lanes], 1, 1)
            gs = (product - probs * jnp.sum(product, axis=-1, keepdims=True)).astype(bfloat)
            gqt.append(dot(kt[lanes], gs, 1, 1))
            gkt.append(dot(qt[lanes], gs, 1, 0))
            gvt.append(dot(gmt[lanes], low_p, 1, 0))
        gqt = (jnp.concatenate(gqt, 0) * scale).astype(bfloat)
        gkt = (jnp.concatenate(gkt, 0) * scale).astype(bfloat)
        gvt = jnp.concatenate(gvt, 0).astype(bfloat)
        parts.append((gqt, gkt, gvt))
        a = acc_a[span] + dot(gqt.T, wbuf[j, :cols], 1, 0)
        b = dot(gkt.T, wbuf[j, cols : 2 * cols], 1, 0) + dot(gvt.T, wbuf[j, 2 * cols : 3 * cols], 1, 0)
        if cross:
            acc_a[span] = a
            acc_b[span] += b
        else:
            acc_a[span] = a + b
    gqt, gkt, gvt = (jnp.concatenate([p[n] for p in parts], 1) for n in range(3))
    ones = jnp.ones((8, images * patches), bfloat)
    sums_ref[pl.ds(j, 1), :cols] = dot(ones, gqt, 1, 1)[0:1]
    sums_ref[pl.ds(j, 1), cols : 2 * cols] = dot(ones, gvt, 1, 1)[0:1]
    qn = qn_ref[...]
    cn = cn_ref[...] if cross else qn
    pack_ref[0, 0:cols] = dot(gqt, qn, 1, 0).astype(bfloat)
    pack_ref[0, cols : 2 * cols] = dot(gkt, cn, 1, 0).astype(bfloat)
    pack_ref[0, 2 * cols : 3 * cols] = dot(gvt, cn, 1, 0).astype(bfloat)
    pack_ref[0, 3 * cols :] = dot(mix_ref[0], low, 0, 0).astype(bfloat)

    @pl.when(j == 1)
    def _():
        gn = acc_a[...]
        if not last:
            outa_ref[...] = gn
            if cross:
                outb_ref[...] = acc_b[...]
            return
        x = x_ref[...].astype(single)
        unit, factor = norm_parts(x)
        sums_ref[4:5] = column_sum(gn * unit)
        sums_ref[5:6] = column_sum(gn)
        gx = h_ref[...] + norm_back(gn, unit, factor, rows_ref[1:2])
        if cross:
            seen = seen_ref[...] > 0
            unit, factor = norm_parts(jnp.where(seen, latent_ref[...], x))
            gn = acc_b[...]
            sums_ref[6:7] = column_sum(gn * unit)
            sums_ref[7:8] = column_sum(gn)
            flow = norm_back(gn, unit, factor, rows_ref[2:3])
            gx = gx + jnp.where(seen, 0.0, flow)
            outb_ref[...] = dlat_ref[...].astype(single) + jnp.where(seen, flow, 0.0)
        store_blocks(outa_ref, gx)


def attention_grads(slots, parts, h, x, cross, gains, scale, branch, qn, cn, q, k, v, p, mix, weights, blocks, deps=()):
    last = parts is not None
    rows, width = x.shape
    cols = q.shape[2]
    params = jnp.stack([scale, gains[0]] + ([gains[1]] if cross else []))
    pack = (2, 4 * cols, width)
    ins = [(whole(v.shape), v) for v in (h, params, branch, qn) + ((cn,) if cross else ())]
    ins += [(half_specs(e.shape, slots), e) for e in (q, k, v, p, mix)]
    if last:
        ins += [(whole(e.shape), e) for e in (x, *parts, *(cross or ()))]
    ins += [(ANY, weights[r]) for r in slots]
    outs = [(blocks, bfloat) if last else ((rows, width), single)]
    outs += [((rows, width), single)] if cross else []
    specs = [whole(s) for s, _ in outs] + [by_slot(pack), whole((SUMS, width))]
    outs += [(pack, bfloat), ((SUMS, width), single)]
    accs = [pltpu.VMEM((rows, width), single)] * (2 if cross else 1)
    return run(
        ins,
        outs,
        specs,
        deps,
        body=functools.partial(attention_grads_kernel, bool(cross), last),
        grid=(2,),
        name="attention_grads",
        scratch_shapes=[
            pltpu.VMEM((2,) + weights[0].shape, bfloat),
            pltpu.VMEM((rows, width), bfloat),
            *accs,
            pltpu.SemaphoreType.DMA((2,)),
        ],
    )


def spread_kernel(names, me_ref, *refs):
    j = pl.program_id(0)
    count = len(refs) - names
    for r in range(count):

        @pl.when(j == r)
        def _(r=r):
            for n in range(names):
                refs[count + n][0] = refs[r][n].astype(single)


def spread(me, pieces):
    names, *block = pieces[0].shape
    zeros = (0,) * len(block)
    spec = pl.BlockSpec((1, *block), lambda j, me_ref: (me_ref[0] ^ j,) + zeros)
    return pl.pallas_call(
        functools.partial(spread_kernel, names),
        grid_spec=pltpu.PrefetchScalarGridSpec(
            num_scalar_prefetch=1,
            grid=(len(pieces),),
            in_specs=[pl.BlockSpec(p.shape, lambda j, me_ref: (0,) + zeros) for p in pieces],
            out_specs=[spec] * names,
        ),
        out_shape=[jax.ShapeDtypeStruct((len(pieces), *block), single)] * names,
        name="spread",
    )(me.reshape(1), *pieces)


def pack_kernel(skip, *refs):
    in_ref, out_ref, inbias_ref, expbias_ref, pack_ref = refs[skip:]
    cols = in_ref.shape[2]
    width = in_ref.shape[1]
    for n in range(3):
        pack_ref[n * cols : (n + 1) * cols] = in_ref[n].T
    pack_ref[3 * cols : 4 * cols] = out_ref[...]

    def halves(values):
        high = values.astype(bfloat).astype(single)
        return high, values - high

    lines = [*halves(inbias_ref[...]), *halves(expbias_ref[...])]
    lines = [jnp.concatenate(lines[:2], 1)] + lines[2:] + [jnp.zeros((BIAS_ROWS - 3, width), single)]
    pack_ref[4 * cols :] = jnp.concatenate(lines, 0).astype(bfloat)


def attention_pack(inproj, outproj, inbias, expbias, deps):
    cols, width = outproj.shape
    return pl.pallas_call(
        functools.partial(pack_kernel, len(deps)),
        in_specs=[ANY] * len(deps) + [pl.BlockSpec(memory_space=pltpu.VMEM)] * 4,
        out_shape=jax.ShapeDtypeStruct((4 * cols + BIAS_ROWS, width), bfloat),
        name="pack",
    )(*deps, inproj, outproj, inbias.reshape(1, -1), expbias.reshape(1, -1))


def swap(values, axis, count, bit):
    return lax.ppermute(values, axis, [(i, i ^ bit) for i in range(count)])


def near_core(values):
    return swap(values, "tensor", SLOTS, 1)


def over_chip(values):
    return swap(values, "tensor", SLOTS, 2)


def part_at(values, index, parts, axis=0):
    size = values.shape[axis] // parts
    return lax.dynamic_slice_in_dim(values, index * size, size, axis)


def add_low(*terms):
    total = terms[0].astype(single)
    for term in terms[1:]:
        total = total + term.astype(single)
    return total.astype(bfloat)


def placed(mine, own, other, axis=0):
    first = mine == 0
    return jnp.concatenate([jnp.where(first, own, other), jnp.where(first, other, own)], axis)


def tie(*values):
    return lax.optimization_barrier(values)


def gather_stages(count):
    stages, stride = [], 1
    while stride < count:
        radix = 2 if stride == 1 else min(4, count // stride)
        stages.append((radix, stride))
        stride *= radix
    return stages


def gather_piece(count):
    place, piece = lax.axis_index("dp"), 0
    for radix, stride in gather_stages(count):
        piece = piece * radix + (place // stride) % radix
    return piece


def gather_send(values, count, stage):
    radix, stride = gather_stages(count)[stage]
    return [values] + [swap(values, "dp", count, hop * stride) for hop in range(1, radix)]


def gather_join(pieces, count, stage, axis):
    radix, stride = gather_stages(count)[stage]
    mine = (lax.axis_index("dp") // stride) % radix
    size = pieces[0].shape[axis]
    shape = list(pieces[0].shape)
    shape[axis] = size * radix
    whole_array = jnp.zeros(shape, pieces[0].dtype)
    for hop, piece in enumerate(pieces):
        whole_array = lax.dynamic_update_slice_in_dim(whole_array, piece, (mine ^ hop) * size, axis)
    return whole_array


class Unit:
    def __init__(self, count, send, across_first):
        self.count, self.across_first = count, across_first
        self.pending = near_core(send)
        self.bits = []
        stride = 1
        while stride < count:
            self.bits.append(stride)
            stride *= 2
        self.stage = 0
        self.steps = 3 + 2 * (len(self.bits) - 1)

    def bit(self, n):
        return (lax.axis_index("dp") // self.bits[n]) % 2

    def hop(self, values, n):
        return swap(values, "dp", self.count, self.bits[n])

    def kept(self):
        return (self.near, getattr(self, "first", None), getattr(self, "value", None))[min(self.stage - 1, 2)]

    def keep_tied(self, kept):
        setattr(self, ("near", "first", "value")[min(self.stage - 1, 2)], kept)

    def follow(self, previous):
        self.pending, kept = tie(self.pending, previous.kept())
        previous.keep_tied(kept)

    def step(self):
        pending = self.pending
        stage, last = self.stage, len(self.bits) - 1
        self.stage += 1
        x = self.bit(0)
        if stage == 0:
            self.near = near = pending
            keep = self.keep
            if self.across_first:
                sent = add_low(keep[1], near[1])
                self.pending = over_chip(sent)
            else:
                sent = add_low(part_at(keep, 1 - x, 2, 1), part_at(near, 1 - x, 2, 1))
                self.pending = self.hop(sent, 0)
        elif stage == 1:
            keep, near = self.keep, self.near
            self.first = pending
            if self.across_first:
                sent = add_low(*(part_at(v, 1 - x, 2) for v in (keep[0], near[0], pending)))
                self.pending = self.hop(sent, 0)
            else:
                sent = add_low(part_at(keep[1], x, 2), part_at(near[1], x, 2), pending[1])
                self.pending = over_chip(sent)
        elif stage == 2:
            self.value = self.halves(pending)
            sent = self.scatter(1)
        elif stage < 2 + last:
            n = stage - 2
            self.value = add_low(part_at(self.value, self.bit(n), 2), pending)
            sent = self.scatter(n + 1)
        elif stage == 2 + last:
            sent = self.value = add_low(part_at(self.value, self.bit(last), 2), pending)
            self.pending = self.hop(sent, last)
        else:
            n = last - (stage - 3 - last)
            sent = self.value = placed(self.bit(n), self.value, pending)
            self.pending = self.hop(sent, n - 1)
        return sent

    def halves(self, pending):
        x = self.bit(0)
        first = part_at(self.first, x, 2) if self.across_first else self.first[0]
        return add_low(part_at(self.keep[0], x, 2), part_at(self.near[0], x, 2), first, pending)

    def scatter(self, n):
        sent = part_at(self.value, 1 - self.bit(n), 2)
        self.pending = self.hop(sent, n)
        return sent

    def result(self):
        return placed(self.bit(0), self.value, self.pending)


class Pair:
    def __init__(self, units):
        self.units = units
        self.count, self.bits, self.steps = units[0].count, units[0].bits, units[0].steps

    stage = 2

    @property
    def pending(self):
        return [u.pending for u in self.units] if self.stage == 2 else self.sent

    @pending.setter
    def pending(self, values):
        if self.stage == 2:
            for u, v in zip(self.units, values):
                u.pending = v
        else:
            self.sent = values

    def kept(self):
        return self.value

    def keep_tied(self, kept):
        self.value = kept

    def follow(self, previous):
        pending, kept = lax.optimization_barrier((self.pending, previous.kept()))
        self.pending = pending
        previous.keep_tied(kept)

    def bit(self, n):
        return self.units[0].bit(n)

    def hop(self, values, n):
        return self.units[0].hop(values, n)

    def scatter(self, n):
        sent = part_at(self.value, 1 - self.bit(n), 2, 1)
        self.sent = self.hop(sent, n)
        return sent

    def step(self):
        pending, stage, last = self.pending, self.stage, len(self.bits) - 1
        self.stage += 1
        if stage == 2:
            self.value = jnp.stack([u.halves(p) for u, p in zip(self.units, pending)])
            return self.scatter(1)
        if stage < 2 + last:
            n = stage - 2
            self.value = add_low(part_at(self.value, self.bit(n), 2, 1), pending)
            return self.scatter(n + 1)
        if stage == 2 + last:
            self.value = add_low(part_at(self.value, self.bit(last), 2, 1), pending)
            self.sent = self.hop(self.value, last)
        else:
            n = last - (stage - 3 - last)
            self.value = placed(self.bit(n), self.value, pending, 1)
            self.sent = self.hop(self.value, n - 1)
        return self.value

    def result(self):
        return placed(self.bit(0), self.value, self.sent, 1)


def steps_after(done, units):
    sent = []
    for n, u in enumerate(units):
        if n:
            u.follow(units[n - 1])
        else:
            u.pending, done = lax.optimization_barrier((u.pending, done))
        sent.append(u.step())
    return done, sent


TAIL = (
    "ea", "ef_e", "rf", "ef_s", "ra", "rf", "ra", "ea", "ef", "rf", "ra", "ef", "ea", "ra", "ef", "ea", "ra", "ef", "ea",
    "ef", "ea", "ea",
)


def make_local(count):
    def local(
        patches, mask_queries, visible, lengths, d_latent, d_regress,
        e_gain, e_shift, e_scale, e_inproj, e_inbias, e_outproj, e_outbias, e_expand, e_expbias, e_shrink,
        r_gain, r_shift, r_scale, r_inproj, r_inbias, r_outproj, r_outbias, r_expand, r_expbias, r_shrink,
    ):
        micro, images, part, width = patches.shape
        patch_count = visible.shape[2]
        rows = images * patch_count
        cols = e_inbias.shape[1]
        hidden = e_expbias.shape[0]
        blocks = (SLOTS, images, part, width)
        me = lax.axis_index("tensor")

        def pieces_of(*arrays):
            taken = []
            for r in range(SLOTS):
                one = [lax.dynamic_index_in_dim(a, me ^ r, 0, keepdims=False).astype(bfloat) for a in arrays]
                taken.append(jnp.stack(one) if len(one) > 1 else one[0])
            return taken

        def exchange(pieces):
            return [swap(p, "tensor", SLOTS, r) if r else p for r, p in enumerate(pieces)]

        def join(pieces):
            return jnp.stack(pieces, 1).reshape(rows, width)

        pieces = pieces_of(patches)
        tokens_sent = exchange(pieces)
        piece = gather_piece(count)
        stages = len(gather_stages(count))

        def feed_piece(expand, shrink):
            return jnp.stack([part_at(expand, piece, count), part_at(shrink, piece, count)])

        def gather_to_last(sent):
            for stage in range(stages - 1, 0, -1):
                joined = gather_join(sent, count, stage, 1)
                sent = gather_send(joined, count, stage - 1)
            return joined, sent

        e_piece, r_piece = feed_piece(e_expand, e_shrink), feed_piece(r_expand, r_shrink)
        e_slice = over_chip(e_piece)
        e_pack = attention_pack(e_inproj, e_outproj, e_inbias, e_expbias, [*pieces[1:], e_piece])
        e_pack_t, r_piece, e_exp_t, e_shr_t, *tokens_sent = tie(e_pack, r_piece, e_expand, e_shrink, *tokens_sent)
        e_pack1, e_pack2 = near_core(e_pack_t), over_chip(e_pack_t)
        e_exp1, e_shr1 = near_core(e_exp_t), near_core(e_shr_t)
        r_slice = over_chip(r_piece)
        e_sent = gather_send(e_slice, count, stages - 1)
        r_slice, e_sent[1] = tie(r_slice, e_sent[1])
        e_gathered, e_half = gather_to_last(e_sent)

        tensor_order = jnp.stack([me ^ r for r in range(SLOTS)])
        position = (tensor_order[:, None] * part + jnp.arange(part)[None, :]).reshape(-1)
        my_lengths = lax.dynamic_index_in_dim(lengths, me, 0, keepdims=False)
        my_visible = lax.dynamic_index_in_dim(visible, me, 0, keepdims=False)
        my_visible = jnp.concatenate([part_at(my_visible, me ^ r, SLOTS, 1) for r in range(SLOTS)], 1)
        valid = position[None, :] < my_lengths[:, None]
        seen = (my_visible == 1) | (position[None, :] == 0)
        seen_rows = seen.reshape(rows, 1).astype(single)
        e_mask = jnp.where(valid & seen, 0.0, -1e30).astype(single)[:, None, :]
        r_mask = jnp.where(valid, 0.0, -1e30).astype(single)[:, None, :]

        tokens = join(tokens_sent)
        r_pack = attention_pack(r_inproj, r_outproj, r_inbias, r_expbias, [e_pack])
        q_pieces = pieces_of(mask_queries)
        g_pieces = pieces_of(d_regress, d_latent)
        e_pack2, e_gathered, r_slice = tie(e_pack2, e_gathered, r_slice)
        e_pack3 = near_core(e_pack2)
        r_sent = gather_send(r_slice, count, stages - 1)
        e_packs = [e_pack, e_pack1, e_pack2, e_pack3]
        e_mid, e_ba, n0, q0, k0, v0, p0, mix0 = attention(
            tokens, None, e_gain, e_shift, e_outbias[0], e_scale[0], e_mask, e_packs,
            [e_gathered, r_slice, r_pack, *q_pieces, *g_pieces, e_exp1, e_shr1],
        )

        hops = len(r_sent)
        e_mid, e_half[1], r_pack_t, *rest = tie(e_mid, e_half[1], r_pack, *r_sent, *q_pieces)
        queries_sent = exchange(rest[hops:])
        r_pack1, r_pack2 = near_core(r_pack_t), over_chip(r_pack_t)
        r_gathered, r_half = gather_to_last(rest[:hops])
        e_feed2 = gather_join(e_half, count, 0, 1)
        e_feed3 = near_core(e_feed2)
        e_feeds = [e_expand, e_shrink, e_exp1, e_shr1, e_feed2, e_feed3]
        latent, latent_low, e_bf, n1, e_act, e_slope = feed_forward(
            e_mid, e_gain[1], e_shift[1], e_outbias[1], e_scale[1], e_feeds, e_packs, blocks, True,
            [r_pack1, r_gathered, *queries_sent[1:]],
        )

        latent, r_pack2, r_half[1], r_exp_t, r_shr_t, *g_pieces = tie(
            latent, r_pack2, r_half[1], r_expand, r_shrink, *g_pieces
        )
        r_pack3 = near_core(r_pack2)
        r_feed2 = gather_join(r_half, count, 0, 1)
        r_feed3 = near_core(r_feed2)
        r_exp1, r_shr1 = near_core(r_exp_t), near_core(r_shr_t)
        queries = join(queries_sent)
        r_packs = [r_pack, r_pack1, r_pack2, r_pack3]
        r_mid, r_ba, qn, cn, q1, k1, v1, p1, mix1 = attention(
            queries, (latent, seen_rows), r_gain, r_shift, r_outbias[0], r_scale[0], r_mask, r_packs, [r_feed2]
        )

        r_mid, *g_pieces = tie(r_mid, *g_pieces)
        g_sent = exchange(g_pieces)
        r_feeds = [r_expand, r_shrink, r_exp1, r_shr1, r_feed2, r_feed3]
        regressed_low, r_bf, n2, r_act, r_slope = feed_forward(
            r_mid, r_gain[2], r_shift[2], r_outbias[1], r_scale[1], r_feeds, r_packs, blocks, False
        )

        regressed_low, *g_sent = tie(regressed_low, *g_sent)
        g_regress = join([g[0] for g in g_sent])
        g_latent = join([g[1] for g in g_sent])
        outs_sent = exchange([jnp.stack([latent_low[r], regressed_low[r]]) for r in range(SLOTS)])

        def feed_back(orders, g, x, gain, scale, branch, n, act, slope, feed, deps):
            part_sum, send_e, send_s, sums_send = feed_grads(
                SEND, None, g, x, gain, scale, branch, n, act, slope, feed, deps
            )
            unit_e = Unit(count, send_e, orders[0])
            unit_s = Unit(count, send_s, orders[1])
            h, unit_e.keep, unit_s.keep, sums_keep = feed_grads(
                KEEP, part_sum, g, x, gain, scale, branch, n, act, slope, feed
            )
            return h, unit_e, unit_s, (sums_send, sums_keep)

        h, rf_e, rf_s, sums_rf = feed_back(
            (True, False), g_regress, r_mid, r_gain[2], r_scale[1], r_bf, n2, r_act, r_slope, r_feeds, []
        )
        h, sent = steps_after(h, [rf_e, rf_s])
        args = (h, queries, (latent, seen_rows, g_latent), r_gain, r_scale[0], r_ba, qn, cn, q1, k1, v1, p1, mix1, r_packs, blocks)
        part_a, part_b, send, sums_send = attention_grads(SEND, None, *args, sent)
        ra = Unit(count, send, True)
        gq_low, g, ra.keep, sums_keep = attention_grads(KEEP, (part_a, part_b), *args, outs_sent[1:])
        sums_ra = (sums_send, sums_keep)

        g, sent = steps_after(g, [ra, rf_e, rf_s])
        outs2_sent = exchange([gq_low[r] for r in range(SLOTS)])
        h, ef_e, ef_s, sums_ef = feed_back(
            (False, True), g, e_mid, e_gain[1], e_scale[1], e_bf, n1, e_act, e_slope, e_feeds, sent
        )
        rf = Pair([rf_e, rf_s])
        h, sent = steps_after(h, [ef_e, ra, ef_s])
        args = (h, tokens, None, e_gain, e_scale[0], e_ba, n0, None, q0, k0, v0, p0, mix0, e_packs, blocks)
        part_a, send, sums_send = attention_grads(SEND, None, *args, sent)
        ea = Unit(count, send, False)
        part_a, sent = steps_after(part_a, [rf])
        gp_low, ea.keep, sums_keep = attention_grads(KEEP, (part_a,), *args, [*sent, *outs2_sent[1:]])
        sums_ea = (sums_send, sums_keep)

        pairs = (sums_ef, sums_ea, sums_rf, sums_ra)
        small = jnp.stack([p[n] for n in (1, 0) for p in pairs])
        line = lax.broadcasted_iota(jnp.int32, (1, SUMS, 1), 1)
        distances = [2**n for n in range(count.bit_length() - 1)]
        small_now = [small, near_core(small), 0]

        def small_step(u):
            totals, near, stage = small_now
            if near is None:
                return
            near, kept = tie(near, u.kept())
            u.keep_tied(kept)
            if stage == 0:
                totals = totals[:4] + jnp.where(line < 2, near[4:], near[:4])
                near = over_chip(totals)
            else:
                totals = totals + (jnp.where(line == 0, near[:, 1:2], near) if stage == 1 else near)
                near = swap(totals, "dp", count, distances.pop(0)) if distances else None
            small_now[:] = [totals, near, stage + 1]

        ef_e.pending, rf.pending, ea.keep = tie(ef_e.pending, rf.pending, ea.keep)
        units = dict(ea=ea, rf=rf, ra=ra, ef_e=ef_e, ef_s=ef_s, ef=Pair([ef_e, ef_s]))
        previous = None
        for turn, name in enumerate(TAIL, 1):
            u = units[name]
            if u.stage == u.steps:
                continue
            if previous is not None and previous is not u:
                u.follow(previous)
            u.step()
            previous = u
            if turn >= 4 and turn % 3 == 1:
                small_step(u)
            if turn == 8:
                kept, gp_low = tie(u.kept(), gp_low)
                u.keep_tied(kept)
            if turn == 14:
                kept, *late = tie(u.kept(), *outs_sent, *outs2_sent)
                u.keep_tied(kept)
                outs_sent, outs2_sent = late[:SLOTS], late[SLOTS:]
        while small_now[1] is not None:
            small_step(u)
        totals = small_now[0]
        for name in ("rf", "ra", "ef", "ea") * 16:
            if units[name].stage < units[name].steps:
                units[name].step()
        outs3_sent = exchange([gp_low[r] for r in range(SLOTS)])
        out_latent, out_regressed = spread(me, outs_sent)
        (out_queries,) = spread(me, [o[None] for o in outs2_sent])
        (out_patches,) = spread(me, [o[None] for o in outs3_sent])
        (rf_e, rf_s), ra, (ef_e, ef_s), ea = (units[name].result() for name in ("rf", "ra", "ef", "ea"))

        e_f, e_a, r_f, r_a = totals
        e_inb_g = e_a[0, : 2 * cols].reshape(2, cols)
        r_inb_g = r_a[0, : 2 * cols].reshape(2, cols)
        e_exb_g, r_exb_g = e_f[0], r_f[0]

        def attention_outputs(shard):
            shard = shard.astype(single)
            return shard[: 3 * cols].reshape(3, cols, width).transpose(0, 2, 1), shard[3 * cols :]

        e_in_g, e_out_g = attention_outputs(ea)
        r_in_g, r_out_g = attention_outputs(ra)
        return (
            out_latent, out_regressed, out_patches, out_queries,
            jnp.stack([e_a[4], e_f[2]]), jnp.stack([e_a[5], e_f[3]]), jnp.stack([e_a[2], e_f[4]]),
            e_in_g, e_inb_g, e_out_g, jnp.stack([e_a[3], e_f[5]]), ef_e.astype(single), e_exb_g, ef_s.astype(single),
            jnp.stack([r_a[4], r_a[6], r_f[2]]), jnp.stack([r_a[5], r_a[7], r_f[3]]), jnp.stack([r_a[2], r_f[4]]),
            r_in_g, r_inb_g, r_out_g, jnp.stack([r_a[3], r_f[5]]), rf_e.astype(single), r_exb_g, rf_s.astype(single),
        )

    return local


def solution(mesh):
    assert mesh.shape["tensor"] == SLOTS
    rows = P(None, "dp", "tensor", None)

    def block():
        return (
            P(), P(), P(), P(None, None, "tensor"), P(None, "tensor"), P("tensor", None), P(),
            P(None, "tensor"), P("tensor"), P("tensor", None),
        )

    return jax.shard_map(
        make_local(mesh.shape["dp"]),
        mesh=mesh,
        in_specs=(rows, rows, P(None, "dp", None), P(None, "dp"), rows, rows, *block(), *block()),
        out_specs=(rows, rows, rows, rows, *block(), *block()),
        check_vma=False,
    )
```

```python
import functools
import jax
import jax.numpy as jnp
from jax import lax
from jax.experimental import pallas as pl
from jax.experimental.pallas import tpu as pltpu
from jax.sharding import PartitionSpec as P

HDIM = 64
epsilon = 1e-06
bfloat = jnp.bfloat16
single = jnp.float32
SLOTS = 4
GRANT = 18 * 2**20


def dot(a, b, ca, cb):
    return lax.dot_general(a, b, (((ca,), (cb,)), ((), ())), preferred_element_type=single)


def norm_parts(values):
    average = jnp.mean(values, axis=-1, keepdims=True)
    centred = values - average
    variance = jnp.mean(centred * centred, axis=-1, keepdims=True)
    factor = lax.rsqrt(variance + epsilon)
    return centred * factor, factor


def norm_back(gradient, unit, factor, gain_row):
    scaled = gradient * gain_row
    return factor * (
        scaled
        - jnp.mean(scaled, axis=-1, keepdims=True)
        - unit * jnp.mean(scaled * unit, axis=-1, keepdims=True)
    )


def column_sum(values):
    return jnp.sum(values, axis=0, keepdims=True)


def gelu_parts(hidden):
    size = jnp.abs(hidden)
    bell = jnp.exp(-0.5 * hidden * hidden)
    t = 1.0 / (1.0 + (0.3275911 * 0.5**0.5) * size)
    poly = t * (0.127414796 + t * (-0.142248368 + t * (0.7107068705 + t * (-0.7265760135 + t * 0.5307027145))))
    tail = poly * bell
    below = jnp.where(hidden < 0, tail, 1.0 - tail)
    return hidden * below, below + hidden * bell * 0.3989422804


def start_copies(step, sources, buffer, sems):
    @pl.when(step == 0)
    def _():
        for r, source in enumerate(sources):
            pltpu.make_async_copy(source, buffer.at[r], sems.at[r]).start()


def wait_copy(step, sources, buffer, sems):
    for r, source in enumerate(sources):

        @pl.when(step == r)
        def _(r=r, source=source):
            pltpu.make_async_copy(source, buffer.at[r], sems.at[r]).wait()


def whole(shape):
    zeros = (0,) * len(shape)
    return pl.BlockSpec(shape, lambda j: zeros, pipeline_mode=pl.Buffered(1))


def by_slot(shape):
    zeros = (0,) * (len(shape) - 1)
    return pl.BlockSpec((1,) + shape[1:], lambda j: (j,) + zeros)


ANY = pl.BlockSpec(memory_space=pl.ANY)
SEND, KEEP = (1, 3), (0, 2)
BIAS_ROWS = 16
SUMS = 8


def store_blocks(low_ref, values):
    blocks, images, part = low_ref.shape[:3]
    for r in range(blocks):
        for i in range(images):
            start = (i * blocks + r) * part
            low_ref[r, i] = values[start : start + part].astype(bfloat)


def run(call_inputs, outs, specs, deps, body, **kwargs):
    skip = len(deps)
    return pl.pallas_call(
        lambda *refs: body(*refs[skip:]),
        in_specs=[ANY] * skip + [s for s, _ in call_inputs],
        out_specs=specs,
        out_shape=[jax.ShapeDtypeStruct(s, d) for s, d in outs],
        compiler_params=pltpu.CompilerParams(vmem_limit_bytes=GRANT),
        cost_estimate=pl.CostEstimate(flops=40 * 10**9, bytes_accessed=2**27, transcendentals=0),
        **kwargs,
    )(*deps, *[v for _, v in call_inputs])


def feed_sources(refs):
    near, far = refs[:4], refs[4:]
    return [near[0], near[2], *(f.at[0] for f in far)], [near[1], near[3], *(f.at[1] for f in far)]


def feed_forward_kernel(wide, *refs):
    x_ref, rows_ref = refs[:2]
    expand, shrink = feed_sources(refs[2:8])
    biases = refs[8:12]
    outs = refs[12 : 17 + wide]
    out_ref = outs[0] if wide else None
    low_ref, branch_ref, n_ref, act_ref, slope_ref = outs[wide:]
    ebuf, sbuf, bbuf, acc, esem, ssem, bsem = refs[17 + wide :]
    j = pl.program_id(0)
    width = x_ref.shape[1]
    tops = [b.at[pl.ds(width, BIAS_ROWS)] for b in biases]
    start_copies(j, tops, bbuf, bsem)
    start_copies(j, expand, ebuf, esem)
    start_copies(j, shrink, sbuf, ssem)

    @pl.when(j == 0)
    def _():
        unit, _ = norm_parts(x_ref[...])
        n_ref[...] = (unit * rows_ref[0:1] + rows_ref[1:2]).astype(bfloat)
        acc[...] = jnp.zeros_like(acc)

    wait_copy(j, tops, bbuf, bsem)
    wait_copy(j, expand, ebuf, esem)
    bias = bbuf[j].astype(single)
    bias = bias[1:2] + bias[2:3]
    hidden_width = ebuf.shape[2]
    step = 256
    n = n_ref[...]
    for c in range(0, hidden_width, step):
        hidden = dot(n, ebuf[j, :, c : c + step], 1, 0) + bias[:, c : c + step]
        act, slope = gelu_parts(hidden)
        act_ref[0, :, c : c + step] = act.astype(bfloat)
        slope_ref[0, :, c : c + step] = slope.astype(bfloat)
    wait_copy(j, shrink, sbuf, ssem)
    acc[...] += dot(act_ref[0], sbuf[j], 1, 0)

    @pl.when(j == SLOTS - 1)
    def _():
        branch = acc[...] + rows_ref[2:3]
        branch_ref[...] = branch.astype(bfloat)
        out = x_ref[...] + rows_ref[3:4] * branch
        if wide:
            out_ref[...] = out
        store_blocks(low_ref, out)


def feed_forward(x, gain, shift, outbias, scale, weights, biases, blocks, wide, deps=()):
    rows, width = x.shape
    hidden = weights[0].shape[1]
    params = jnp.stack([gain, shift, outbias, scale])
    outs = [((rows, width), single)] if wide else []
    outs += [(blocks, bfloat)] + [((rows, width), bfloat)] * 2 + [((SLOTS, rows, hidden), bfloat)] * 2
    specs = [whole(s) for s, _ in outs[:-2]] + [by_slot(s) for s, _ in outs[-2:]]
    return run(
        [(whole(x.shape), x), (whole(params.shape), params)] + [(ANY, w) for w in (*weights, *biases)],
        outs,
        specs,
        deps,
        body=functools.partial(feed_forward_kernel, wide),
        grid=(SLOTS,),
        name="feed_forward",
        scratch_shapes=[
            pltpu.VMEM((SLOTS, width, hidden), bfloat),
            pltpu.VMEM((SLOTS, hidden, width), bfloat),
            pltpu.VMEM((SLOTS, BIAS_ROWS, width), bfloat),
            pltpu.VMEM((rows, width), single),
            pltpu.SemaphoreType.DMA((SLOTS,)),
            pltpu.SemaphoreType.DMA((SLOTS,)),
            pltpu.SemaphoreType.DMA((SLOTS,)),
        ],
    )


def half_specs(shape, slots):
    zeros = (0,) * (len(shape) - 1)
    first, step = slots[0], slots[1] - slots[0]
    return pl.BlockSpec((1,) + shape[1:], lambda j: (first + step * j,) + zeros)


def feed_grads_kernel(last, *refs):
    g_ref, rows_ref, branch_ref, n_ref, act_ref, slope_ref = refs[:6]
    refs = refs[6:]
    if last:
        x_ref, part_ref = refs[:2]
        refs = refs[2:]
    expand, shrink = (refs[0], refs[2].at[0]), (refs[1], refs[2].at[1])
    h_ref, egrad_ref, sgrad_ref, sums_ref = refs[3:7]
    part_out = h_ref
    refs = refs[7:]
    ebuf, sbuf, gb, nt, acc, esem, ssem = refs
    j = pl.program_id(0)
    start_copies(j, shrink, sbuf, ssem)
    start_copies(j, expand, ebuf, esem)

    @pl.when(j == 0)
    def _():
        g = g_ref[...].astype(single)
        low = (rows_ref[1:2] * g).astype(bfloat)
        gb[...] = low
        nt[...] = n_ref[...].T
        sums_ref[...] = jnp.zeros_like(sums_ref)
        if last:
            sums_ref[4:5] = column_sum(g * branch_ref[...].astype(single))
            sums_ref[5:6] = column_sum(low.astype(single))
            acc[...] = part_ref[...]
        else:
            acc[...] = jnp.zeros_like(acc)

    wait_copy(j, shrink, sbuf, ssem)
    wait_copy(j, expand, ebuf, esem)
    width, hidden = ebuf.shape[1], ebuf.shape[2]
    step = 256
    low = gb[...]
    for c in range(0, hidden, step):
        gact = dot(low, sbuf[j, c : c + step, :], 1, 1)
        gh = (slope_ref[0, :, c : c + step].astype(single) * gact).astype(bfloat)
        sums_ref[pl.ds(j, 1), c : c + step] = column_sum(gh.astype(single))
        acc[...] += dot(gh, ebuf[j, :, c : c + step], 1, 1)
        egrad_ref[0, :, c : c + step] = dot(nt[...], gh, 1, 0).astype(bfloat)
        sgrad_ref[0, c : c + step, :] = dot(act_ref[0, :, c : c + step], low, 0, 0).astype(bfloat)

    @pl.when(j == 1)
    def _():
        gn = acc[...]
        if last:
            unit, factor = norm_parts(x_ref[...])
            sums_ref[2:3] = column_sum(gn * unit)
            sums_ref[3:4] = column_sum(gn)
            h_ref[...] = g_ref[...].astype(single) + norm_back(gn, unit, factor, rows_ref[0:1])
        else:
            part_out[...] = gn


def feed_grads(slots, part, g, x, gain, scale, branch, n, act, slope, weights, deps=()):
    first = 2 if slots == SEND else 0
    weights = (weights[first], weights[first + 1], weights[5 if slots == SEND else 4])
    last = part is not None
    rows, width = n.shape
    hidden = weights[0].shape[1]
    params = jnp.stack([gain, scale])
    unit = (2, width, hidden)
    outs = [((rows, width), single), (unit, bfloat), ((2, hidden, width), bfloat), ((SUMS, width), single)]
    specs = [whole((rows, width)), by_slot(unit), by_slot((2, hidden, width)), whole((SUMS, width))]
    ins = [(whole(v.shape), v) for v in (g, params, branch, n)]
    ins += [(half_specs(v.shape, slots), v) for v in (act, slope)]
    if last:
        ins += [(whole(v.shape), v) for v in (x, part)]
    ins += [(ANY, w) for w in weights]
    return run(
        ins,
        outs,
        specs,
        deps,
        body=functools.partial(feed_grads_kernel, last),
        grid=(2,),
        name="feed_grads",
        scratch_shapes=[
            pltpu.VMEM((2, width, hidden), bfloat),
            pltpu.VMEM((2, hidden, width), bfloat),
            pltpu.VMEM((rows, width), bfloat),
            pltpu.VMEM((width, rows), bfloat),
            pltpu.VMEM((rows, width), single),
            pltpu.SemaphoreType.DMA((2,)),
            pltpu.SemaphoreType.DMA((2,)),
        ],
    )


def attention_kernel(cross, *refs):
    x_ref = refs[0]
    refs = refs[1:]
    if cross:
        latent_ref, seen_ref = refs[:2]
        refs = refs[2:]
    rows_ref, mask_ref = refs[:2]
    weights = refs[2:6]
    mid_ref, branch_ref, qn_ref = refs[6:9]
    refs = refs[9:]
    if cross:
        cn_ref = refs[0]
        refs = refs[1:]
    q_ref, k_ref, v_ref, p_ref, mix_ref, wbuf, acc, wsem = refs
    j = pl.program_id(0)
    start_copies(j, weights, wbuf, wsem)

    @pl.when(j == 0)
    def _():
        x = x_ref[...].astype(single)
        unit, _ = norm_parts(x)
        qn_ref[...] = (unit * rows_ref[0:1] + rows_ref[1:2]).astype(bfloat)
        if cross:
            context = jnp.where(seen_ref[...] > 0, latent_ref[...], x)
            unit, _ = norm_parts(context)
            cn_ref[...] = (unit * rows_ref[4:5] + rows_ref[5:6]).astype(bfloat)
        acc[...] = jnp.zeros_like(acc)

    wait_copy(j, weights, wbuf, wsem)
    qn = qn_ref[...]
    cn = cn_ref[...] if cross else qn
    cols = q_ref.shape[2]
    bias = wbuf[j, 4 * cols : 4 * cols + BIAS_ROWS].astype(single)[0:1]
    bias = bias[:, : 2 * cols] + bias[:, 2 * cols :]
    q = (dot(qn, wbuf[j, :cols], 1, 1) + bias[:, :cols]).astype(bfloat)
    k = dot(cn, wbuf[j, cols : 2 * cols], 1, 1).astype(bfloat)
    v = (dot(cn, wbuf[j, 2 * cols : 3 * cols], 1, 1) + bias[:, cols:]).astype(bfloat)
    q_ref[0] = q
    k_ref[0] = k
    v_ref[0] = v
    images = mask_ref.shape[0]
    patches = mask_ref.shape[2]
    heads = cols // HDIM
    scaled = q * jnp.asarray(HDIM**-0.5, bfloat)
    for i in range(images):
        span = slice(i * patches, (i + 1) * patches)
        mixed = []
        for h in range(heads):
            lanes = slice(h * HDIM, (h + 1) * HDIM)
            scores = dot(scaled[span, lanes], k[span, lanes], 1, 1) + mask_ref[i]
            expo = jnp.exp(scores - jnp.max(scores, axis=-1, keepdims=True))
            probs = (expo * (1.0 / jnp.sum(expo, axis=-1, keepdims=True))).astype(bfloat)
            p_ref[0, i * heads + h] = probs
            mixed.append(dot(probs, v[span, lanes], 1, 0))
        mix_ref[0, span, :] = jnp.concatenate(mixed, axis=1).astype(bfloat)
    acc[...] += dot(mix_ref[0], wbuf[j, 3 * cols : 4 * cols], 1, 0)

    @pl.when(j == SLOTS - 1)
    def _():
        branch = acc[...] + rows_ref[2:3]
        branch_ref[...] = branch.astype(bfloat)
        mid_ref[...] = x_ref[...].astype(single) + rows_ref[3:4] * branch


def attention(x, cross, gains, shifts, outbias, scale, mask, weights, deps=()):
    rows, width = x.shape
    cols = (weights[0].shape[0] - BIAS_ROWS) // 4
    images, _, patches = mask.shape
    heads = cols // HDIM
    params = [gains[0], shifts[0], outbias, scale] + ([gains[1], shifts[1]] if cross else [])
    params = jnp.stack(params)
    extra = list(cross) if cross else []
    outs = [((rows, width), single), ((rows, width), bfloat), ((rows, width), bfloat)]
    outs += [((rows, width), bfloat)] if cross else []
    outs += [((SLOTS, rows, cols), bfloat)] * 3
    outs += [((SLOTS, images * heads, patches, patches), bfloat), ((SLOTS, rows, cols), bfloat)]
    return run(
        [(whole(v.shape), v) for v in (x, *extra, params, mask)] + [(ANY, w) for w in weights],
        outs,
        [whole(s) if len(s) == 2 else by_slot(s) for s, _ in outs],
        deps,
        body=functools.partial(attention_kernel, bool(cross)),
        grid=(SLOTS,),
        name="attention",
        scratch_shapes=[
            pltpu.VMEM((SLOTS,) + weights[0].shape, bfloat),
            pltpu.VMEM((rows, width), single),
            pltpu.SemaphoreType.DMA((SLOTS,)),
        ],
    )


def attention_grads_kernel(cross, last, *refs):
    refs = list(refs)
    take = lambda n: [refs.pop(0) for _ in range(n)]
    h_ref, rows_ref, branch_ref, qn_ref = take(4)
    cn_ref = take(1)[0] if cross else qn_ref
    q_ref, k_ref, v_ref, p_ref, mix_ref = take(5)
    if last:
        x_ref, parta_ref = take(2)
        if cross:
            partb_ref, latent_ref, seen_ref, dlat_ref = take(4)
    weights = take(2)
    outa_ref = take(1)[0]
    outb_ref = take(1)[0] if cross else None
    pack_ref, sums_ref = take(2)
    wbuf, ga, acc_a = take(3)
    acc_b = take(1)[0] if cross else None
    (wsem,) = take(1)
    j = pl.program_id(0)
    start_copies(j, weights, wbuf, wsem)

    @pl.when(j == 0)
    def _():
        h = h_ref[...]
        low = (rows_ref[0:1] * h).astype(bfloat)
        ga[...] = low
        sums_ref[...] = jnp.zeros_like(sums_ref)
        if last:
            sums_ref[2:3] = column_sum(h * branch_ref[...].astype(single))
            sums_ref[3:4] = column_sum(low.astype(single))
            acc_a[...] = parta_ref[...]
            if cross:
                acc_b[...] = partb_ref[...]
        else:
            acc_a[...] = jnp.zeros_like(acc_a)
            if cross:
                acc_b[...] = jnp.zeros_like(acc_b)

    wait_copy(j, weights, wbuf, wsem)
    cols = q_ref.shape[2]
    heads = cols // HDIM
    patches = p_ref.shape[2]
    images = p_ref.shape[1] // heads
    scale = HDIM**-0.5
    low = ga[...]
    gm = dot(low, wbuf[j, 3 * cols : 4 * cols], 1, 1).astype(bfloat)
    parts = []
    for i in range(images):
        span = slice(i * patches, (i + 1) * patches)
        q, k, v = q_ref[0, span], k_ref[0, span], v_ref[0, span]
        gmi = gm[span]
        qt, kt, gmt = q.T, k.T, gmi.T
        gqt, gkt, gvt = [], [], []
        for h in range(heads):
            lanes = slice(h * HDIM, (h + 1) * HDIM)
            low_p = p_ref[0, i * heads + h]
            probs = low_p.astype(single)
            product = probs * dot(gmi[:, lanes], v[:, lanes], 1, 1)
            gs = (product - probs * jnp.sum(product, axis=-1, keepdims=True)).astype(bfloat)
            gqt.append(dot(kt[lanes], gs, 1, 1))
            gkt.append(dot(qt[lanes], gs, 1, 0))
            gvt.append(dot(gmt[lanes], low_p, 1, 0))
        gqt = (jnp.concatenate(gqt, 0) * scale).astype(bfloat)
        gkt = (jnp.concatenate(gkt, 0) * scale).astype(bfloat)
        gvt = jnp.concatenate(gvt, 0).astype(bfloat)
        parts.append((gqt, gkt, gvt))
        a = acc_a[span] + dot(gqt.T, wbuf[j, :cols], 1, 0)
        b = dot(gkt.T, wbuf[j, cols : 2 * cols], 1, 0) + dot(gvt.T, wbuf[j, 2 * cols : 3 * cols], 1, 0)
        if cross:
            acc_a[span] = a
            acc_b[span] += b
        else:
            acc_a[span] = a + b
    gqt, gkt, gvt = (jnp.concatenate([p[n] for p in parts], 1) for n in range(3))
    ones = jnp.ones((8, images * patches), bfloat)
    sums_ref[pl.ds(j, 1), :cols] = dot(ones, gqt, 1, 1)[0:1]
    sums_ref[pl.ds(j, 1), cols : 2 * cols] = dot(ones, gvt, 1, 1)[0:1]
    qn = qn_ref[...]
    cn = cn_ref[...] if cross else qn
    pack_ref[0, 0:cols] = dot(gqt, qn, 1, 0).astype(bfloat)
    pack_ref[0, cols : 2 * cols] = dot(gkt, cn, 1, 0).astype(bfloat)
    pack_ref[0, 2 * cols : 3 * cols] = dot(gvt, cn, 1, 0).astype(bfloat)
    pack_ref[0, 3 * cols :] = dot(mix_ref[0], low, 0, 0).astype(bfloat)

    @pl.when(j == 1)
    def _():
        gn = acc_a[...]
        if not last:
            outa_ref[...] = gn
            if cross:
                outb_ref[...] = acc_b[...]
            return
        x = x_ref[...].astype(single)
        unit, factor = norm_parts(x)
        sums_ref[4:5] = column_sum(gn * unit)
        sums_ref[5:6] = column_sum(gn)
        gx = h_ref[...] + norm_back(gn, unit, factor, rows_ref[1:2])
        if cross:
            seen = seen_ref[...] > 0
            unit, factor = norm_parts(jnp.where(seen, latent_ref[...], x))
            gn = acc_b[...]
            sums_ref[6:7] = column_sum(gn * unit)
            sums_ref[7:8] = column_sum(gn)
            flow = norm_back(gn, unit, factor, rows_ref[2:3])
            gx = gx + jnp.where(seen, 0.0, flow)
            outb_ref[...] = dlat_ref[...].astype(single) + jnp.where(seen, flow, 0.0)
        store_blocks(outa_ref, gx)


def attention_grads(slots, parts, h, x, cross, gains, scale, branch, qn, cn, q, k, v, p, mix, weights, blocks, deps=()):
    last = parts is not None
    rows, width = x.shape
    cols = q.shape[2]
    params = jnp.stack([scale, gains[0]] + ([gains[1]] if cross else []))
    pack = (2, 4 * cols, width)
    ins = [(whole(v.shape), v) for v in (h, params, branch, qn) + ((cn,) if cross else ())]
    ins += [(half_specs(e.shape, slots), e) for e in (q, k, v, p, mix)]
    if last:
        ins += [(whole(e.shape), e) for e in (x, *parts, *(cross or ()))]
    ins += [(ANY, weights[r]) for r in slots]
    outs = [(blocks, bfloat) if last else ((rows, width), single)]
    outs += [((rows, width), single)] if cross else []
    specs = [whole(s) for s, _ in outs] + [by_slot(pack), whole((SUMS, width))]
    outs += [(pack, bfloat), ((SUMS, width), single)]
    accs = [pltpu.VMEM((rows, width), single)] * (2 if cross else 1)
    return run(
        ins,
        outs,
        specs,
        deps,
        body=functools.partial(attention_grads_kernel, bool(cross), last),
        grid=(2,),
        name="attention_grads",
        scratch_shapes=[
            pltpu.VMEM((2,) + weights[0].shape, bfloat),
            pltpu.VMEM((rows, width), bfloat),
            *accs,
            pltpu.SemaphoreType.DMA((2,)),
        ],
    )


def spread_kernel(names, me_ref, *refs):
    j = pl.program_id(0)
    count = len(refs) - names
    for r in range(count):

        @pl.when(j == r)
        def _(r=r):
            for n in range(names):
                refs[count + n][0] = refs[r][n].astype(single)


def spread(me, pieces):
    names, *block = pieces[0].shape
    zeros = (0,) * len(block)
    spec = pl.BlockSpec((1, *block), lambda j, me_ref: (me_ref[0] ^ j,) + zeros)
    return pl.pallas_call(
        functools.partial(spread_kernel, names),
        grid_spec=pltpu.PrefetchScalarGridSpec(
            num_scalar_prefetch=1,
            grid=(len(pieces),),
            in_specs=[pl.BlockSpec(p.shape, lambda j, me_ref: (0,) + zeros) for p in pieces],
            out_specs=[spec] * names,
        ),
        out_shape=[jax.ShapeDtypeStruct((len(pieces), *block), single)] * names,
        name="spread",
    )(me.reshape(1), *pieces)


def pack_kernel(skip, *refs):
    in_ref, out_ref, inbias_ref, expbias_ref, pack_ref = refs[skip:]
    cols = in_ref.shape[2]
    width = in_ref.shape[1]
    for n in range(3):
        pack_ref[n * cols : (n + 1) * cols] = in_ref[n].T
    pack_ref[3 * cols : 4 * cols] = out_ref[...]

    def halves(values):
        high = values.astype(bfloat).astype(single)
        return high, values - high

    lines = [*halves(inbias_ref[...]), *halves(expbias_ref[...])]
    lines = [jnp.concatenate(lines[:2], 1)] + lines[2:] + [jnp.zeros((BIAS_ROWS - 3, width), single)]
    pack_ref[4 * cols :] = jnp.concatenate(lines, 0).astype(bfloat)


def attention_pack(inproj, outproj, inbias, expbias, deps):
    cols, width = outproj.shape
    return pl.pallas_call(
        functools.partial(pack_kernel, len(deps)),
        in_specs=[ANY] * len(deps) + [pl.BlockSpec(memory_space=pltpu.VMEM)] * 4,
        out_shape=jax.ShapeDtypeStruct((4 * cols + BIAS_ROWS, width), bfloat),
        name="pack",
    )(*deps, inproj, outproj, inbias.reshape(1, -1), expbias.reshape(1, -1))


def swap(values, axis, count, bit):
    return lax.ppermute(values, axis, [(i, i ^ bit) for i in range(count)])


def near_core(values):
    return swap(values, "tensor", SLOTS, 1)


def over_chip(values):
    return swap(values, "tensor", SLOTS, 2)


def part_at(values, index, parts, axis=0):
    size = values.shape[axis] // parts
    return lax.dynamic_slice_in_dim(values, index * size, size, axis)


def add_low(*terms):
    total = terms[0].astype(single)
    for term in terms[1:]:
        total = total + term.astype(single)
    return total.astype(bfloat)


def placed(mine, own, other, axis=0):
    first = mine == 0
    return jnp.concatenate([jnp.where(first, own, other), jnp.where(first, other, own)], axis)


def tie(*values):
    return lax.optimization_barrier(values)


def gather_stages(count):
    stages, stride = [], 1
    while stride < count:
        radix = 2 if stride == 1 else min(4, count // stride)
        stages.append((radix, stride))
        stride *= radix
    return stages


def gather_piece(count):
    place, piece = lax.axis_index("dp"), 0
    for radix, stride in gather_stages(count):
        piece = piece * radix + (place // stride) % radix
    return piece


def gather_send(values, count, stage):
    radix, stride = gather_stages(count)[stage]
    return [values] + [swap(values, "dp", count, hop * stride) for hop in range(1, radix)]


def gather_join(pieces, count, stage, axis):
    radix, stride = gather_stages(count)[stage]
    mine = (lax.axis_index("dp") // stride) % radix
    size = pieces[0].shape[axis]
    shape = list(pieces[0].shape)
    shape[axis] = size * radix
    whole_array = jnp.zeros(shape, pieces[0].dtype)
    for hop, piece in enumerate(pieces):
        whole_array = lax.dynamic_update_slice_in_dim(whole_array, piece, (mine ^ hop) * size, axis)
    return whole_array


class Unit:
    def __init__(self, count, send, across_first):
        self.count, self.across_first = count, across_first
        self.pending = near_core(send)
        self.bits = []
        stride = 1
        while stride < count:
            self.bits.append(stride)
            stride *= 2
        self.stage = 0
        self.steps = 3 + 2 * (len(self.bits) - 1)

    def bit(self, n):
        return (lax.axis_index("dp") // self.bits[n]) % 2

    def hop(self, values, n):
        return swap(values, "dp", self.count, self.bits[n])

    def kept(self):
        return (self.near, getattr(self, "first", None), getattr(self, "value", None))[min(self.stage - 1, 2)]

    def keep_tied(self, kept):
        setattr(self, ("near", "first", "value")[min(self.stage - 1, 2)], kept)

    def follow(self, previous):
        self.pending, kept = tie(self.pending, previous.kept())
        previous.keep_tied(kept)

    def step(self):
        pending = self.pending
        stage, last = self.stage, len(self.bits) - 1
        self.stage += 1
        x = self.bit(0)
        if stage == 0:
            self.near = near = pending
            keep = self.keep
            if self.across_first:
                sent = add_low(keep[1], near[1])
                self.pending = over_chip(sent)
            else:
                sent = add_low(part_at(keep, 1 - x, 2, 1), part_at(near, 1 - x, 2, 1))
                self.pending = self.hop(sent, 0)
        elif stage == 1:
            keep, near = self.keep, self.near
            self.first = pending
            if self.across_first:
                sent = add_low(*(part_at(v, 1 - x, 2) for v in (keep[0], near[0], pending)))
                self.pending = self.hop(sent, 0)
            else:
                sent = add_low(part_at(keep[1], x, 2), part_at(near[1], x, 2), pending[1])
                self.pending = over_chip(sent)
        elif stage == 2:
            self.value = self.halves(pending)
            sent = self.scatter(1)
        elif stage < 2 + last:
            n = stage - 2
            self.value = add_low(part_at(self.value, self.bit(n), 2), pending)
            sent = self.scatter(n + 1)
        elif stage == 2 + last:
            sent = self.value = add_low(part_at(self.value, self.bit(last), 2), pending)
            self.pending = self.hop(sent, last)
        else:
            n = last - (stage - 3 - last)
            sent = self.value = placed(self.bit(n), self.value, pending)
            self.pending = self.hop(sent, n - 1)
        return sent

    def halves(self, pending):
        x = self.bit(0)
        first = part_at(self.first, x, 2) if self.across_first else self.first[0]
        return add_low(part_at(self.keep[0], x, 2), part_at(self.near[0], x, 2), first, pending)

    def scatter(self, n):
        sent = part_at(self.value, 1 - self.bit(n), 2)
        self.pending = self.hop(sent, n)
        return sent

    def result(self):
        return placed(self.bit(0), self.value, self.pending)


class Pair:
    def __init__(self, units):
        self.units = units
        self.count, self.bits, self.steps = units[0].count, units[0].bits, units[0].steps

    stage = 2

    @property
    def pending(self):
        return [u.pending for u in self.units] if self.stage == 2 else self.sent

    @pending.setter
    def pending(self, values):
        if self.stage == 2:
            for u, v in zip(self.units, values):
                u.pending = v
        else:
            self.sent = values

    def kept(self):
        return self.value

    def keep_tied(self, kept):
        self.value = kept

    def follow(self, previous):
        pending, kept = lax.optimization_barrier((self.pending, previous.kept()))
        self.pending = pending
        previous.keep_tied(kept)

    def bit(self, n):
        return self.units[0].bit(n)

    def hop(self, values, n):
        return self.units[0].hop(values, n)

    def scatter(self, n):
        sent = part_at(self.value, 1 - self.bit(n), 2, 1)
        self.sent = self.hop(sent, n)
        return sent

    def step(self):
        pending, stage, last = self.pending, self.stage, len(self.bits) - 1
        self.stage += 1
        if stage == 2:
            self.value = jnp.stack([u.halves(p) for u, p in zip(self.units, pending)])
            return self.scatter(1)
        if stage < 2 + last:
            n = stage - 2
            self.value = add_low(part_at(self.value, self.bit(n), 2, 1), pending)
            return self.scatter(n + 1)
        if stage == 2 + last:
            self.value = add_low(part_at(self.value, self.bit(last), 2, 1), pending)
            self.sent = self.hop(self.value, last)
        else:
            n = last - (stage - 3 - last)
            self.value = placed(self.bit(n), self.value, pending, 1)
            self.sent = self.hop(self.value, n - 1)
        return self.value

    def result(self):
        return placed(self.bit(0), self.value, self.sent, 1)


def steps_after(done, units):
    sent = []
    for n, u in enumerate(units):
        if n:
            u.follow(units[n - 1])
        else:
            u.pending, done = lax.optimization_barrier((u.pending, done))
        sent.append(u.step())
    return done, sent


TAIL = (
    "ea", "ef_e", "rf", "ef_s", "ra", "rf", "ra", "ea", "ef", "rf", "ra", "ef", "ea", "ra", "ef", "ea", "ra", "ef", "ea",
    "ef", "ea", "ea",
)


def make_local(count):
    def local(
        patches, mask_queries, visible, lengths, d_latent, d_regress,
        e_gain, e_shift, e_scale, e_inproj, e_inbias, e_outproj, e_outbias, e_expand, e_expbias, e_shrink,
        r_gain, r_shift, r_scale, r_inproj, r_inbias, r_outproj, r_outbias, r_expand, r_expbias, r_shrink,
    ):
        micro, images, part, width = patches.shape
        patch_count = visible.shape[2]
        rows = images * patch_count
        cols = e_inbias.shape[1]
        hidden = e_expbias.shape[0]
        blocks = (SLOTS, images, part, width)
        me = lax.axis_index("tensor")

        def pieces_of(*arrays):
            taken = []
            for r in range(SLOTS):
                one = [lax.dynamic_index_in_dim(a, me ^ r, 0, keepdims=False).astype(bfloat) for a in arrays]
                taken.append(jnp.stack(one) if len(one) > 1 else one[0])
            return taken

        def exchange(pieces):
            return [swap(p, "tensor", SLOTS, r) if r else p for r, p in enumerate(pieces)]

        def join(pieces):
            return jnp.stack(pieces, 1).reshape(rows, width)

        pieces = pieces_of(patches)
        tokens_sent = exchange(pieces)
        piece = gather_piece(count)
        stages = len(gather_stages(count))

        def feed_piece(expand, shrink):
            return jnp.stack([part_at(expand, piece, count), part_at(shrink, piece, count)])

        def gather_to_last(sent):
            for stage in range(stages - 1, 0, -1):
                joined = gather_join(sent, count, stage, 1)
                sent = gather_send(joined, count, stage - 1)
            return joined, sent

        e_piece, r_piece = feed_piece(e_expand, e_shrink), feed_piece(r_expand, r_shrink)
        e_slice = over_chip(e_piece)
        e_pack = attention_pack(e_inproj, e_outproj, e_inbias, e_expbias, [*pieces[1:], e_piece])
        e_pack_t, r_piece, e_exp_t, e_shr_t, *tokens_sent = tie(e_pack, r_piece, e_expand, e_shrink, *tokens_sent)
        e_pack1, e_pack2 = near_core(e_pack_t), over_chip(e_pack_t)
        e_exp1, e_shr1 = near_core(e_exp_t), near_core(e_shr_t)
        r_slice = over_chip(r_piece)
        e_sent = gather_send(e_slice, count, stages - 1)
        r_slice, e_sent[1] = tie(r_slice, e_sent[1])
        e_gathered, e_half = gather_to_last(e_sent)

        tensor_order = jnp.stack([me ^ r for r in range(SLOTS)])
        position = (tensor_order[:, None] * part + jnp.arange(part)[None, :]).reshape(-1)
        my_lengths = lax.dynamic_index_in_dim(lengths, me, 0, keepdims=False)
        my_visible = lax.dynamic_index_in_dim(visible, me, 0, keepdims=False)
        my_visible = jnp.concatenate([part_at(my_visible, me ^ r, SLOTS, 1) for r in range(SLOTS)], 1)
        valid = position[None, :] < my_lengths[:, None]
        seen = (my_visible == 1) | (position[None, :] == 0)
        seen_rows = seen.reshape(rows, 1).astype(single)
        e_mask = jnp.where(valid & seen, 0.0, -1e30).astype(single)[:, None, :]
        r_mask = jnp.where(valid, 0.0, -1e30).astype(single)[:, None, :]

        tokens = join(tokens_sent)
        r_pack = attention_pack(r_inproj, r_outproj, r_inbias, r_expbias, [e_pack])
        q_pieces = pieces_of(mask_queries)
        g_pieces = pieces_of(d_regress, d_latent)
        e_pack2, e_gathered, r_slice = tie(e_pack2, e_gathered, r_slice)
        e_pack3 = near_core(e_pack2)
        r_sent = gather_send(r_slice, count, stages - 1)
        e_packs = [e_pack, e_pack1, e_pack2, e_pack3]
        e_mid, e_ba, n0, q0, k0, v0, p0, mix0 = attention(
            tokens, None, e_gain, e_shift, e_outbias[0], e_scale[0], e_mask, e_packs,
            [e_gathered, r_slice, r_pack, *q_pieces, *g_pieces, e_exp1, e_shr1],
        )

        hops = len(r_sent)
        e_mid, e_half[1], r_pack_t, *rest = tie(e_mid, e_half[1], r_pack, *r_sent, *q_pieces)
        queries_sent = exchange(rest[hops:])
        r_pack1, r_pack2 = near_core(r_pack_t), over_chip(r_pack_t)
        r_gathered, r_half = gather_to_last(rest[:hops])
        e_feed2 = gather_join(e_half, count, 0, 1)
        e_feed3 = near_core(e_feed2)
        e_feeds = [e_expand, e_shrink, e_exp1, e_shr1, e_feed2, e_feed3]
        latent, latent_low, e_bf, n1, e_act, e_slope = feed_forward(
            e_mid, e_gain[1], e_shift[1], e_outbias[1], e_scale[1], e_feeds, e_packs, blocks, True,
            [r_pack1, r_gathered, *queries_sent[1:]],
        )

        latent, r_pack2, r_half[1], r_exp_t, r_shr_t, *g_pieces = tie(
            latent, r_pack2, r_half[1], r_expand, r_shrink, *g_pieces
        )
        r_pack3 = near_core(r_pack2)
        r_feed2 = gather_join(r_half, count, 0, 1)
        r_feed3 = near_core(r_feed2)
        r_exp1, r_shr1 = near_core(r_exp_t), near_core(r_shr_t)
        queries = join(queries_sent)
        r_packs = [r_pack, r_pack1, r_pack2, r_pack3]
        r_mid, r_ba, qn, cn, q1, k1, v1, p1, mix1 = attention(
            queries, (latent, seen_rows), r_gain, r_shift, r_outbias[0], r_scale[0], r_mask, r_packs, [r_feed2]
        )

        r_mid, *g_pieces = tie(r_mid, *g_pieces)
        g_sent = exchange(g_pieces)
        r_feeds = [r_expand, r_shrink, r_exp1, r_shr1, r_feed2, r_feed3]
        regressed_low, r_bf, n2, r_act, r_slope = feed_forward(
            r_mid, r_gain[2], r_shift[2], r_outbias[1], r_scale[1], r_feeds, r_packs, blocks, False
        )

        regressed_low, *g_sent = tie(regressed_low, *g_sent)
        g_regress = join([g[0] for g in g_sent])
        g_latent = join([g[1] for g in g_sent])
        outs_sent = exchange([jnp.stack([latent_low[r], regressed_low[r]]) for r in range(SLOTS)])

        def feed_back(orders, g, x, gain, scale, branch, n, act, slope, feed, deps):
            part_sum, send_e, send_s, sums_send = feed_grads(
                SEND, None, g, x, gain, scale, branch, n, act, slope, feed, deps
            )
            unit_e = Unit(count, send_e, orders[0])
            unit_s = Unit(count, send_s, orders[1])
            h, unit_e.keep, unit_s.keep, sums_keep = feed_grads(
                KEEP, part_sum, g, x, gain, scale, branch, n, act, slope, feed
            )
            return h, unit_e, unit_s, (sums_send, sums_keep)

        h, rf_e, rf_s, sums_rf = feed_back(
            (True, False), g_regress, r_mid, r_gain[2], r_scale[1], r_bf, n2, r_act, r_slope, r_feeds, []
        )
        h, sent = steps_after(h, [rf_e, rf_s])
        args = (h, queries, (latent, seen_rows, g_latent), r_gain, r_scale[0], r_ba, qn, cn, q1, k1, v1, p1, mix1, r_packs, blocks)
        part_a, part_b, send, sums_send = attention_grads(SEND, None, *args, sent)
        ra = Unit(count, send, True)
        gq_low, g, ra.keep, sums_keep = attention_grads(KEEP, (part_a, part_b), *args, outs_sent[1:])
        sums_ra = (sums_send, sums_keep)

        g, sent = steps_after(g, [ra, rf_e, rf_s])
        outs2_sent = exchange([gq_low[r] for r in range(SLOTS)])
        h, ef_e, ef_s, sums_ef = feed_back(
            (False, True), g, e_mid, e_gain[1], e_scale[1], e_bf, n1, e_act, e_slope, e_feeds, sent
        )
        rf = Pair([rf_e, rf_s])
        h, sent = steps_after(h, [ef_e, ra, ef_s])
        args = (h, tokens, None, e_gain, e_scale[0], e_ba, n0, None, q0, k0, v0, p0, mix0, e_packs, blocks)
        part_a, send, sums_send = attention_grads(SEND, None, *args, sent)
        ea = Unit(count, send, False)
        part_a, sent = steps_after(part_a, [rf])
        gp_low, ea.keep, sums_keep = attention_grads(KEEP, (part_a,), *args, [*sent, *outs2_sent[1:]])
        sums_ea = (sums_send, sums_keep)

        pairs = (sums_ef, sums_ea, sums_rf, sums_ra)
        small = jnp.stack([p[n] for n in (1, 0) for p in pairs])
        line = lax.broadcasted_iota(jnp.int32, (1, SUMS, 1), 1)
        distances = [2**n for n in range(count.bit_length() - 1)]
        small_now = [small, near_core(small), 0]

        def small_step(u):
            totals, near, stage = small_now
            if near is None:
                return
            near, kept = tie(near, u.kept())
            u.keep_tied(kept)
            if stage == 0:
                totals = totals[:4] + jnp.where(line < 2, near[4:], near[:4])
                near = over_chip(totals)
            else:
                totals = totals + (jnp.where(line == 0, near[:, 1:2], near) if stage == 1 else near)
                near = swap(totals, "dp", count, distances.pop(0)) if distances else None
            small_now[:] = [totals, near, stage + 1]

        ef_e.pending, rf.pending, ea.keep = tie(ef_e.pending, rf.pending, ea.keep)
        units = dict(ea=ea, rf=rf, ra=ra, ef_e=ef_e, ef_s=ef_s, ef=Pair([ef_e, ef_s]))
        previous = None
        for turn, name in enumerate(TAIL, 1):
            u = units[name]
            if u.stage == u.steps:
                continue
            if previous is not None and previous is not u:
                u.follow(previous)
            u.step()
            previous = u
            if turn >= 4 and turn % 3 == 1:
                small_step(u)
            if turn == 8:
                kept, gp_low = tie(u.kept(), gp_low)
                u.keep_tied(kept)
            if turn == 14:
                kept, *late = tie(u.kept(), *outs_sent, *outs2_sent)
                u.keep_tied(kept)
                outs_sent, outs2_sent = late[:SLOTS], late[SLOTS:]
        while small_now[1] is not None:
            small_step(u)
        totals = small_now[0]
        for name in ("rf", "ra", "ef", "ea") * 16:
            if units[name].stage < units[name].steps:
                units[name].step()
        outs3_sent = exchange([gp_low[r] for r in range(SLOTS)])
        out_latent, out_regressed = spread(me, outs_sent)
        (out_queries,) = spread(me, [o[None] for o in outs2_sent])
        (out_patches,) = spread(me, [o[None] for o in outs3_sent])
        (rf_e, rf_s), ra, (ef_e, ef_s), ea = (units[name].result() for name in ("rf", "ra", "ef", "ea"))

        e_f, e_a, r_f, r_a = totals
        e_inb_g = e_a[0, : 2 * cols].reshape(2, cols)
        r_inb_g = r_a[0, : 2 * cols].reshape(2, cols)
        e_exb_g, r_exb_g = e_f[0], r_f[0]

        def attention_outputs(shard):
            shard = shard.astype(single)
            return shard[: 3 * cols].reshape(3, cols, width).transpose(0, 2, 1), shard[3 * cols :]

        e_in_g, e_out_g = attention_outputs(ea)
        r_in_g, r_out_g = attention_outputs(ra)
        return (
            out_latent, out_regressed, out_patches, out_queries,
            jnp.stack([e_a[4], e_f[2]]), jnp.stack([e_a[5], e_f[3]]), jnp.stack([e_a[2], e_f[4]]),
            e_in_g, e_inb_g, e_out_g, jnp.stack([e_a[3], e_f[5]]), ef_e.astype(single), e_exb_g, ef_s.astype(single),
            jnp.stack([r_a[4], r_a[6], r_f[2]]), jnp.stack([r_a[5], r_a[7], r_f[3]]), jnp.stack([r_a[2], r_f[4]]),
            r_in_g, r_inb_g, r_out_g, jnp.stack([r_a[3], r_f[5]]), rf_e.astype(single), r_exb_g, rf_s.astype(single),
        )

    return local


def solution(mesh):
    assert mesh.shape["tensor"] == SLOTS
    rows = P(None, "dp", "tensor", None)

    def block():
        return (
            P(), P(), P(), P(None, None, "tensor"), P(None, "tensor"), P("tensor", None), P(),
            P(None, "tensor"), P("tensor"), P("tensor", None),
        )

    return jax.shard_map(
        make_local(mesh.shape["dp"]),
        mesh=mesh,
        in_specs=(rows, rows, P(None, "dp", None), P(None, "dp"), rows, rows, *block(), *block()),
        out_specs=(rows, rows, rows, rows, *block(), *block()),
        check_vma=False,
    )
```
